32 devices in a mesh: fsdp: 16 (over z, y, core), tp: 2 (over x).
Axes of the slice: x: 2, y: 2, z: 4, core: 2. Of those that a mesh axis runs over, the one named last changes fastest.
Arguments:
- tokens: bfloat16 [16, 512, 768], P('fsdp', 'tp'), may hold values from -6 to 6
- segments: int32 [16, 512], P('fsdp'), may hold values from 0 to 2, as said below
- valid: int32 [16, 512], P('fsdp', 'tp'), may hold values from 0 to 1, as said below
- teacher: bfloat16 [16, 512, 768], P('fsdp', 'tp'), may hold values from -6 to 6
- attn_in: bfloat16 [2, 768, 3, 768], P(None, 'fsdp', None, 'tp'), may hold values from -0.3125 to 0.3125
- attn_out: bfloat16 [2, 768, 768], P(None, 'fsdp', 'tp'), may hold values from -0.625 to 0.625
- ff_in: bfloat16 [2, 768, 3072], P(None, 'fsdp', 'tp'), may hold values from -0.21875 to 0.21875
- ff_out: bfloat16 [2, 768, 3072], P(None, 'fsdp', 'tp'), may hold values from -0.109375 to 0.109375
- biases: bfloat16 [2, 5, 768], P(None, None, 'fsdp'), may hold values from -1.5 to 1.5
- gains: bfloat16 [2, 2, 768], P(None, None, 'fsdp'), may hold values from 0.5 to 1.5
- ff_bias: bfloat16 [2, 3072], P(None, 'fsdp'), may hold values from -1.5 to 1.5
- query_bias: bfloat16 [2, 768], P(None, 'fsdp'), may hold values from -1.5 to 1.5
Outputs:
- mixed: bfloat16 [16, 512, 768], P('fsdp', 'tp')
- tokens_grad: float32 [16, 512, 768], P('fsdp', 'tp')
- loss: float32 [], replicated
- attn_in_grad: float32 [2, 768, 3, 768], P(None, 'fsdp', None, 'tp')
- attn_out_grad: float32 [2, 768, 768], P(None, 'fsdp', 'tp')
- ff_in_grad: float32 [2, 768, 3072], P(None, 'fsdp', 'tp')
- ff_out_grad: float32 [2, 768, 3072], P(None, 'fsdp', 'tp')
- biases_grad: float32 [2, 5, 768], P(None, None, 'fsdp')
- gains_grad: float32 [2, 2, 768], P(None, None, 'fsdp')
- ff_bias_grad: float32 [2, 3072], P(None, 'fsdp')
- query_bias_grad: float32 [2, 768], P(None, 'fsdp')
The draws below stay inside these ranges and needn't reach their ends.
Inputs may be any that keep to these rules, and one draw needn't show every extreme that they name: `segments`: along each sequence the ids are 1, 2, 3, ... in runs of 200 to 480 tokens (documents), then 0 (padding) to the end; padding is shorter than 480 tokens; some document of the batch has exactly 480 tokens, and some sequence consists of documents of exactly 200 tokens. `valid`: each flag is 1 independently, with a probability that rises linearly from 1/4 in the first sequence to 3/4 in the last.
All inputs are finite; a program needn't handle non-finite values.
Results may differ from the reference program's by a relative error of at most 0.035.
Values may be sent and summed in bfloat16 or wider, within the bound.
A program may use at most 192 MiB of HBM per device.

```python
import jax
import jax.numpy as jnp
from jax import lax

D = 768
HEADS = 12
HEAD_DIM = 64
FF = 3072
LAYERS = 2
SEQ = 512
DOC_MIN = 200
DOC_MAX = 480
NSEQ = 16
TOKENS = 8192


def draw_segments(key, part):
    pieces = SEQ // DOC_MIN + 1
    first_key, second_key = jax.random.split(key)
    doc_lengths = jax.random.randint(first_key, (NSEQ, pieces), DOC_MIN, DOC_MAX + 1)
    chosen = jax.random.randint(second_key, (), 0, NSEQ)
    shortest = (chosen + 1) % NSEQ
    seq_rows = jnp.arange(NSEQ, dtype=jnp.int32)[:, None]
    doc_cols = jnp.arange(pieces, dtype=jnp.int32)[None, :]
    doc_lengths = jnp.where(seq_rows == shortest, DOC_MIN, doc_lengths)
    doc_lengths = jnp.where((seq_rows == chosen) & (doc_cols == 0), DOC_MAX, doc_lengths)
    doc_ends = jnp.cumsum(doc_lengths, axis=1)
    places = jnp.arange(SEQ, dtype=jnp.int32)
    doc_index = jnp.sum((doc_ends[:, None, :] <= places[None, :, None]).astype(jnp.int32), axis=2)
    finish = jnp.take_along_axis(doc_ends, doc_index, axis=1)
    return jnp.where(finish <= SEQ, doc_index + 1, 0).astype(jnp.int32)


def draw_valid(key, part):
    seq_rank = jnp.arange(NSEQ, dtype=jnp.int32)[:, None]
    span_all = 4 * (NSEQ - 1)
    rolled = jax.random.randint(key, (NSEQ, SEQ), 0, span_all)
    return (rolled < NSEQ - 1 + 2 * seq_rank).astype(jnp.int32)


def block_levels(stream_key, shape, cuts, low, top_value):
    level = 1.0
    for position, blocks in cuts:
        steps = jax.random.uniform(jax.random.fold_in(jax.random.fold_in(stream_key, 6), position), (blocks,), jnp.float32, low / len(cuts), top_value / len(cuts))
        level = level * jnp.repeat(jnp.exp(steps), shape[position] // blocks).reshape((-1,) + (1,) * (len(shape) - 1 - position))
    return level


def bell_draw(rng, shape, width, bound, cuts=(), kind=jnp.bfloat16):
    level = block_levels(rng, shape, cuts, -0.22, 0.18) if cuts else 1.0
    values = jax.random.normal(rng, shape, jnp.float32) * width * level
    return jnp.minimum(jnp.maximum(values, -bound), bound).astype(kind)


def setup_inputs(seed: int = 0) -> dict:
    splits = jax.random.split(jax.random.key(seed), 13)
    return {
        "tokens": bell_draw(splits[0], (NSEQ, SEQ, D), 1.0, 6.0, ((0, 16), (1, 2))),
        "segments": draw_segments(jax.random.fold_in(splits[12], 71), 0),
        "valid": draw_valid(jax.random.fold_in(splits[12], 71), 0),
        "teacher": bell_draw(splits[3], (NSEQ, SEQ, D), 1.0, 6.0, ((0, 16), (1, 2))),
        "attn_in": bell_draw(splits[4], (LAYERS, D, 3, D), (D // 2) ** -0.5, 0.3125, ((1, 16), (3, 2))),
        "attn_out": bell_draw(splits[5], (LAYERS, D, D), (D // 8) ** -0.5, 0.625, ((1, 16), (2, 2))),
        "ff_in": bell_draw(splits[6], (LAYERS, D, FF), D ** -0.5, 0.21875, ((1, 16), (2, 2))),
        "ff_out": bell_draw(splits[7], (LAYERS, D, FF), FF ** -0.5, 0.109375, ((1, 16), (2, 2))),
        "biases": bell_draw(splits[8], (LAYERS, 5, D), 0.3, 1.5, ((2, 16),)),
        "gains": jnp.clip(1.0 + 0.1 * jax.random.normal(splits[9], (LAYERS, 2, D), jnp.float32), 0.5, 1.5).astype(jnp.bfloat16),
        "ff_bias": bell_draw(splits[10], (LAYERS, FF), 0.3, 1.5, ((1, 16),)),
        "query_bias": bell_draw(splits[11], (LAYERS, D), 0.3, 1.5, ((1, 16),)),
    }


epsilon = 1e-05
root_half = 0.7071067811865476

@jax.custom_vjp
def low(v):
    return lax.optimization_barrier(v.astype(jnp.bfloat16)).astype(jnp.float32)

@jax.custom_vjp
def low_back(v):
    return v

def low_keep(v):
    return (low(v), None)

def low_pass(kept, grad):
    return (grad,)

def back_keep(v):
    return (v, None)

def back_low(kept, grad):
    return (low(grad),)
low.defvjp(low_keep, low_pass)
low_back.defvjp(back_keep, back_low)

def matmul(left, right):
    return jnp.dot(left, right, precision=lax.Precision.HIGHEST, preferred_element_type=jnp.float32)

def gelu_exact(inputs):
    return 0.5 * inputs * (1.0 + lax.erf(inputs * root_half))

def layer_norm(stream, gain, shift):
    centred = stream - lax.optimization_barrier(jnp.mean(stream, axis=-1, keepdims=True))
    scaled = centred * lax.rsqrt(lax.optimization_barrier(jnp.mean(centred * centred, axis=-1, keepdims=True)) + epsilon)
    return scaled * gain + shift

def attend_one(queries, keys_in, values_in, seg_ids):
    allowed = (seg_ids[None, :] > 0) & ((seg_ids[:, None] == seg_ids[None, :]) | (seg_ids[:, None] == 0))
    scores = jnp.einsum('qhd,khd->hqk', queries, keys_in, precision=lax.Precision.HIGHEST) * HEAD_DIM ** (-0.5)
    scores = low_back(scores)
    scores = jnp.where(allowed[None], scores, -jnp.inf)
    highest = lax.optimization_barrier(jnp.max(scores, axis=-1, keepdims=True))
    exponent = jnp.exp(scores - highest)
    attn_probs = low(exponent / lax.optimization_barrier(jnp.sum(exponent, axis=-1, keepdims=True)))
    return jnp.einsum('hqk,khd->qhd', attn_probs, values_in, precision=lax.Precision.HIGHEST)

def attend_item(group_item):
    return jax.checkpoint(attend_one)(group_item[0], group_item[1], group_item[2], group_item[3])

def layer_forward(stream, seg_ids, attn_in, attn_out, ff_in, ff_out, biases, gains, ff_bias, query_bias):
    seqs_here = stream.shape[0]
    rows_in = stream.reshape(-1, D)
    low_in = low(rows_in)
    joined_qkv = matmul(low_in, attn_in.reshape(D, 3 * D)).reshape(-1, 3, D)
    queries = low(low_back(joined_qkv[:, 0] + query_bias))
    keys_in = low(low_back(joined_qkv[:, 1]))
    values_in = low(low_back(joined_qkv[:, 2] + biases[0]))
    head_shape = (seqs_here, SEQ, HEADS, HEAD_DIM)
    heads_out = lax.map(attend_item, (queries.reshape(head_shape), keys_in.reshape(head_shape), values_in.reshape(head_shape), seg_ids))
    heads_low = low(low_back(heads_out.reshape(-1, D)))
    attn_sum = low_back(matmul(heads_low, attn_out.T)) + biases[1]
    hidden = layer_norm(rows_in + attn_sum, gains[0], biases[2])
    hidden_low = low(hidden)
    pre_act = low_back(matmul(hidden_low, ff_in)) + ff_bias
    act_low = low(gelu_exact(pre_act))
    mlp_sum = low_back(matmul(act_low, ff_out.T)) + biases[3]
    return layer_norm(hidden + mlp_sum, gains[1], biases[4]).reshape(seqs_here, SEQ, D)

def group_objective(stream, params, seg_ids, weight_rows, target, loss_scale):
    for layer_num in range(LAYERS):
        stream = layer_forward(stream, seg_ids, *[parameter[layer_num] for parameter in params])
    deviation = stream - target
    objective = 0.5 * loss_scale * jnp.sum(weight_rows[..., None] * deviation * deviation)
    return (stream, objective)

def reference(tokens, segments, valid, teacher, attn_in, attn_out, ff_in, ff_out, biases, gains, ff_bias, query_bias):
    weight_all = (valid * (segments > 0).astype(jnp.int32)).astype(jnp.float32)
    total_count = jnp.sum(weight_all)
    loss_scale = TOKENS / total_count
    params = tuple((parameter.astype(jnp.float32) for parameter in (attn_in, attn_out, ff_in, ff_out, biases, gains, ff_bias, query_bias)))
    group_seqs = min(NSEQ, max(1, 4096 // SEQ))
    groups = NSEQ // group_seqs
    inputs = (tokens.astype(jnp.float32).reshape(groups, group_seqs, SEQ, D), segments.reshape(groups, group_seqs, SEQ), weight_all.reshape(groups, group_seqs, SEQ), teacher.astype(jnp.float32).reshape(groups, group_seqs, SEQ, D))

    def step_group(state_pair, group_item):
        grad_sums, square_sum = state_pair
        stream, seg_ids, weight_rows, target = group_item

        def objective_of(stream_in, params_in):
            return group_objective(stream_in, params_in, seg_ids, weight_rows, target, loss_scale)
        (result, objective), pullback = jax.vjp(objective_of, stream, params)
        stream_grad, param_grads = pullback((jnp.zeros_like(result), jnp.ones_like(objective)))
        deviation = result - target
        square_sum = square_sum + jnp.sum(weight_rows[..., None] * deviation * deviation)
        grad_sums = jax.tree.map(jnp.add, grad_sums, param_grads)
        return ((grad_sums, square_sum), (result.astype(jnp.bfloat16), stream_grad))
    zeros_init = tuple((jnp.zeros_like(parameter) for parameter in params))
    (grad_sums, square_sum), (mixed, tokens_grad) = lax.scan(step_group, (zeros_init, jnp.zeros((), jnp.float32)), inputs)
    loss = square_sum / (total_count * D)
    return (mixed.reshape(NSEQ, SEQ, D), tokens_grad.reshape(NSEQ, SEQ, D), loss, grad_sums[0], grad_sums[1], grad_sums[2], grad_sums[3], grad_sums[4], grad_sums[5], grad_sums[6], grad_sums[7])
```

```python
import functools

import jax
import jax.numpy as jnp
from jax import lax
from jax.experimental import pallas as pl
from jax.experimental.pallas import tpu as pltpu
from jax.sharding import PartitionSpec as P

HEAD_DIM = 64
MESH = pl.DeviceIdType.MESH
PIECE = 384


def group_place(extra):
    spot = lax.axis_index("fsdp") // extra
    return spot // 4, (spot // 2) % 2, spot % 2


def group_peer(extra, row, col, core):
    rest = lax.axis_index("fsdp") % extra
    return {"fsdp": ((row * 2 + col) * 2 + core) * extra + rest, "tp": lax.axis_index("tp")}


def gather_kernel(extra, pieces, own_ref, full_ref, z_send, z_recv, hop_send, hop_recv, local_sem):
    z, y, c = group_place(extra)
    z_peers = [group_peer(extra, (z + step) % 4, y, c) for step in (1, 2, 3)]
    y_peer = group_peer(extra, z, 1 - y, c)
    c_peer = group_peer(extra, z, y, 1 - c)
    barrier = pltpu.get_barrier_semaphore()
    for peer in (*z_peers, y_peer, c_peer):
        pl.semaphore_signal(barrier, inc=1, device_id=peer, device_id_type=MESH)
    pl.semaphore_wait(barrier, 5)

    def z_copy(piece, step):
        return pltpu.make_async_remote_copy(
            src_ref=own_ref.at[piece],
            dst_ref=full_ref.at[piece, z, y, c],
            send_sem=z_send.at[piece, step],
            recv_sem=z_recv.at[piece, step],
            device_id=z_peers[step],
            device_id_type=MESH,
        )

    def own_copy(piece):
        return pltpu.make_async_copy(own_ref.at[piece], full_ref.at[piece, z, y, c], local_sem.at[piece])

    def hop_copy(piece, kind):
        column = 1 - y if kind == 2 else y
        return pltpu.make_async_remote_copy(
            src_ref=full_ref.at[piece, :, column, c],
            dst_ref=full_ref.at[piece, :, column, c],
            send_sem=hop_send.at[piece, kind],
            recv_sem=hop_recv.at[piece, kind],
            device_id=y_peer if kind == 0 else c_peer,
            device_id_type=MESH,
        )

    def issue(piece, carry):
        own_copy(piece).start()
        for step in range(3):
            z_copy(piece, step).start()
        return carry

    lax.fori_loop(0, pieces, issue, 0)

    def forward(step, carry):
        @pl.when(step < pieces)
        def _():
            own_copy(step).wait()
            for k in range(3):
                z_copy(step, k).wait_recv()
            hop_copy(step, 0).start()
            hop_copy(step, 1).start()

        @pl.when(step > 0)
        def _():
            hop_copy(step - 1, 0).wait_recv()
            hop_copy(step - 1, 2).start()

        return carry

    lax.fori_loop(0, pieces + 1, forward, 0)

    def finish(piece, carry):
        hop_copy(piece, 1).wait_recv()
        hop_copy(piece, 2).wait_recv()
        for k in range(3):
            z_copy(piece, k).wait_send()
            hop_copy(piece, k).wait_send()
        return carry

    lax.fori_loop(0, pieces, finish, 0)


def gather_all(own, extra):
    pieces, rows, cols = own.shape
    return pl.pallas_call(
        functools.partial(gather_kernel, extra, pieces),
        out_shape=jax.ShapeDtypeStruct((pieces, 4, 2, 2, rows, cols), own.dtype),
        in_specs=[pl.BlockSpec(memory_space=pl.ANY)],
        out_specs=pl.BlockSpec(memory_space=pltpu.VMEM),
        scratch_shapes=[
            pltpu.SemaphoreType.DMA((pieces, 3)),
            pltpu.SemaphoreType.DMA((pieces, 3)),
            pltpu.SemaphoreType.DMA((pieces, 3)),
            pltpu.SemaphoreType.DMA((pieces, 3)),
            pltpu.SemaphoreType.DMA((pieces,)),
        ],
        compiler_params=pltpu.CompilerParams(
            collective_id=0, has_side_effects=True, vmem_limit_bytes=40 * 1024 * 1024
        ),
        name="gather_weights",
    )(own)


def shard_pieces(shard):
    layers, rows = shard.shape[0], shard.shape[1]
    return jnp.swapaxes(shard.reshape(layers, rows, -1, PIECE), 1, 2)


def widen(shard, extra):
    if extra == 1:
        return shard
    size = lax.axis_size("fsdp")
    groups = [list(range(first, first + extra)) for first in range(0, size, extra)]
    return lax.all_gather(shard, "fsdp", axis=1, axis_index_groups=groups, tiled=True)


def fetch_matrices(attn_in, attn_out, ff_in, ff_out):
    extra = lax.axis_size("fsdp") // 16
    layers = attn_in.shape[0]
    stacked = jnp.concatenate(
        [shard_pieces(widen(part, extra)) for part in (attn_in, attn_out, ff_in, ff_out)], axis=1
    )
    per_layer, rows = stacked.shape[1], stacked.shape[2]
    full = gather_all(stacked.reshape(layers * per_layer, rows, PIECE), extra)
    full = full.reshape(layers, per_layer, 16 * rows, PIECE)
    counts = [part.size // layers // (part.shape[1] * PIECE) for part in (attn_in, attn_out, ff_in, ff_out)]
    joined, start = [], 0
    for count in counts:
        block = full[:, start : start + count]
        joined.append(jnp.swapaxes(block, 1, 2).reshape(layers, 16 * rows, count * PIECE))
        start += count
    joined[0] = joined[0].reshape(layers, 16 * rows, 3, -1)
    return joined


epsilon = 1e-05
root_half = 0.7071067811865476
inv_root_tau = 0.3989422804014327


def layer_norm(stream, gain, shift):
    centred = stream - jnp.mean(stream, axis=-1, keepdims=True)
    inverse = lax.rsqrt(jnp.mean(centred * centred, axis=-1, keepdims=True) + epsilon)
    normed = centred * inverse
    return (normed * gain + shift, normed, inverse)


def norm_back(grad_out, normed, inverse, gain):
    scaled = grad_out * gain
    return inverse * (
        scaled
        - jnp.mean(scaled, axis=-1, keepdims=True)
        - normed * jnp.mean(scaled * normed, axis=-1, keepdims=True)
    )


def gelu_exact(inputs):
    return 0.5 * inputs * (1.0 + lax.erf(inputs * root_half))


def gelu_slope(inputs):
    return (
        0.5 * (1.0 + lax.erf(inputs * root_half))
        + inputs * jnp.exp(-0.5 * inputs * inputs) * inv_root_tau
    )


def mask_rows(seg_ids):
    return (seg_ids[None, :] > 0) & (
        (seg_ids[:, None] == seg_ids[None, :]) | (seg_ids[:, None] == 0)
    )


def attention_forward(queries, keys_in, values_in, seg_ids):
    length = queries.shape[0]
    block_rows = min(512, length)
    score_scale = queries.shape[2] ** (-0.5)

    def one_block(block_num):
        allowed = mask_rows(seg_ids)
        scores = (
            jnp.einsum("qhd,khd->hqk", queries, keys_in, preferred_element_type=jnp.float32)
            * score_scale
        )
        scores = jnp.where(allowed[None], scores, -jnp.inf)
        highest = jnp.max(scores, axis=-1, keepdims=True)
        exponent = jnp.exp(scores - highest)
        totals = jnp.sum(exponent, axis=-1, keepdims=True)
        attn_probs = (exponent / totals).astype(jnp.bfloat16)
        mixed_rows = jnp.einsum(
            "hqk,khd->qhd", attn_probs, values_in, preferred_element_type=jnp.float32
        )
        return (mixed_rows.astype(jnp.bfloat16), (highest + jnp.log(totals))[:, :, 0])

    outputs, log_totals = lax.map(one_block, jnp.arange(length // block_rows))
    return (outputs.reshape(length, -1), log_totals)


def attention_back(queries, keys_in, values_in, seg_ids, log_totals, grad_heads):
    length = queries.shape[0]
    block_rows = min(512, length)
    score_scale = queries.shape[2] ** (-0.5)

    def one_block(sums_pair, block_item):
        block_num, log_rows = block_item
        key_sum, value_sum = sums_pair
        allowed = mask_rows(seg_ids)
        scores = (
            jnp.einsum("qhd,khd->hqk", queries, keys_in, preferred_element_type=jnp.float32)
            * score_scale
        )
        attn_probs = jnp.where(allowed[None], jnp.exp(scores - log_rows[:, :, None]), 0.0)
        value_sum = value_sum + jnp.einsum(
            "hqk,qhd->khd",
            attn_probs.astype(jnp.bfloat16),
            grad_heads,
            preferred_element_type=jnp.float32,
        )
        grad_probs = jnp.einsum(
            "qhd,khd->hqk", grad_heads, values_in, preferred_element_type=jnp.float32
        )
        grad_scores = attn_probs * (
            grad_probs - jnp.sum(attn_probs * grad_probs, axis=-1, keepdims=True)
        )
        low_scores = grad_scores.astype(jnp.bfloat16)
        query_grad = (
            jnp.einsum("hqk,khd->qhd", low_scores, keys_in, preferred_element_type=jnp.float32)
            * score_scale
        )
        key_sum = (
            key_sum
            + jnp.einsum("hqk,qhd->khd", low_scores, queries, preferred_element_type=jnp.float32)
            * score_scale
        )
        return ((key_sum, value_sum), query_grad)

    zero_sum = jnp.zeros(keys_in.shape, jnp.float32)
    (key_sum, value_sum), query_grads = lax.scan(
        one_block, (zero_sum, zero_sum), (jnp.arange(length // block_rows), log_totals)
    )
    return (query_grads.reshape(keys_in.shape), key_sum, value_sum)


def gather_rows(values_low):
    return lax.all_gather(values_low, "tp", axis=0, tiled=True)


def gather_grads(values_low):
    return lax.all_gather(values_low, "tp", axis=0, tiled=True)


def row_product(left, weight_mat):
    return lax.dot_general(
        left, weight_mat, (((1,), (1,)), ((), ())), preferred_element_type=jnp.float32
    )


def summed_rows(left, weight_mat, rows_dev):

    def term_rows(row_start, row_count):
        return row_product(left, weight_mat)

    return lax.psum_scatter(
        term_rows(jnp.int32(0), lax.axis_size("tp") * rows_dev).astype(jnp.bfloat16),
        "tp",
        scatter_dimension=0,
        tiled=True,
    ).astype(jnp.float32)


def summed_grads(left, weight_mat, rows_dev):

    def term_rows(row_start, row_count):
        return row_product(left, weight_mat)

    return lax.psum_scatter(
        term_rows(jnp.int32(0), lax.axis_size("tp") * rows_dev).astype(jnp.bfloat16),
        "tp",
        scatter_dimension=0,
        tiled=True,
    ).astype(jnp.float32)


def outer_rows(left, right):
    return lax.dot_general(
        left, right, (((0,), (0,)), ((), ())), preferred_element_type=jnp.float32
    )


def on_device(
    tokens,
    segments,
    valid,
    teacher,
    attn_in,
    attn_out,
    ff_in,
    ff_out,
    biases,
    gains,
    ff_bias,
    query_bias,
):
    rows_dev = tokens.shape[1]
    tp_rank = lax.axis_index("tp")
    tp_count = lax.axis_size("tp")
    seg_ids = segments[0]
    length = seg_ids.shape[0]
    width = tokens.shape[2]
    heads_width = attn_in.shape[3]
    hidden_width = ff_in.shape[2]
    layers = attn_in.shape[0]
    head_shape = (length, heads_width // HEAD_DIM, HEAD_DIM)
    own_seg = lax.dynamic_slice_in_dim(seg_ids, tp_rank * rows_dev, rows_dev, 0)
    weight_rows = (valid[0] * (own_seg > 0).astype(jnp.int32)).astype(jnp.float32)
    stream = tokens[0].astype(jnp.float32)
    saved_acts = []
    full_attn_in, full_attn_out, full_ff_in, full_ff_out = fetch_matrices(
        attn_in, attn_out, ff_in, ff_out
    )
    for layer_num in range(layers):
        fetched = (
            full_attn_in[layer_num],
            full_attn_out[layer_num],
            full_ff_in[layer_num],
            full_ff_out[layer_num],
            lax.all_gather(biases[layer_num], "fsdp", axis=1, tiled=True),
            lax.all_gather(gains[layer_num], "fsdp", axis=1, tiled=True),
            lax.all_gather(ff_bias[layer_num], "fsdp", axis=0, tiled=True),
            lax.all_gather(query_bias[layer_num], "fsdp", axis=0, tiled=True),
        )
        w_in, w_out, w_up, w_down, bias_low, gain_low, up_low, query_low = fetched
        bias_all = bias_low.astype(jnp.float32)
        gain_all = gain_low.astype(jnp.float32)
        full_in = gather_rows(stream.astype(jnp.bfloat16))
        joined_qkv = jnp.dot(
            full_in, w_in.reshape(width, 3 * heads_width), preferred_element_type=jnp.float32
        ).reshape(length, 3, heads_width)
        bias_query = lax.dynamic_slice_in_dim(
            query_low.astype(jnp.float32), tp_rank * heads_width, heads_width, 0
        )
        bias_value = lax.dynamic_slice_in_dim(bias_all[0], tp_rank * heads_width, heads_width, 0)
        queries = (joined_qkv[:, 0] + bias_query).astype(jnp.bfloat16).reshape(head_shape)
        keys_in = joined_qkv[:, 1].astype(jnp.bfloat16).reshape(head_shape)
        values_in = (joined_qkv[:, 2] + bias_value).astype(jnp.bfloat16).reshape(head_shape)
        heads_low, log_totals = attention_forward(queries, keys_in, values_in, seg_ids)
        attn_sum = summed_rows(heads_low, w_out, rows_dev)
        hidden, normed_a, inverse_a = layer_norm(
            stream + attn_sum + bias_all[1], gain_all[0], bias_all[2]
        )
        full_hidden = gather_rows(hidden.astype(jnp.bfloat16))
        up_shift = lax.dynamic_slice_in_dim(
            up_low.astype(jnp.float32), tp_rank * hidden_width, hidden_width, 0
        )
        pre_act = jnp.dot(full_hidden, w_up, preferred_element_type=jnp.float32) + up_shift
        act_low = gelu_exact(pre_act).astype(jnp.bfloat16)
        mlp_sum = summed_rows(act_low, w_down, rows_dev)
        stream, normed_b, inverse_b = layer_norm(
            hidden + mlp_sum + bias_all[3], gain_all[1], bias_all[4]
        )
        saved_acts.append(
            (
                full_in,
                queries,
                keys_in,
                values_in,
                log_totals,
                heads_low,
                normed_a,
                inverse_a,
                full_hidden,
                pre_act,
                act_low,
                normed_b,
                inverse_b,
                (w_in, w_out, w_up, w_down, gain_low),
            )
        )
    deviation = stream - teacher[0].astype(jnp.float32)
    count_all, square_all = lax.psum(
        (jnp.sum(weight_rows), jnp.sum(weight_rows[:, None] * deviation * deviation)),
        ("fsdp", "tp"),
    )
    loss = square_all / (count_all * width)
    token_total = length * lax.axis_size("fsdp")
    grad_rows = token_total / count_all * weight_rows[:, None] * deviation
    layer_grads_list = [None] * layers
    for layer_num in reversed(range(layers)):
        (
            full_in,
            queries,
            keys_in,
            values_in,
            log_totals,
            heads_low,
            normed_a,
            inverse_a,
            full_hidden,
            pre_act,
            act_low,
            normed_b,
            inverse_b,
            kept_weights,
        ) = saved_acts[layer_num]
        w_in, w_out, w_up, w_down, gain_low = kept_weights
        gain_all = gain_low.astype(jnp.float32)
        d_out = norm_back(grad_rows, normed_b, inverse_b, gain_all[1])
        gain_b_grad = jnp.sum(grad_rows * normed_b, axis=0)
        shift_b_grad = jnp.sum(grad_rows, axis=0)
        down_bias_grad = jnp.sum(d_out, axis=0)
        full_dout = gather_grads(d_out.astype(jnp.bfloat16))
        act_grad = jnp.dot(full_dout, w_down, preferred_element_type=jnp.float32)
        down_grad = outer_rows(full_dout, act_low)
        pre_grad = act_grad * gelu_slope(pre_act)
        up_bias_grad = jnp.sum(pre_grad, axis=0)
        pre_low = pre_grad.astype(jnp.bfloat16)
        up_grad = outer_rows(full_hidden, pre_low)
        hidden_grad = d_out + summed_grads(pre_low, w_up, rows_dev)
        d_mid = norm_back(hidden_grad, normed_a, inverse_a, gain_all[0])
        gain_a_grad = jnp.sum(hidden_grad * normed_a, axis=0)
        shift_a_grad = jnp.sum(hidden_grad, axis=0)
        out_bias_grad = jnp.sum(d_mid, axis=0)
        full_dmid = gather_grads(d_mid.astype(jnp.bfloat16))
        heads_grad = (
            jnp.dot(full_dmid, w_out, preferred_element_type=jnp.float32)
            .astype(jnp.bfloat16)
            .reshape(head_shape)
        )
        out_grad = outer_rows(full_dmid, heads_low)
        query_grad, key_grad, value_grad = attention_back(
            queries, keys_in, values_in, seg_ids, log_totals, heads_grad
        )
        qkv_low = (
            jnp.stack([query_grad, key_grad, value_grad], axis=1)
            .astype(jnp.bfloat16)
            .reshape(length, 3, heads_width)
        )
        qkv_sums = jnp.sum(qkv_low.astype(jnp.float32), axis=0)
        in_grad = outer_rows(full_in, qkv_low)
        grad_rows = d_mid + summed_grads(
            qkv_low.reshape(length, 3 * heads_width), w_in.reshape(width, 3 * heads_width), rows_dev
        )
        empty_row = jnp.zeros((width,), jnp.float32)
        bias_grad = jnp.stack(
            [
                lax.dynamic_update_slice_in_dim(empty_row, qkv_sums[2], tp_rank * heads_width, 0),
                out_bias_grad,
                shift_a_grad,
                down_bias_grad,
                shift_b_grad,
            ]
        )
        query_full = lax.dynamic_update_slice_in_dim(
            empty_row, qkv_sums[0], tp_rank * heads_width, 0
        )
        gain_grad = jnp.stack([gain_a_grad, gain_b_grad])
        up_bias_full = lax.dynamic_update_slice_in_dim(
            jnp.zeros((hidden_width * tp_count,), jnp.float32),
            up_bias_grad,
            tp_rank * hidden_width,
            0,
        )
        pieces_layer = (
            in_grad,
            out_grad,
            up_grad,
            down_grad,
            bias_grad,
            gain_grad,
            up_bias_full,
            query_full,
        )
        layer_grads_list[layer_num] = (
            lax.psum_scatter(pieces_layer[0], "fsdp", scatter_dimension=0, tiled=True),
            lax.psum_scatter(pieces_layer[1], "fsdp", scatter_dimension=0, tiled=True),
            lax.psum_scatter(pieces_layer[2], "fsdp", scatter_dimension=0, tiled=True),
            lax.psum_scatter(pieces_layer[3], "fsdp", scatter_dimension=0, tiled=True),
            lax.psum_scatter(pieces_layer[4], "fsdp", scatter_dimension=1, tiled=True),
            lax.psum_scatter(pieces_layer[5], "fsdp", scatter_dimension=1, tiled=True),
            lax.psum_scatter(pieces_layer[6], "fsdp", scatter_dimension=0, tiled=True),
            lax.psum_scatter(pieces_layer[7], "fsdp", scatter_dimension=0, tiled=True),
        )
    stacked = tuple(
        (
            jnp.stack([layer_entry[member] for layer_entry in layer_grads_list])
            for member in range(8)
        )
    )
    bias_shards, gain_shards, up_shards, query_shards = lax.psum(
        (stacked[4], stacked[5], stacked[6], stacked[7]), "tp"
    )
    return (
        stream.astype(jnp.bfloat16)[None],
        grad_rows[None],
        loss,
        stacked[0],
        stacked[1],
        stacked[2],
        stacked[3],
        bias_shards,
        gain_shards,
        up_shards,
        query_shards,
    )


def solution(mesh):
    in_specs = (
        P("fsdp", "tp", None),
        P("fsdp", None),
        P("fsdp", "tp"),
        P("fsdp", "tp", None),
        P(None, "fsdp", None, "tp"),
        P(None, "fsdp", "tp"),
        P(None, "fsdp", "tp"),
        P(None, "fsdp", "tp"),
        P(None, None, "fsdp"),
        P(None, None, "fsdp"),
        P(None, "fsdp"),
        P(None, "fsdp"),
    )
    out_specs = (
        P("fsdp", "tp", None),
        P("fsdp", "tp", None),
        P(),
        P(None, "fsdp", None, "tp"),
        P(None, "fsdp", "tp"),
        P(None, "fsdp", "tp"),
        P(None, "fsdp", "tp"),
        P(None, None, "fsdp"),
        P(None, None, "fsdp"),
        P(None, "fsdp"),
        P(None, "fsdp"),
    )
    return jax.shard_map(
        on_device, mesh=mesh, in_specs=in_specs, out_specs=out_specs, check_vma=False
    )
```

```python
import functools

import jax
import jax.numpy as jnp
from jax import lax
from jax.experimental import pallas as pl
from jax.experimental.pallas import tpu as pltpu
from jax.sharding import PartitionSpec as P

HEAD_DIM = 64
MESH = pl.DeviceIdType.MESH
PIECE = 384
CHUNKS = 2
LANES = 128
GROUP = 16

epsilon = 1e-05
root_half = 0.7071067811865476
inv_root_tau = 0.3989422804014327
masked = -1e30


def product(left, right):
    return lax.dot_general(left, right, (((1,), (0,)), ((), ())), preferred_element_type=jnp.float32)


def product_nt(left, right):
    return lax.dot_general(left, right, (((1,), (1,)), ((), ())), preferred_element_type=jnp.float32)


def norm_stats(total):
    centred = total - jnp.mean(total, axis=-1, keepdims=True)
    inverse = lax.rsqrt(jnp.mean(centred * centred, axis=-1, keepdims=True) + epsilon)
    return centred * inverse, inverse


def norm_back(grad_out, normed, inverse, gain):
    scaled = grad_out * gain
    return inverse * (
        scaled
        - jnp.mean(scaled, axis=-1, keepdims=True)
        - normed * jnp.mean(scaled * normed, axis=-1, keepdims=True)
    )


def step_kernel(
    extra,
    token_total,
    own_ref,
    small_ref,
    tokens_ref,
    teacher_ref,
    weight_ref,
    seg_col_ref,
    seg_row_ref,
    mixed_ref,
    tokens_grad_ref,
    grad_ref,
    sums_ref,
    count_ref,
    mats,
    small_all,
    param,
    ff_shift,
    from_core,
    from_col,
    from_row,
    x_low,
    qkv,
    heads,
    log_sum,
    h_low,
    act,
    slope,
    normed,
    inverse,
    hidden,
    stream,
    out_part,
    in_part,
    own_part,
    d_low,
    d_qkv,
    d_heads,
    d_rows,
    mask,
    k_turn,
    v_turn,
    probs_all,
    scores_all,
    turned,
    sums_in,
    count_mine,
    count_theirs,
    z_send,
    z_recv,
    hop_send,
    hop_recv,
    local_sem,
    s_send,
    s_recv,
    x_send,
    x_recv,
    r_send,
    r_recv,
    a_send,
    a_recv,
    c_send,
    c_recv,
):
    pieces = own_ref.shape[0]
    layers = x_low.shape[0]
    per_layer = pieces // layers
    half_rows = tokens_ref.shape[0]
    width = tokens_ref.shape[1]
    length = 2 * half_rows
    rows = half_rows // CHUNKS
    pairs = PIECE // LANES
    ups = act.shape[1]

    spot = lax.axis_index("fsdp") // extra
    rest = lax.axis_index("fsdp") % extra
    t = lax.axis_index("tp")
    z, y, c = spot // 4, (spot // 2) % 2, spot % 2

    def peer(row, col, core):
        return {"fsdp": ((row * 2 + col) * 2 + core) * extra + rest, "tp": t}

    z_peers = [peer((z + step) % 4, y, c) for step in (1, 2, 3)]
    y_peer = peer(z, 1 - y, c)
    c_peer = peer(z, y, 1 - c)
    x_peer = {"fsdp": lax.axis_index("fsdp"), "tp": 1 - t}
    everyone = (*z_peers, y_peer, c_peer, x_peer)
    barrier = pltpu.get_barrier_semaphore()
    for other in everyone:
        pl.semaphore_signal(barrier, inc=1, device_id=other, device_id_type=MESH)
    pl.semaphore_wait(barrier, len(everyone))

    def remote(src, dst, send_sem, recv_sem, device):
        return pltpu.make_async_remote_copy(
            src_ref=src,
            dst_ref=dst,
            send_sem=send_sem,
            recv_sem=recv_sem,
            device_id=device,
            device_id_type=MESH,
        )

    def z_copy(piece, step):
        return remote(
            own_ref.at[piece],
            mats.at[piece, z, y, c],
            z_send.at[piece, step],
            z_recv.at[piece, step],
            z_peers[step],
        )

    def own_copy(piece):
        return pltpu.make_async_copy(own_ref.at[piece], mats.at[piece, z, y, c], local_sem.at[piece])

    def hop_copy(piece, kind):
        column = 1 - y if kind == 2 else y
        block = mats.at[piece, :, column, c]
        return remote(
            block,
            block,
            hop_send.at[piece, kind],
            hop_recv.at[piece, kind],
            y_peer if kind == 0 else c_peer,
        )

    def small_z(step):
        block = small_all.at[z, y, c]
        return remote(small_ref, block, s_send.at[step], s_recv.at[step], z_peers[step])

    def small_hop(kind):
        column = 1 - y if kind == 2 else y
        block = small_all.at[:, column, c]
        return remote(
            block, block, s_send.at[3 + kind], s_recv.at[3 + kind], y_peer if kind == 0 else c_peer
        )

    def first_half(piece):
        own_copy(piece).wait()
        for step in range(3):
            z_copy(piece, step).wait_recv()
        hop_copy(piece, 0).start()
        hop_copy(piece, 1).start()

    def second_half(piece):
        hop_copy(piece, 0).wait_recv()
        hop_copy(piece, 2).start()

    def advance(step):
        if isinstance(step, int):
            if step < pieces:
                first_half(step)
            if 0 < step <= pieces:
                second_half(step - 1)
        else:
            pl.when(step < pieces)(lambda: first_half(step))
            pl.when(step <= pieces)(lambda: second_half(step - 1))

    def need(first, count=1):
        for piece in range(first, first + count):
            hop_copy(piece, 1).wait_recv()
            hop_copy(piece, 2).wait_recv()

    def chunk_rows(chunk):
        if isinstance(chunk, int):
            return pl.ds(chunk * rows, rows)
        return pl.ds(pl.multiple_of(chunk * rows, rows), rows)

    def give_rows(number, chunk, block):
        place = block.at[t, chunk_rows(chunk)]
        return remote(place, place, x_send.at[number, chunk], x_recv.at[number, chunk], x_peer)

    def give_part(number, chunk):
        return remote(
            out_part.at[chunk_rows(chunk)],
            in_part.at[chunk_rows(chunk)],
            x_send.at[number, chunk],
            x_recv.at[number, chunk],
            x_peer,
        )

    def put_part(number, previous, chunk, value):
        if previous is not None:
            give_part(previous, chunk).wait_send()
        out_part[chunk_rows(chunk)] = value.astype(jnp.bfloat16)
        give_part(number, chunk).start()

    def place_part(index, number, previous, value):
        chunk = index % CHUNKS

        @pl.when(index < CHUNKS)
        def _():
            put_part(number, previous, chunk, value)

        @pl.when(index >= CHUNKS)
        def _():
            own_part[chunk_rows(chunk)] = value

    def core_copy(piece):
        return remote(
            mats.at[piece, :, :, 1 - c],
            from_core.at[piece],
            r_send.at[piece, 0],
            r_recv.at[piece, 0],
            c_peer,
        )

    def col_copy(piece):
        return remote(
            from_core.at[piece, :, 1 - y],
            from_col.at[piece],
            r_send.at[piece, 1],
            r_recv.at[piece, 1],
            y_peer,
        )

    def row_copy(piece, step):
        return remote(
            from_core.at[piece, (z + step + 1) % 4, y],
            from_row.at[piece, step],
            r_send.at[piece, 2 + step],
            r_recv.at[piece, 2 + step],
            z_peers[step],
        )

    def reduce_core(piece):
        core_copy(piece).wait_recv()
        for row in range(4):
            from_core[piece, row] = (
                from_core[piece, row].astype(jnp.float32)
                + mats[piece, row, :, c].astype(jnp.float32)
            ).astype(jnp.bfloat16)
        col_copy(piece).start()

    def reduce_col(piece):
        col_copy(piece).wait_recv()
        from_core[piece, :, y] = (
            from_core[piece, :, y].astype(jnp.float32) + from_col[piece].astype(jnp.float32)
        ).astype(jnp.bfloat16)
        for step in range(3):
            row_copy(piece, step).start()

    def reduce_row(piece):
        for step in range(3):
            row_copy(piece, step).wait_recv()
        total = from_core[piece, z, y].astype(jnp.float32)
        for step in range(3):
            total = total + from_row[piece, step].astype(jnp.float32)
        grad_ref[piece] = total

    LAG = 2

    def reduce_step(index):
        if isinstance(index, int):
            if index < pieces:
                reduce_core(pieces - 1 - index)
            if 0 <= index - LAG < pieces:
                reduce_col(pieces - 1 - (index - LAG))
            if 0 <= index - 2 * LAG < pieces:
                reduce_row(pieces - 1 - (index - 2 * LAG))
        else:
            reduce_core(pieces - 1 - index)
            pl.when(index >= LAG)(lambda: reduce_col(pieces - 1 - (index - LAG)))
            pl.when(index >= 2 * LAG)(lambda: reduce_row(pieces - 1 - (index - 2 * LAG)))

    def put_grad(piece, value):
        mats[piece] = value.astype(jnp.bfloat16).reshape(mats.shape[1:])
        core_copy(piece).start()

    sum_blocks = ((8, 24), (0, 8))

    def sum_copy(phase, step):
        first, count = sum_blocks[phase]
        part = sums_ref.at[pl.ds(first, count)]
        slot = step if step < 3 else 3 + z
        device = (c_peer, y_peer, x_peer)[step] if step < 3 else z_peers[step - 3]
        return remote(
            part,
            sums_in.at[slot, pl.ds(first, count)],
            a_send.at[phase, step],
            a_recv.at[phase, step],
            device,
        )

    def sum_start(phase, step):
        if step < 3:
            sum_copy(phase, step).start()
            return
        first, count = sum_blocks[phase]
        for k in range(3, 6):
            sum_copy(phase, k).start()
        sums_in[3 + z, pl.ds(first, count)] = sums_ref[pl.ds(first, count)]

    def sum_finish(phase, step):
        first, count = sum_blocks[phase]
        block = pl.ds(first, count)
        if step < 3:
            sum_copy(phase, step).wait()
            sums_ref[block] = sums_ref[block] + sums_in[step, block]
            return
        for k in range(3, 6):
            sum_copy(phase, k).wait()
        sums_ref[block] = (sums_in[3, block] + sums_in[4, block]) + (
            sums_in[5, block] + sums_in[6, block]
        )

    def add_sum(row, value, column=None):
        if column is None:
            sums_ref[pl.ds(row, 1)] += value
        else:
            sums_ref[pl.ds(row, 1), column] += value

    def par(row):
        return param[pl.ds(row, 1)]

    def matrix(piece):
        return mats[piece].reshape(width, PIECE)

    own_columns = pl.ds(pl.multiple_of(t * PIECE, LANES), PIECE)

    small_all[z, y, c] = small_ref[...]
    for step in range(3):
        small_z(step).start()
    for chunk in range(CHUNKS):
        place = x_low.at[0, t, chunk_rows(chunk)]
        remote(
            tokens_ref.at[chunk_rows(chunk)],
            place,
            x_send.at[0, chunk],
            x_recv.at[0, chunk],
            x_peer,
        ).start()

    def issue(piece, carry):
        own_copy(piece).start()
        for step in range(3):
            z_copy(piece, step).start()
        return carry

    lax.fori_loop(0, pieces, issue, 0)
    x_low[0, t] = tokens_ref[...]
    stream[...] = tokens_ref[...].astype(jnp.float32)
    seg_k, seg_q = seg_col_ref[...], seg_row_ref[pl.ds(0, 1)]
    allowed = (seg_k > 0) & ((seg_k == seg_q) | (seg_q == 0))
    mask[...] = jnp.where(allowed, 0.0, masked)
    sums_ref[...] = jnp.zeros_like(sums_ref)
    lane = lax.broadcasted_iota(jnp.int32, (1, LANES), 1)
    low_lanes = lane < HEAD_DIM
    low_sub = lax.broadcasted_iota(jnp.int32, (LANES, 1), 0) < HEAD_DIM

    for step in range(3):
        small_z(step).wait_recv()
    small_hop(0).start()
    small_hop(1).start()
    small_hop(0).wait_recv()
    small_hop(2).start()
    small_hop(1).wait_recv()
    small_hop(2).wait_recv()
    param[...] = jnp.zeros_like(param)
    ff_shift[...] = jnp.zeros_like(ff_shift)
    share = width // GROUP
    counted = jnp.zeros((8, LANES), jnp.float32)
    for place in range(GROUP):
        block = small_all[place // 4, (place // 2) % 2, place % 2]
        offset = place * share
        tile = min(offset // LANES * LANES, width - 2 * LANES)
        shifted = block[:16] if offset == tile else pltpu.roll(block[:16], offset - tile, 1)
        param[pl.ds(0, 16), pl.ds(tile, 2 * LANES)] += shifted
        counted = counted + block[16:24, :LANES]
    hidden_share = ff_shift.shape[1] // (GROUP // 2)
    for place in range(GROUP // 2):
        block = small_all[2 * t + place // 4, (place // 2) % 2, place % 2][16:24]
        offset = place * hidden_share
        tile = offset // LANES * LANES
        if offset != tile:
            block = pltpu.roll(block, offset - tile, 1)
        ff_shift[:, pl.ds(tile, 2 * LANES)] += block
    count_mine[...] = counted
    remote(count_mine, count_theirs, c_send.at[0], c_recv.at[0], x_peer).start()

    def split_heads(pair):
        return jnp.concatenate(
            [jnp.where(low_lanes, pair, 0), jnp.where(low_lanes, 0, pair)], axis=0
        ).astype(pair.dtype)

    def merge_heads(turned_pair):
        size = turned_pair.shape[1] // 2
        return jnp.where(low_sub, turned_pair[:, :size], turned_pair[:, size:]).T

    def pair_lanes(pair):
        return pl.ds(pair * LANES, LANES)

    def pair_rows(layer, which, pair):
        return qkv[layer, which, :, :, pair_lanes(pair)].reshape(length, LANES)

    def half_of(index):
        return jnp.where(index < CHUNKS, 1 - t, t)

    for layer in range(layers):
        base = layer * per_layer
        ex = 4 * layer
        early = layer == 0

        def project(half, where, j, layer=layer, base=base):
            acc = product(x_low[layer, half, where], matrix(base + j))
            if j == 0:
                acc = acc + param[pl.ds(14 + layer, 1), own_columns]
            if j == 2:
                acc = acc + param[pl.ds(layer * 5, 1), own_columns]
            low = acc.astype(jnp.bfloat16)
            if j == 0:
                low = low * jnp.bfloat16(HEAD_DIM**-0.5)
            qkv[layer, j, half, where] = low

        everything = pl.ds(0, half_rows)
        if early:
            advance(0)
        for j in range(3):
            if early:
                advance(j + 1)
            need(base + j)
            project(t, everything, j)
        for chunk in range(CHUNKS):
            give_rows(ex, chunk, x_low.at[layer]).wait_recv()
        for j in range(3):
            project(1 - t, everything, j)
        for pair in range(pairs):
            v_turn[pair] = pair_rows(layer, 2, pair).T

        def attend(index, carry, layer=layer, base=base, ex=ex, early=early):
            half, chunk = half_of(index), index % CHUNKS
            where = chunk_rows(chunk)
            columns = pl.ds(pl.multiple_of(half * half_rows + chunk * rows, rows), rows)
            bias = mask[:, columns]
            bias = jnp.concatenate([bias, bias], axis=1)
            advance(4 + index if early else 16 + index)
            for pair in range(pairs):
                queries = split_heads(qkv[layer, 0, half, where, pair_lanes(pair)])
                scores = product_nt(pair_rows(layer, 1, pair), queries) + bias
                highest = jnp.max(scores, axis=0, keepdims=True)
                exponent = jnp.exp(scores - highest)
                total = jnp.sum(exponent, axis=0, keepdims=True)
                probs = (exponent * (1.0 / total)).astype(jnp.bfloat16)
                log_sum[layer, pair, half, chunk] = highest + jnp.log(total)
                mixed_pair = merge_heads(product(v_turn[pair], probs))
                heads[layer, half, where, pair_lanes(pair)] = mixed_pair.astype(jnp.bfloat16)
            pl.when(index == 0)(lambda: need(base + 3))
            part = product_nt(heads[layer, half, where], matrix(base + 3))
            place_part(index, ex + 1, None if early else ex - 1, part)
            return carry

        lax.fori_loop(0, 2 * CHUNKS, attend, 0)

        for chunk in range(CHUNKS):
            where = chunk_rows(chunk)
            advance(8 + chunk if early else 20 + chunk)
            give_part(ex + 1, chunk).wait_recv()
            total = (
                stream[where] + own_part[where] + in_part[where].astype(jnp.float32) + par(layer * 5 + 1)
            )
            unit, scale = norm_stats(total)
            normed[layer, 0, where] = unit
            inverse[layer, 0, where] = scale
            value = unit * par(10 + layer * 2) + par(layer * 5 + 2)
            hidden[where] = value
            h_low[layer, t, where] = value.astype(jnp.bfloat16)
            give_rows(ex + 2, chunk, h_low.at[layer]).start()

        if early:
            need(4, 4)
        else:
            need(base + 4, 4)

        def feed(index, carry, layer=layer, base=base, ex=ex, early=early):
            half = jnp.where(index < CHUNKS, t, 1 - t)
            chunk = index % CHUNKS
            where = chunk_rows(chunk)

            @pl.when(index >= CHUNKS)
            def _():
                give_rows(ex + 2, chunk, h_low.at[layer]).wait_recv()

            source = h_low[layer, half, where]
            for j in range(ups):
                u = product(source, matrix(base + 4 + j)) + ff_shift[
                    pl.ds(layer, 1), pl.ds(j * PIECE, PIECE)
                ]
                cdf = 0.5 * (1.0 + lax.erf(u * root_half))
                bell = jnp.exp(-0.5 * u * u) * inv_root_tau
                act[layer, j, half, where] = (u * cdf).astype(jnp.bfloat16)
                slope[layer, j, half, where] = (cdf + u * bell).astype(jnp.bfloat16)

            @pl.when(index == 0)
            def _():
                first = 10 if early else 22
                for step in range(first, first + 3):
                    advance(step)
                need(base + 8, 4)

            part = product_nt(act[layer, 0, half, where], matrix(base + 8))
            for j in range(1, ups):
                part = part + product_nt(act[layer, j, half, where], matrix(base + 8 + j))
            flipped = jnp.where(index < CHUNKS, index + CHUNKS, index - CHUNKS)
            place_part(flipped, ex + 3, ex + 1, part)
            return carry

        lax.fori_loop(0, 2 * CHUNKS, feed, 0)

        if layer == layers - 1:
            remote(count_mine, count_theirs, c_send.at[0], c_recv.at[0], x_peer).wait()
            count_all = (count_mine[...] + count_theirs[...])[2:3, :1]
            count_ref[...] = jnp.broadcast_to(count_all, count_ref.shape)
            loss_scale = token_total / count_all
            squares = jnp.zeros((1, width), jnp.float32)
        for chunk in range(CHUNKS):
            where = chunk_rows(chunk)
            if early:
                advance(13 + chunk)
            give_part(ex + 3, chunk).wait_recv()
            total = (
                hidden[where] + own_part[where] + in_part[where].astype(jnp.float32) + par(layer * 5 + 3)
            )
            unit, scale = norm_stats(total)
            normed[layer, 1, where] = unit
            inverse[layer, 1, where] = scale
            value = unit * par(11 + layer * 2) + par(layer * 5 + 4)
            if layer < layers - 1:
                stream[where] = value
                x_low[layer + 1, t, where] = value.astype(jnp.bfloat16)
                give_rows(ex + 4, chunk, x_low.at[layer + 1]).start()
            else:
                mixed_ref[where] = value.astype(jnp.bfloat16)
                deviation = value - teacher_ref[where].astype(jnp.float32)
                weighted = weight_ref[where] * deviation
                squares = squares + jnp.sum(weighted * deviation, axis=0, keepdims=True)
                d_rows[where] = loss_scale * weighted
        if early:
            advance(15)
    add_sum(24, squares)

    def finish_gather(piece, carry):
        for k in range(3):
            z_copy(piece, k).wait_send()
            hop_copy(piece, k).wait_send()
        return carry

    lax.fori_loop(0, pieces, finish_gather, 0)

    for layer in range(layers - 1, -1, -1):
        base = layer * per_layer
        ex = 4 * layers + 4 * (layers - 1 - layer)
        last = layer == layers - 1
        done = 0 if last else per_layer
        sums_base = layer * 8

        for chunk in range(CHUNKS):
            where = chunk_rows(chunk)
            if not last:
                give_part(ex - 1, chunk).wait_recv()
                d_rows[where] += own_part[where] + in_part[where].astype(jnp.float32)
            grad_out, unit = d_rows[where], normed[layer, 1, where]
            below = norm_back(grad_out, unit, inverse[layer, 1, where], par(11 + layer * 2))
            d_low[layer, 0, t, where] = below.astype(jnp.bfloat16)
            give_rows(ex, chunk, d_low.at[layer, 0]).start()
            d_rows[where] = below
            add_sum(sums_base + 6, jnp.sum(grad_out * unit, axis=0, keepdims=True))
            add_sum(sums_base + 4, jnp.sum(grad_out, axis=0, keepdims=True))
            add_sum(sums_base + 3, jnp.sum(below, axis=0, keepdims=True))

        def feed_back(index, carry, layer=layer, base=base, ex=ex, last=last):
            half = jnp.where(index < CHUNKS, t, 1 - t)
            chunk = index % CHUNKS
            where = chunk_rows(chunk)

            @pl.when(index >= CHUNKS)
            def _():
                give_rows(ex, chunk, d_low.at[layer, 0]).wait_recv()

            source = d_low[layer, 0, half, where]
            for j in range(ups):
                du = product(source, matrix(base + 8 + j)) * slope[layer, j, half, where].astype(
                    jnp.float32
                )
                per_row = width // PIECE
                add_sum(
                    16 + layer * 4 + 2 * t + j // per_row,
                    jnp.sum(du, axis=0, keepdims=True),
                    pl.ds(j % per_row * PIECE, PIECE),
                )
                slope[layer, j, half, where] = du.astype(jnp.bfloat16)
            part = product_nt(slope[layer, 0, half, where], matrix(base + 4))
            for j in range(1, ups):
                part = part + product_nt(slope[layer, j, half, where], matrix(base + 4 + j))
            flipped = jnp.where(index < CHUNKS, index + CHUNKS, index - CHUNKS)
            place_part(flipped, ex + 1, 4 * layers - 1 if last else ex - 1, part)
            return carry

        lax.fori_loop(0, 2 * CHUNKS, feed_back, 0)

        turned[...] = d_low[layer, 0].reshape(length, width).T
        for j in range(ups - 1, -1, -1):
            put_grad(base + 8 + j, product(turned[...], act[layer, j].reshape(length, PIECE)))
        if not last:
            reduce_step(done - 1)

        for chunk in range(CHUNKS):
            where = chunk_rows(chunk)
            give_part(ex + 1, chunk).wait_recv()
            grad_out = d_rows[where] + own_part[where] + in_part[where].astype(jnp.float32)
            unit = normed[layer, 0, where]
            below = norm_back(grad_out, unit, inverse[layer, 0, where], par(10 + layer * 2))
            d_low[layer, 1, t, where] = below.astype(jnp.bfloat16)
            give_rows(ex + 2, chunk, d_low.at[layer, 1]).start()
            d_rows[where] = below
            add_sum(sums_base + 5, jnp.sum(grad_out * unit, axis=0, keepdims=True))
            add_sum(sums_base + 2, jnp.sum(grad_out, axis=0, keepdims=True))
            add_sum(sums_base + 1, jnp.sum(below, axis=0, keepdims=True))

        turned[...] = h_low[layer].reshape(length, width).T
        for j in range(ups - 1, -1, -1):
            put_grad(base + 4 + j, product(turned[...], slope[layer, j].reshape(length, PIECE)))
        reduce_step(done)
        reduce_step(done + 1)

        everything = pl.ds(0, half_rows)
        d_heads[t] = product(d_low[layer, 1, t], matrix(base + 3)).astype(jnp.bfloat16)
        for pair in range(pairs):
            k_turn[pair] = pair_rows(layer, 1, pair).T
        for chunk in range(CHUNKS):
            give_rows(ex + 2, chunk, d_low.at[layer, 1]).wait_recv()
        d_heads[1 - t] = product(d_low[layer, 1, 1 - t], matrix(base + 3)).astype(jnp.bfloat16)
        turned[...] = d_low[layer, 1].reshape(length, width).T
        put_grad(base + 3, product(turned[...], heads[layer].reshape(length, PIECE)))
        if not last:
            for step in range(3):
                sum_start(0, step)
                sum_finish(0, step)
            sum_start(0, 3)

        for pair in range(pairs):
            lanes = pair_lanes(pair)
            keys_in, values_in = pair_rows(layer, 1, pair), pair_rows(layer, 2, pair)

            def attend_back(index, carry, layer=layer, pair=pair, lanes=lanes):
                half, chunk = index // CHUNKS, index % CHUNKS
                where = chunk_rows(chunk)
                columns = pl.ds(pl.multiple_of(index * rows, rows), rows)
                bias = mask[:, columns]
                bias = jnp.concatenate([bias, bias], axis=1)
                keys_in, values_in = pair_rows(layer, 1, pair), pair_rows(layer, 2, pair)
                queries = split_heads(qkv[layer, 0, half, where, lanes])
                grads = split_heads(d_heads[half, where, lanes])
                scores = product_nt(keys_in, queries) + bias
                probs = jnp.exp(scores - log_sum[layer, pair, half, chunk])
                d_probs = product_nt(values_in, grads)
                delta = jnp.sum(probs * d_probs, axis=0, keepdims=True)
                d_scores = (probs * (d_probs - delta)).astype(jnp.bfloat16)
                double = pl.ds(pl.multiple_of(index * 2 * rows, LANES), 2 * rows)
                probs_all[:, double] = probs.astype(jnp.bfloat16)
                scores_all[:, double] = d_scores
                d_query = merge_heads(product(k_turn[pair], d_scores)) * HEAD_DIM**-0.5
                d_qkv[0, half, where, lanes] = d_query.astype(jnp.bfloat16)
                return carry

            lax.fori_loop(0, 2 * CHUNKS, attend_back, 0)
            query_list, grad_list = [], []
            for index in range(2 * CHUNKS):
                half, where = index // CHUNKS, chunk_rows(index % CHUNKS)
                query_list.append(split_heads(qkv[layer, 0, half, where, lanes]))
                grad_list.append(split_heads(d_heads[half, where, lanes]))
            d_keys = product(scores_all[...], jnp.concatenate(query_list, axis=0))
            d_values = product(probs_all[...], jnp.concatenate(grad_list, axis=0))
            d_qkv[1, :, :, lanes] = d_keys.astype(jnp.bfloat16).reshape(2, half_rows, LANES)
            d_qkv[2, :, :, lanes] = d_values.astype(jnp.bfloat16).reshape(2, half_rows, LANES)
            reduce_step(done + 2 + pair)

        def query_parts(index, carry, layer=layer, base=base, ex=ex):
            half, chunk = half_of(index), index % CHUNKS
            where = chunk_rows(chunk)
            part = product_nt(d_qkv[0, half, where], matrix(base))
            for j in range(1, 3):
                part = part + product_nt(d_qkv[j, half, where], matrix(base + j))
            place_part(index, ex + 3, ex + 1, part)
            return carry

        lax.fori_loop(0, 2 * CHUNKS, query_parts, 0)

        turned[...] = x_low[layer].reshape(length, width).T
        for j in range(2, -1, -1):
            put_grad(base + j, product(turned[...], d_qkv[j].reshape(length, PIECE)))
        add_sum(
            sums_base + 7,
            jnp.sum(d_qkv[0].reshape(length, PIECE).astype(jnp.float32), axis=0, keepdims=True),
            own_columns,
        )
        add_sum(
            sums_base,
            jnp.sum(d_qkv[2].reshape(length, PIECE).astype(jnp.float32), axis=0, keepdims=True),
            own_columns,
        )
        for step in range(done + 2 + pairs, done + per_layer - (1 if last else 0)):
            reduce_step(step)

    sum_finish(0, 3)
    sum_start(1, 0)
    ex = 8 * layers - 1
    for chunk in range(CHUNKS):
        where = chunk_rows(chunk)
        give_part(ex, chunk).wait_recv()
        tokens_grad_ref[where] = d_rows[where] + own_part[where] + in_part[where].astype(jnp.float32)
    sum_finish(1, 0)
    sum_start(1, 1)
    reduce_step(pieces)
    sum_finish(1, 1)
    sum_start(1, 2)
    reduce_step(pieces + 1)
    sum_finish(1, 2)
    sum_start(1, 3)
    for step in range(pieces + 2, pieces + 2 * LAG):
        reduce_step(step)
    sum_finish(1, 3)

    for step in range(3):
        small_z(step).wait_send()
        small_hop(step).wait_send()
    for chunk in range(CHUNKS):
        give_part(8 * layers - 1, chunk).wait_send()
        for layer in range(layers):
            give_rows(4 * layer, chunk, x_low.at[layer]).wait_send()
            give_rows(4 * layer + 2, chunk, h_low.at[layer]).wait_send()
            number = 4 * layers + 4 * (layers - 1 - layer)
            give_rows(number, chunk, d_low.at[layer, 0]).wait_send()
            give_rows(number + 2, chunk, d_low.at[layer, 1]).wait_send()

    def finish_grads(piece, carry):
        core_copy(piece).wait_send()
        col_copy(piece).wait_send()
        for step in range(3):
            row_copy(piece, step).wait_send()
        return carry

    lax.fori_loop(0, pieces, finish_grads, 0)


def run_step(extra, token_total, hidden_width, own, small, tokens, teacher, weights, seg_col, seg_row):
    pieces = own.shape[0]
    rows, width = tokens.shape
    length = 2 * rows
    layers = 2
    low, full = jnp.bfloat16, jnp.float32
    share = own.shape[1]
    ups = hidden_width // PIECE
    chunk = rows // CHUNKS
    pairs = PIECE // LANES
    blocks = (4, 2, 2, share, PIECE)
    dma = pltpu.SemaphoreType.DMA
    vmem = pl.BlockSpec(memory_space=pltpu.VMEM)
    return pl.pallas_call(
        functools.partial(step_kernel, extra, token_total),
        out_shape=(
            jax.ShapeDtypeStruct((rows, width), low),
            jax.ShapeDtypeStruct((rows, width), full),
            jax.ShapeDtypeStruct((pieces, share, PIECE), full),
            jax.ShapeDtypeStruct((32, width), full),
            jax.ShapeDtypeStruct((8, LANES), full),
        ),
        in_specs=[pl.BlockSpec(memory_space=pl.ANY)] + [vmem] * 6,
        out_specs=(vmem,) * 5,
        scratch_shapes=[
            pltpu.VMEM((pieces, *blocks), low),
            pltpu.VMEM((4, 2, 2, *small.shape), full),
            pltpu.VMEM((16, width), full),
            pltpu.VMEM((8, hidden_width), full),
            pltpu.VMEM((pieces, 4, 2, share, PIECE), low),
            pltpu.VMEM((pieces, 4, share, PIECE), low),
            pltpu.VMEM((pieces, 3, share, PIECE), low),
            pltpu.VMEM((layers, 2, rows, width), low),
            pltpu.VMEM((layers, 3, 2, rows, PIECE), low),
            pltpu.VMEM((layers, 2, rows, PIECE), low),
            pltpu.VMEM((layers, pairs, 2, CHUNKS, 1, 2 * chunk), full),
            pltpu.VMEM((layers, 2, rows, width), low),
            pltpu.VMEM((layers, ups, 2, rows, PIECE), low),
            pltpu.VMEM((layers, ups, 2, rows, PIECE), low),
            pltpu.VMEM((layers, 2, rows, width), full),
            pltpu.VMEM((layers, 2, rows, 1), full),
            pltpu.VMEM((rows, width), full),
            pltpu.VMEM((rows, width), full),
            pltpu.VMEM((rows, width), low),
            pltpu.VMEM((rows, width), low),
            pltpu.VMEM((rows, width), full),
            pltpu.VMEM((layers, 2, 2, rows, width), low),
            pltpu.VMEM((3, 2, rows, PIECE), low),
            pltpu.VMEM((2, rows, PIECE), low),
            pltpu.VMEM((rows, width), full),
            pltpu.VMEM((length, length), full),
            pltpu.VMEM((pairs, LANES, length), low),
            pltpu.VMEM((pairs, LANES, length), low),
            pltpu.VMEM((length, 2 * length), low),
            pltpu.VMEM((length, 2 * length), low),
            pltpu.VMEM((width, length), low),
            pltpu.VMEM((7, 32, width), full),
            pltpu.VMEM((8, LANES), full),
            pltpu.VMEM((8, LANES), full),
            dma((pieces, 3)),
            dma((pieces, 3)),
            dma((pieces, 3)),
            dma((pieces, 3)),
            dma((pieces,)),
            dma((6,)),
            dma((6,)),
            dma((8 * layers, CHUNKS)),
            dma((8 * layers, CHUNKS)),
            dma((pieces, 5)),
            dma((pieces, 5)),
            dma((2, 6)),
            dma((2, 6)),
            dma((1,)),
            dma((1,)),
        ],
        compiler_params=pltpu.CompilerParams(
            collective_id=0, has_side_effects=True, vmem_limit_bytes=67_043_328
        ),
        name="encoder_step",
    )(own, small, tokens, teacher, weights, seg_col, seg_row)


def sibling_groups(extra):
    size = lax.axis_size("fsdp")
    return [list(range(first, first + extra)) for first in range(0, size, extra)]


def widen(shard, extra, axis):
    if extra == 1:
        return shard
    return lax.all_gather(
        shard, "fsdp", axis=axis, axis_index_groups=sibling_groups(extra), tiled=True
    )


def sum_siblings(value, extra):
    if extra == 1:
        return value
    return lax.psum(value, "fsdp", axis_index_groups=sibling_groups(extra))


def shard_pieces(shard):
    layers, rows = shard.shape[0], shard.shape[1]
    return jnp.swapaxes(shard.reshape(layers, rows, -1, PIECE), 1, 2)


def on_device(
    tokens,
    segments,
    valid,
    teacher,
    attn_in,
    attn_out,
    ff_in,
    ff_out,
    biases,
    gains,
    ff_bias,
    query_bias,
):
    size = lax.axis_size("fsdp")
    extra = size // GROUP
    layers = attn_in.shape[0]
    rows_dev, width = tokens.shape[1], tokens.shape[2]
    hidden_width = ff_in.shape[2]
    seg_ids = segments[0]
    length = seg_ids.shape[0]
    tp_rank = lax.axis_index("tp")

    stacked = jnp.concatenate(
        [shard_pieces(widen(part, extra, 1)) for part in (attn_in, attn_out, ff_in, ff_out)], axis=1
    )
    own = stacked.reshape(-1, stacked.shape[2], PIECE)
    own_seg = lax.dynamic_slice_in_dim(seg_ids, tp_rank * rows_dev, rows_dev, 0)
    weight_rows = (valid[0] * (own_seg > 0).astype(jnp.int32)).astype(jnp.float32)
    counted = sum_siblings(jnp.sum(weight_rows), extra)

    share = width // GROUP
    narrow = jnp.concatenate(
        [
            widen(biases, extra, 2).reshape(-1, share),
            widen(gains, extra, 2).reshape(-1, share),
            widen(query_bias, extra, 1),
        ],
        axis=0,
    ).astype(jnp.float32)
    wide = widen(ff_bias, extra, 1).astype(jnp.float32)
    small = jnp.concatenate(
        [
            jnp.pad(narrow, ((0, 0), (0, 2 * LANES - share))),
            jnp.pad(wide, ((0, 0), (0, 2 * LANES - wide.shape[1]))),
            jnp.broadcast_to(counted, (6, 2 * LANES)),
        ],
        axis=0,
    )
    mixed, tokens_grad, grads, sums, count = run_step(
        extra,
        float(length * size),
        hidden_width,
        own,
        small,
        tokens[0],
        teacher[0],
        weight_rows[:, None],
        seg_ids[:, None],
        jnp.broadcast_to(seg_ids[None], (8, length)),
    )
    if extra > 1:
        grads = lax.psum_scatter(
            grads, "fsdp", scatter_dimension=1, axis_index_groups=sibling_groups(extra), tiled=True
        )
        sums = sum_siblings(sums, extra)
    loss = jnp.sum(sums[24]) / (count[0, 0] * width)
    grads = grads.reshape(layers, -1, grads.shape[1], PIECE)

    def shard_grad(first, number):
        part = jnp.swapaxes(grads[:, first : first + number], 1, 2)
        return part.reshape(layers, part.shape[1], -1)

    ups = hidden_width // PIECE
    place = lax.axis_index("fsdp")
    own_share = width // size
    shard_sums = lax.dynamic_slice_in_dim(sums[:16], place * own_share, own_share, 1)
    shard_sums = shard_sums.reshape(layers, 8, own_share)
    up_share = hidden_width * 2 // size
    up_sums = lax.dynamic_slice_in_dim(
        sums[16:24].reshape(layers, -1), place * up_share, up_share, 1
    )
    return (
        mixed[None],
        tokens_grad[None],
        loss,
        shard_grad(0, 3).reshape(layers, -1, 3, PIECE),
        shard_grad(3, 1),
        shard_grad(4, ups),
        shard_grad(4 + ups, ups),
        shard_sums[:, :5],
        shard_sums[:, 5:7],
        up_sums,
        shard_sums[:, 7],
    )


def solution(mesh):
    in_specs = (
        P("fsdp", "tp", None),
        P("fsdp", None),
        P("fsdp", "tp"),
        P("fsdp", "tp", None),
        P(None, "fsdp", None, "tp"),
        P(None, "fsdp", "tp"),
        P(None, "fsdp", "tp"),
        P(None, "fsdp", "tp"),
        P(None, None, "fsdp"),
        P(None, None, "fsdp"),
        P(None, "fsdp"),
        P(None, "fsdp"),
    )
    out_specs = (
        P("fsdp", "tp", None),
        P("fsdp", "tp", None),
        P(),
        P(None, "fsdp", None, "tp"),
        P(None, "fsdp", "tp"),
        P(None, "fsdp", "tp"),
        P(None, "fsdp", "tp"),
        P(None, None, "fsdp"),
        P(None, None, "fsdp"),
        P(None, "fsdp"),
        P(None, "fsdp"),
    )
    return jax.shard_map(
        on_device, mesh=mesh, in_specs=in_specs, out_specs=out_specs, check_vma=False
    )
```

```python
import functools

import jax
import jax.numpy as jnp
from jax import lax
from jax.experimental import pallas as pl
from jax.experimental.pallas import tpu as pltpu
from jax.sharding import PartitionSpec as P

HEAD_DIM = 64
MESH = pl.DeviceIdType.MESH
PIECE = 384
CHUNKS = 2
LANES = 128
GROUP = 16
WINDOW = 3
PUMPS = (
    {
        "projected": (4,),
        "attend": ((1, 5), (2, 6)),
        "norm": ((0, 7), (1, 8)),
        "feed own": (9,),
        "feed": ((0, 10),),
        "fed": (11, 12),
        "sent": (13,),
        "kept": (14,),
        "end": ((0, 15), (1, 16)),
    },
    {
        "own projected": (17, 18),
        "projected": (19,),
        "attend": ((2, 20),),
        "norm": ((0, 21), (1, 22)),
        "feed": ((0, 23), (1, 24)),
    },
)
LAG = 2

epsilon = 1e-05
root_half = 0.7071067811865476
inv_root_tau = 0.3989422804014327
masked = -1e30


def product(left, right):
    return lax.dot_general(left, right, (((1,), (0,)), ((), ())), preferred_element_type=jnp.float32)


def product_nt(left, right):
    return lax.dot_general(left, right, (((1,), (1,)), ((), ())), preferred_element_type=jnp.float32)


def norm_stats(total):
    centred = total - jnp.mean(total, axis=-1, keepdims=True)
    inverse = lax.rsqrt(jnp.mean(centred * centred, axis=-1, keepdims=True) + epsilon)
    return centred * inverse, inverse


def norm_back(grad_out, normed, inverse, gain):
    scaled = grad_out * gain
    return inverse * (
        scaled
        - jnp.mean(scaled, axis=-1, keepdims=True)
        - normed * jnp.mean(scaled * normed, axis=-1, keepdims=True)
    )


def step_kernel(
    extra,
    token_total,
    attn_in_ref,
    attn_out_ref,
    ff_in_ref,
    ff_out_ref,
    tokens_ref,
    biases_ref,
    gains_ref,
    ff_bias_ref,
    query_ref,
    teacher_ref,
    valid_ref,
    seg_ref,
    count_in_ref,
    mixed_ref,
    tokens_grad_ref,
    grad_ref,
    sums_ref,
    count_ref,
    mats,
    small_all,
    param,
    ff_shift,
    from_core,
    from_col,
    from_row,
    x_low,
    qkv,
    heads,
    log_sum,
    h_low,
    act,
    slope,
    normed,
    inverse,
    stream,
    out_part,
    in_part,
    own_part,
    d_low,
    d_qkv,
    d_heads,
    mask,
    pair_turn,
    probs_all,
    scores_all,
    turned,
    sums_in,
    count_mine,
    count_theirs,
    small_ref,
    weight_ref,
    z_send,
    z_recv,
    hop_send,
    hop_recv,
    local_sem,
    s_send,
    s_recv,
    x_send,
    x_recv,
    r_send,
    r_recv,
    a_send,
    a_recv,
    c_send,
    c_recv,
):
    pieces = mats.shape[0]
    layers = x_low.shape[0]
    per_layer = pieces // layers
    half_rows = tokens_ref.shape[0]
    width = tokens_ref.shape[1]
    length = 2 * half_rows
    rows = half_rows // CHUNKS
    pairs = PIECE // LANES
    ups = act.shape[3] // PIECE

    spot = lax.axis_index("fsdp") // extra
    rest = lax.axis_index("fsdp") % extra
    t = lax.axis_index("tp")
    z, y, c = spot // 4, (spot // 2) % 2, spot % 2

    def peer(row, col, core):
        return {"fsdp": ((row * 2 + col) * 2 + core) * extra + rest, "tp": t}

    z_peers = [peer((z + step) % 4, y, c) for step in (1, 2, 3)]
    y_peer = peer(z, 1 - y, c)
    c_peer = peer(z, y, 1 - c)
    x_peer = {"fsdp": lax.axis_index("fsdp"), "tp": 1 - t}
    shards = []
    for layer in range(layers):
        shards += [attn_in_ref.at[layer, j] for j in range(3)]
        for source in (attn_out_ref, ff_in_ref, ff_out_ref):
            shards += [
                source.at[layer, :, pl.ds(j * PIECE, PIECE)] for j in range(source.shape[2] // PIECE)
            ]

    def own_copy(piece):
        return pltpu.make_async_copy(shards[piece], mats.at[piece, z, y, c], local_sem.at[piece])

    own_tokens = pltpu.make_async_copy(tokens_ref, x_low.at[0, t], local_sem.at[pieces])
    own_tokens.start()
    for piece in range(pieces):
        own_copy(piece).start()
    everyone = (*z_peers, y_peer, c_peer, x_peer)
    barrier = pltpu.get_barrier_semaphore()
    for other in everyone:
        pl.semaphore_signal(barrier, inc=1, device_id=other, device_id_type=MESH)
    pl.semaphore_wait(barrier, len(everyone))

    def remote(src, dst, send_sem, recv_sem, device):
        return pltpu.make_async_remote_copy(
            src_ref=src,
            dst_ref=dst,
            send_sem=send_sem,
            recv_sem=recv_sem,
            device_id=device,
            device_id_type=MESH,
        )

    def z_copy(piece, step):
        return remote(
            mats.at[piece, z, y, c],
            mats.at[piece, z, y, c],
            z_send.at[piece, step],
            z_recv.at[piece, step],
            z_peers[step],
        )

    def push(piece):
        for step in range(3):
            z_copy(piece, step).start()

    def hop_copy(piece, kind):
        column = 1 - y if kind == 2 else y
        block = mats.at[piece, :, column, c]
        return remote(
            block,
            block,
            hop_send.at[piece, kind],
            hop_recv.at[piece, kind],
            y_peer if kind == 0 else c_peer,
        )

    def small_z(step):
        block = small_all.at[z, y, c]
        return remote(small_ref, block, s_send.at[step], s_recv.at[step], z_peers[step])

    def small_hop(kind):
        column = 1 - y if kind == 2 else y
        block = small_all.at[:, column, c]
        return remote(
            block, block, s_send.at[3 + kind], s_recv.at[3 + kind], y_peer if kind == 0 else c_peer
        )

    def first_half(piece):
        for step in range(3):
            z_copy(piece, step).wait_recv()
        if isinstance(piece, int):
            if piece + WINDOW < pieces:
                push(piece + WINDOW)
        else:
            pl.when(piece + WINDOW < pieces)(lambda: push(piece + WINDOW))
        hop_copy(piece, 0).start()
        hop_copy(piece, 1).start()

    def second_half(piece):
        hop_copy(piece, 0).wait_recv()
        hop_copy(piece, 2).start()

    def advance(step):
        if isinstance(step, int):
            if step < pieces:
                first_half(step)
            if 0 < step <= pieces:
                second_half(step - 1)
        else:
            pl.when(step < pieces)(lambda: first_half(step))
            pl.when(step <= pieces)(lambda: second_half(step - 1))

    def need(first, count=1):
        for piece in range(first, first + count):
            hop_copy(piece, 1).wait_recv()
            hop_copy(piece, 2).wait_recv()

    def chunk_rows(chunk):
        if isinstance(chunk, int):
            return pl.ds(chunk * rows, rows)
        return pl.ds(pl.multiple_of(chunk * rows, rows), rows)

    def give_rows(number, chunk, block):
        place = block.at[t, chunk_rows(chunk)]
        return remote(place, place, x_send.at[number, chunk], x_recv.at[number, chunk], x_peer)

    def give_part(number, chunk):
        return remote(
            out_part.at[chunk_rows(chunk)],
            in_part.at[chunk_rows(chunk)],
            x_send.at[number, chunk],
            x_recv.at[number, chunk],
            x_peer,
        )

    def put_part(number, previous, chunk, value):
        if previous is not None:
            give_part(previous, chunk).wait_send()
        out_part[chunk_rows(chunk)] = value.astype(jnp.bfloat16)
        give_part(number, chunk).start()

    def place_part(index, number, previous, value):
        chunk = index % CHUNKS

        @pl.when(index < CHUNKS)
        def _():
            put_part(number, previous, chunk, value)

        @pl.when(index >= CHUNKS)
        def _():
            own_part[chunk_rows(chunk)] = value

    def core_copy(piece):
        return remote(
            mats.at[piece, :, :, 1 - c],
            from_core.at[piece],
            r_send.at[piece, 0],
            r_recv.at[piece, 0],
            c_peer,
        )

    def col_copy(piece):
        return remote(
            from_core.at[piece, :, 1 - y],
            from_col.at[piece],
            r_send.at[piece, 1],
            r_recv.at[piece, 1],
            y_peer,
        )

    def row_copy(piece, step):
        return remote(
            from_core.at[piece, (z + step + 1) % 4, y],
            from_row.at[piece, step],
            r_send.at[piece, 2 + step],
            r_recv.at[piece, 2 + step],
            z_peers[step],
        )

    def reduce_core(piece):
        core_copy(piece).wait_recv()

        def add_row(row, carry):
            from_core[piece, row] = (
                from_core[piece, row].astype(jnp.float32)
                + mats[piece, row, :, c].astype(jnp.float32)
            ).astype(jnp.bfloat16)
            return carry

        lax.fori_loop(0, 4, add_row, 0)
        col_copy(piece).start()

    def reduce_col(piece):
        col_copy(piece).wait_recv()

        def add_row(row, carry):
            from_core[piece, row, y] = (
                from_core[piece, row, y].astype(jnp.float32) + from_col[piece, row].astype(jnp.float32)
            ).astype(jnp.bfloat16)
            return carry

        lax.fori_loop(0, 4, add_row, 0)
        for step in range(3):
            row_copy(piece, step).start()

    def reduce_row(piece):
        for step in range(3):
            row_copy(piece, step).wait_recv()
        total = from_core[piece, z, y].astype(jnp.float32)
        for step in range(3):
            total = total + from_row[piece, step].astype(jnp.float32)
        grad_ref[piece] = total

    def reduce_step(index):
        if isinstance(index, int):
            if index < pieces:
                reduce_core(pieces - 1 - index)
            if 0 <= index - LAG < pieces:
                reduce_col(pieces - 1 - (index - LAG))
            if 0 <= index - 2 * LAG < pieces:
                reduce_row(pieces - 1 - (index - 2 * LAG))
        else:
            pl.when(index < pieces)(lambda: reduce_core(pieces - 1 - index))
            pl.when((index >= LAG) & (index < pieces + LAG))(
                lambda: reduce_col(pieces - 1 - (index - LAG))
            )
            pl.when(index >= 2 * LAG)(lambda: reduce_row(pieces - 1 - (index - 2 * LAG)))

    def put_grad(piece, value):
        mats[piece] = value.astype(jnp.bfloat16).reshape(mats.shape[1:])
        core_copy(piece).start()

    sum_blocks = ((8, 24), (0, 8))

    def sum_copy(phase, step):
        first, count = sum_blocks[phase]
        part = sums_ref.at[pl.ds(first, count)]
        slot = step if step < 3 else 3 + z
        device = (c_peer, y_peer, x_peer)[step] if step < 3 else z_peers[step - 3]
        return remote(
            part,
            sums_in.at[slot, pl.ds(first, count)],
            a_send.at[phase, step],
            a_recv.at[phase, step],
            device,
        )

    def sum_start(phase, step):
        if step < 3:
            sum_copy(phase, step).start()
            return
        first, count = sum_blocks[phase]
        for k in range(3, 6):
            sum_copy(phase, k).start()
        sums_in[3 + z, pl.ds(first, count)] = sums_ref[pl.ds(first, count)]

    def sum_finish(phase, step):
        first, count = sum_blocks[phase]
        block = pl.ds(first, count)
        if step < 3:
            sum_copy(phase, step).wait()
            sums_ref[block] = sums_ref[block] + sums_in[step, block]
            return
        for k in range(3, 6):
            sum_copy(phase, k).wait()
        sums_ref[block] = (sums_in[3, block] + sums_in[4, block]) + (
            sums_in[5, block] + sums_in[6, block]
        )

    def add_sum(row, value, column=None):
        if column is None:
            sums_ref[pl.ds(row, 1)] += value
        else:
            sums_ref[pl.ds(row, 1), column] += value

    def par(row):
        return param[pl.ds(row, 1)]

    def matrix(piece, count=1):
        parts = [mats[piece + j].reshape(width, PIECE) for j in range(count)]
        return parts[0] if count == 1 else jnp.concatenate(parts, axis=1)

    def turn(source):
        def turn_rows(index, carry):
            half, chunk = index // CHUNKS, index % CHUNKS
            columns = pl.ds(pl.multiple_of(index * rows, LANES), rows)
            turned[:, columns] = source[half, chunk_rows(chunk)].T
            return carry

        lax.fori_loop(0, 2 * CHUNKS, turn_rows, 0)

    own_columns = pl.ds(pl.multiple_of(t * PIECE, LANES), PIECE)

    for piece in range(WINDOW):
        own_copy(piece).wait()
        push(piece)
    for chunk in range(CHUNKS):
        place = x_low.at[0, t, chunk_rows(chunk)]
        remote(
            tokens_ref.at[chunk_rows(chunk)],
            place,
            x_send.at[0, chunk],
            x_recv.at[0, chunk],
            x_peer,
        ).start()
    seg_q = seg_ref[...].astype(jnp.float32)
    half_lanes = pl.ds(pl.multiple_of(t * half_rows, LANES), half_rows)
    counted_rows = valid_ref[...] * (seg_ref[:, half_lanes] > 0).astype(jnp.int32)
    weights = jnp.broadcast_to(counted_rows.astype(jnp.float32), (8, half_rows)).T
    weight_ref[...] = weights[:, :1]
    if count_in_ref is None:
        count_local = jnp.sum(weights[:, :1], axis=0, keepdims=True)
    else:
        count_local = count_in_ref[:1, :1]
    small_ref[...] = jnp.zeros_like(small_ref)
    share = biases_ref.shape[2]
    kinds = biases_ref.shape[0]
    for layer in range(layers):
        for kind in range(kinds):
            line = biases_ref[kind].astype(jnp.float32)[layer : layer + 1]
            small_ref[pl.ds(layer * kinds + kind, 1), pl.ds(0, share)] = line
        small_ref[pl.ds(10 + layer * 2, 2), pl.ds(0, share)] = gains_ref[layer].astype(jnp.float32)
    small_ref[pl.ds(14, layers), pl.ds(0, share)] = query_ref[...].astype(jnp.float32)
    small_ref[pl.ds(16, layers), pl.ds(0, ff_bias_ref.shape[1])] = ff_bias_ref[...].astype(jnp.float32)
    small_ref[pl.ds(18, 6)] = jnp.broadcast_to(count_local, (6, small_ref.shape[1]))
    own_tokens.wait()
    stream[...] = x_low[0, t].astype(jnp.float32)
    small_all[z, y, c] = small_ref[...]
    for step in range(3):
        small_z(step).start()
    for piece in range(WINDOW, pieces):
        own_copy(piece).wait()
    seg_k = jnp.broadcast_to(seg_q, (8, length)).T[:, :1]
    allowed = (seg_k > 0) & ((seg_k == seg_q) | (seg_q == 0))
    mask[...] = jnp.where(allowed, 0.0, masked)
    sums_ref[...] = jnp.zeros_like(sums_ref)
    lane = lax.broadcasted_iota(jnp.int32, (1, LANES), 1)
    low_lanes = lane < HEAD_DIM
    low_sub = lax.broadcasted_iota(jnp.int32, (LANES, 1), 0) < HEAD_DIM

    for step in range(3):
        small_z(step).wait_recv()
    small_hop(0).start()
    small_hop(1).start()
    small_hop(0).wait_recv()
    small_hop(2).start()
    small_hop(1).wait_recv()
    small_hop(2).wait_recv()
    param[...] = jnp.zeros_like(param)
    ff_shift[...] = jnp.zeros_like(ff_shift)
    counted = jnp.zeros((8, LANES), jnp.float32)
    for place in range(GROUP):
        block = small_all[place // 4, (place // 2) % 2, place % 2]
        offset = place * share
        tile = min(offset // LANES * LANES, width - 2 * LANES)
        shifted = block[:16] if offset == tile else pltpu.roll(block[:16], offset - tile, 1)
        param[pl.ds(0, 16), pl.ds(tile, 2 * LANES)] += shifted
        counted = counted + block[16:24, :LANES]
    hidden_share = ff_shift.shape[1] // (GROUP // 2)
    for place in range(GROUP // 2):
        block = small_all[2 * t + place // 4, (place // 2) % 2, place % 2][16:24]
        offset = place * hidden_share
        tile = offset // LANES * LANES
        if offset != tile:
            block = pltpu.roll(block, offset - tile, 1)
        ff_shift[:, pl.ds(tile, 2 * LANES)] += block
    count_mine[...] = counted
    remote(count_mine, count_theirs, c_send.at[0], c_recv.at[0], x_peer).start()

    def split_heads(pair):
        return jnp.concatenate(
            [jnp.where(low_lanes, pair, 0), jnp.where(low_lanes, 0, pair)], axis=0
        ).astype(pair.dtype)

    def merge_heads(turned_pair):
        size = turned_pair.shape[1] // 2
        return jnp.where(low_sub, turned_pair[:, :size], turned_pair[:, size:]).T

    def pair_lanes(pair):
        return pl.ds(pl.multiple_of(pair * LANES, LANES), LANES)

    def pair_rows(layer, which, pair):
        return qkv[layer, which, :, :, pair_lanes(pair)].reshape(length, LANES)

    def half_of(index):
        return jnp.where(index < CHUNKS, 1 - t, t)

    for layer in range(layers):
        base = layer * per_layer
        ex = 4 * layer
        early = layer == 0

        def project(half, first, count, layer=layer, base=base):
            acc = product(x_low[layer, half], matrix(base + first, count))
            for j in range(first, first + count):
                part = acc[:, (j - first) * PIECE : (j - first + 1) * PIECE]
                if j == 0:
                    part = part + param[pl.ds(14 + layer, 1), own_columns]
                if j == 2:
                    part = part + param[pl.ds(layer * 5, 1), own_columns]
                low = part.astype(jnp.bfloat16)
                if j == 0:
                    low = low * jnp.bfloat16(HEAD_DIM**-0.5)
                qkv[layer, j, half] = low

        def pump(slot, index=None, layer=layer):
            steps = PUMPS[layer].get(slot, ())
            if index is None:
                for step in steps:
                    advance(step)
                return
            for place, step in steps:
                pl.when(index == place)(lambda step=step: advance(step))

        if early:
            advance(0)
            for j in range(3):
                advance(j + 1)
                need(base + j)
                project(t, j, 1)
        else:
            need(base, 3)
            project(t, 0, 3)
        pump("own projected")
        for chunk in range(CHUNKS):
            give_rows(ex, chunk, x_low.at[layer]).wait_recv()
        project(1 - t, 0, 3)
        pump("projected")
        for pair in range(pairs):
            pair_turn[pair] = pair_rows(layer, 2, pair).T

        def attend(index, carry, layer=layer, base=base, ex=ex, early=early, pump=pump):
            half, chunk = half_of(index), index % CHUNKS
            where = chunk_rows(chunk)
            columns = pl.ds(pl.multiple_of(half * half_rows + chunk * rows, rows), rows)
            bias = mask[:, columns]
            bias = jnp.concatenate([bias, bias], axis=1)
            pump("attend", index)
            for pair in range(pairs):
                queries = split_heads(qkv[layer, 0, half, where, pair_lanes(pair)])
                scores = product_nt(pair_rows(layer, 1, pair), queries) + bias
                highest = jnp.max(scores, axis=0, keepdims=True)
                exponent = jnp.exp(scores - highest)
                total = jnp.sum(exponent, axis=0, keepdims=True)
                probs = (exponent * (1.0 / total)).astype(jnp.bfloat16)
                log_sum[layer, pair, half, chunk] = highest + jnp.log(total)
                mixed_pair = merge_heads(product(pair_turn[pair], probs))
                heads[layer, half, where, pair_lanes(pair)] = mixed_pair.astype(jnp.bfloat16)
            pl.when(index == 0)(lambda: need(base + 3))
            part = product_nt(heads[layer, half, where], matrix(base + 3))
            place_part(index, ex + 1, None if early else ex - 1, part)
            return carry

        lax.fori_loop(0, 2 * CHUNKS, attend, 0)

        def norm_rows(chunk, carry, layer=layer, ex=ex, pump=pump):
            where = chunk_rows(chunk)
            pump("norm", chunk)
            give_part(ex + 1, chunk).wait_recv()
            total = (
                stream[where] + own_part[where] + in_part[where].astype(jnp.float32) + par(layer * 5 + 1)
            )
            unit, scale = norm_stats(total)
            normed[layer, 0, where] = unit
            inverse[layer, 0, where] = scale
            value = unit * par(10 + layer * 2) + par(layer * 5 + 2)
            stream[where] = value
            h_low[layer, t, where] = value.astype(jnp.bfloat16)
            give_rows(ex + 2, chunk, h_low.at[layer]).start()
            return carry

        lax.fori_loop(0, CHUNKS, norm_rows, 0)

        need(base + 4, 4)

        def feed(half, where, layer=layer, base=base):
            source = h_low[layer, half, where]
            for j in range(0, ups, 2):
                lanes = pl.ds(j * PIECE, 2 * PIECE)
                u = product(source, matrix(base + 4 + j, 2)) + ff_shift[pl.ds(layer, 1), lanes]
                cdf = 0.5 * (1.0 + lax.erf(u * root_half))
                bell = jnp.exp(-0.5 * u * u) * inv_root_tau
                act[layer, half, where, lanes] = (u * cdf).astype(jnp.bfloat16)
                slope[layer, half, where, lanes] = (cdf + u * bell).astype(jnp.bfloat16)

        def feed_peer(chunk, carry, layer=layer, ex=ex, feed=feed, pump=pump):
            pump("feed", chunk)
            give_rows(ex + 2, chunk, h_low.at[layer]).wait_recv()
            feed(1 - t, chunk_rows(chunk))
            return carry

        def down(half, where, layer=layer, base=base):
            return product_nt(act[layer, half, where], matrix(base + 8, ups))

        def down_peer(chunk, carry, down=down, ex=ex):
            put_part(ex + 3, ex + 1, chunk, down(1 - t, chunk_rows(chunk)))
            return carry

        everything = pl.ds(0, half_rows)
        pump("feed own")
        feed(t, everything)
        lax.fori_loop(0, CHUNKS, feed_peer, 0)
        pump("fed")
        need(base + 8, 4)
        lax.fori_loop(0, CHUNKS, down_peer, 0)
        pump("sent")
        own_part[...] = down(t, everything)
        pump("kept")

        if layer == layers - 1:
            remote(count_mine, count_theirs, c_send.at[0], c_recv.at[0], x_peer).wait()
            count_all = (count_mine[...] + count_theirs[...])[2:3, :1]
            count_ref[...] = jnp.broadcast_to(count_all, count_ref.shape)
            loss_scale = token_total / count_all
        def end_rows(chunk, carry, layer=layer, ex=ex, pump=pump):
            where = chunk_rows(chunk)
            give_part(ex + 3, chunk).wait_recv()
            total = (
                stream[where] + own_part[where] + in_part[where].astype(jnp.float32) + par(layer * 5 + 3)
            )
            unit, scale = norm_stats(total)
            normed[layer, 1, where] = unit
            inverse[layer, 1, where] = scale
            value = unit * par(11 + layer * 2) + par(layer * 5 + 4)
            if layer < layers - 1:
                stream[where] = value
                x_low[layer + 1, t, where] = value.astype(jnp.bfloat16)
                give_rows(ex + 4, chunk, x_low.at[layer + 1]).start()
            else:
                mixed_ref[where] = value.astype(jnp.bfloat16)
                deviation = value - teacher_ref[where].astype(jnp.float32)
                weighted = weight_ref[where] * deviation
                add_sum(24, jnp.sum(weighted * deviation, axis=0, keepdims=True))
                stream[where] = loss_scale * weighted
            pump("end", chunk)
            return carry

        lax.fori_loop(0, CHUNKS, end_rows, 0)

    def finish_gather(piece, carry):
        for k in range(3):
            z_copy(piece, k).wait_send()
            hop_copy(piece, k).wait_send()
        return carry

    lax.fori_loop(0, pieces, finish_gather, 0)

    for layer in range(layers - 1, -1, -1):
        base = layer * per_layer
        ex = 4 * layers + 4 * (layers - 1 - layer)
        last = layer == layers - 1
        done = 0 if last else per_layer
        sums_base = layer * 8

        def top_rows(chunk, carry, layer=layer, ex=ex, last=last, sums_base=sums_base):
            where = chunk_rows(chunk)
            if not last:
                give_part(ex - 1, chunk).wait_recv()
                stream[where] += own_part[where] + in_part[where].astype(jnp.float32)
            grad_out, unit = stream[where], normed[layer, 1, where]
            below = norm_back(grad_out, unit, inverse[layer, 1, where], par(11 + layer * 2))
            d_low[layer, 0, t, where] = below.astype(jnp.bfloat16)
            give_rows(ex, chunk, d_low.at[layer, 0]).start()
            stream[where] = below
            add_sum(sums_base + 6, jnp.sum(grad_out * unit, axis=0, keepdims=True))
            add_sum(sums_base + 4, jnp.sum(grad_out, axis=0, keepdims=True))
            add_sum(sums_base + 3, jnp.sum(below, axis=0, keepdims=True))
            return carry

        lax.fori_loop(0, CHUNKS, top_rows, 0)
        if not last:
            reduce_step(9)

        def feed_back(half, where, layer=layer, base=base):
            source = d_low[layer, 0, half, where]
            per_row = width // PIECE
            for j in range(0, ups, 2):
                lanes = pl.ds(j * PIECE, 2 * PIECE)
                du = product(source, matrix(base + 8 + j, 2)) * slope[
                    layer, half, where, lanes
                ].astype(jnp.float32)
                total = jnp.sum(du, axis=0, keepdims=True)
                for k in range(j, j + 2):
                    add_sum(
                        16 + layer * 4 + 2 * t + k // per_row,
                        total[:, (k - j) * PIECE : (k - j + 1) * PIECE],
                        pl.ds(k % per_row * PIECE, PIECE),
                    )
                slope[layer, half, where, lanes] = du.astype(jnp.bfloat16)

        def up_back(half, where, layer=layer, base=base):
            return product_nt(slope[layer, half, where], matrix(base + 4, ups))

        def feed_back_peer(chunk, carry, layer=layer, ex=ex, last=last, feed_back=feed_back, up_back=up_back):
            if not last:
                reduce_step(10 + chunk)
            where = chunk_rows(chunk)
            give_rows(ex, chunk, d_low.at[layer, 0]).wait_recv()
            feed_back(1 - t, where)
            put_part(ex + 1, 4 * layers - 1 if last else ex - 1, chunk, up_back(1 - t, where))
            return carry

        feed_back(t, everything)
        lax.fori_loop(0, CHUNKS, feed_back_peer, 0)

        def mid_rows(chunk, layer=layer, ex=ex, sums_base=sums_base):
            where = chunk_rows(chunk)
            give_part(ex + 1, chunk).wait_recv()
            grad_out = stream[where] + own_part[where] + in_part[where].astype(jnp.float32)
            unit = normed[layer, 0, where]
            below = norm_back(grad_out, unit, inverse[layer, 0, where], par(10 + layer * 2))
            d_low[layer, 1, t, where] = below.astype(jnp.bfloat16)
            give_rows(ex + 2, chunk, d_low.at[layer, 1]).start()
            stream[where] = below
            add_sum(sums_base + 5, jnp.sum(grad_out * unit, axis=0, keepdims=True))
            add_sum(sums_base + 2, jnp.sum(grad_out, axis=0, keepdims=True))
            add_sum(sums_base + 1, jnp.sum(below, axis=0, keepdims=True))

        def pair_grad(piece, left, right, j):
            lanes = pl.ds(j * PIECE, 2 * PIECE)
            if not isinstance(j, int):
                lanes = pl.ds(pl.multiple_of(j * PIECE, LANES), 2 * PIECE)
            both = product(left, right[:, :, lanes].reshape(length, 2 * PIECE))
            put_grad(piece + 1, both[:, PIECE:])
            put_grad(piece, both[:, :PIECE])

        def up_grad(j, layer=layer, base=base, pair_grad=pair_grad):
            pair_grad(base + 4 + j, turned[...], slope.at[layer], j)

        turn(d_low.at[layer, 0])

        def down_grads(index, carry, layer=layer, base=base, pair_grad=pair_grad):
            j = ups - 2 - 2 * index
            pair_grad(base + 8 + j, turned[...], act.at[layer], j)
            return carry

        lax.fori_loop(0, ups // 2, down_grads, 0)
        if not last:
            sum_start(0, 0)
        own_part[...] = up_back(t, everything)
        mid_rows(0)
        reduce_step(done)
        if not last:
            sum_finish(0, 0)
            sum_start(0, 1)
        turn(h_low.at[layer])
        up_grad(ups - 2)
        mid_rows(1)
        reduce_step(done + 1)
        if not last:
            sum_finish(0, 1)
            sum_start(0, 2)
        for j in range(ups - 4, -1, -2):
            up_grad(j)
        d_heads[t] = product(d_low[layer, 1, t], matrix(base + 3)).astype(jnp.bfloat16)
        for pair in range(pairs):
            pair_turn[pair] = pair_rows(layer, 1, pair).T
        reduce_step(done + 2)
        if not last:
            sum_finish(0, 2)
            sum_start(0, 3)
        reduce_step(done + 3)
        for chunk in range(CHUNKS):
            give_rows(ex + 2, chunk, d_low.at[layer, 1]).wait_recv()
        d_heads[1 - t] = product(d_low[layer, 1, 1 - t], matrix(base + 3)).astype(jnp.bfloat16)

        def pair_back(pair, carry, layer=layer, done=done):
            lanes = pair_lanes(pair)
            keys_in, values_in = pair_rows(layer, 1, pair), pair_rows(layer, 2, pair)

            def attend_back(index, carry, layer=layer, pair=pair, lanes=lanes, done=done):
                spent = pair * 2 * CHUNKS + index
                pl.when(spent % 3 == 2)(lambda: reduce_step(done + 4 + spent // 3))
                half, chunk = index // CHUNKS, index % CHUNKS
                where = chunk_rows(chunk)
                columns = pl.ds(pl.multiple_of(index * rows, rows), rows)
                bias = mask[:, columns]
                bias = jnp.concatenate([bias, bias], axis=1)
                keys_in, values_in = pair_rows(layer, 1, pair), pair_rows(layer, 2, pair)
                queries = split_heads(qkv[layer, 0, half, where, lanes])
                grads = split_heads(d_heads[half, where, lanes])
                scores = product_nt(keys_in, queries) + bias
                probs = jnp.exp(scores - log_sum[layer, pair, half, chunk])
                d_probs = product_nt(values_in, grads)
                delta = jnp.sum(probs * d_probs, axis=0, keepdims=True)
                d_scores = (probs * (d_probs - delta)).astype(jnp.bfloat16)
                double = pl.ds(pl.multiple_of(index * 2 * rows, LANES), 2 * rows)
                probs_all[:, double] = probs.astype(jnp.bfloat16)
                scores_all[:, double] = d_scores
                d_query = merge_heads(product(pair_turn[pair], d_scores)) * HEAD_DIM**-0.5
                d_qkv[0, half, where, lanes] = d_query.astype(jnp.bfloat16)
                return carry

            lax.fori_loop(0, 2 * CHUNKS, attend_back, 0)
            query_list, grad_list = [], []
            for index in range(2 * CHUNKS):
                half, where = index // CHUNKS, chunk_rows(index % CHUNKS)
                query_list.append(split_heads(qkv[layer, 0, half, where, lanes]))
                grad_list.append(split_heads(d_heads[half, where, lanes]))
            d_keys = product(scores_all[...], jnp.concatenate(query_list, axis=0))
            d_values = product(probs_all[...], jnp.concatenate(grad_list, axis=0))
            d_qkv[1, :, :, lanes] = d_keys.astype(jnp.bfloat16).reshape(2, half_rows, LANES)
            d_qkv[2, :, :, lanes] = d_values.astype(jnp.bfloat16).reshape(2, half_rows, LANES)
            return carry

        lax.fori_loop(0, pairs, pair_back, 0)

        def query_parts(index, carry, layer=layer, base=base, ex=ex):
            half, chunk = half_of(index), index % CHUNKS
            where = chunk_rows(chunk)
            parts = jnp.concatenate([d_qkv[j, half, where] for j in range(3)], axis=1)
            part = product_nt(parts, matrix(base, 3))
            place_part(index, ex + 3, ex + 1, part)
            return carry

        add_sum(
            sums_base + 7,
            jnp.sum(d_qkv[0].reshape(length, PIECE).astype(jnp.float32), axis=0, keepdims=True),
            own_columns,
        )
        add_sum(
            sums_base,
            jnp.sum(d_qkv[2].reshape(length, PIECE).astype(jnp.float32), axis=0, keepdims=True),
            own_columns,
        )
        if not last:
            sum_start(1, 0)
        lax.fori_loop(0, 2 * CHUNKS, query_parts, 0)
        turn(d_low.at[layer, 1])
        put_grad(base + 3, product(turned[...], heads[layer].reshape(length, PIECE)))
        turn(x_low.at[layer])
        for j in range(2, -1, -1):
            put_grad(base + j, product(turned[...], d_qkv[j].reshape(length, PIECE)))
        reduce_step(done + 8)

    sum_finish(1, 0)
    sum_start(1, 1)
    ex = 8 * layers - 1
    for chunk in range(CHUNKS):
        where = chunk_rows(chunk)
        give_part(ex, chunk).wait_recv()
        tokens_grad_ref[where] = stream[where] + own_part[where] + in_part[where].astype(jnp.float32)
    sum_finish(0, 3)
    sum_finish(1, 1)
    sum_start(1, 2)
    reduce_step(pieces - 3)
    sum_finish(1, 2)
    sum_start(1, 3)

    def drain(step, carry):
        reduce_step(step)
        return carry

    lax.fori_loop(pieces - 2, pieces + 2 * LAG, drain, 0)
    sum_finish(1, 3)

    for step in range(3):
        small_z(step).wait_send()
        small_hop(step).wait_send()
    for chunk in range(CHUNKS):
        give_part(8 * layers - 1, chunk).wait_send()
        for layer in range(layers):
            give_rows(4 * layer, chunk, x_low.at[layer]).wait_send()
            give_rows(4 * layer + 2, chunk, h_low.at[layer]).wait_send()
            number = 4 * layers + 4 * (layers - 1 - layer)
            give_rows(number, chunk, d_low.at[layer, 0]).wait_send()
            give_rows(number + 2, chunk, d_low.at[layer, 1]).wait_send()

    def finish_grads(piece, carry):
        core_copy(piece).wait_send()
        col_copy(piece).wait_send()
        for step in range(3):
            row_copy(piece, step).wait_send()
        return carry

    lax.fori_loop(0, pieces, finish_grads, 0)


def run_step(extra, token_total, matrices, vectors, tokens, teacher, valid, seg_ids, counted):
    attn_in, attn_out, ff_in, ff_out = matrices
    rows, width = tokens.shape
    length = 2 * rows
    layers, share, hidden_width = ff_in.shape
    ups = hidden_width // PIECE
    pieces = layers * (4 + 2 * ups)
    low, full = jnp.bfloat16, jnp.float32
    chunk = rows // CHUNKS
    pairs = PIECE // LANES
    blocks = (4, 2, 2, share, PIECE)
    dma = pltpu.SemaphoreType.DMA
    vmem = pl.BlockSpec(memory_space=pltpu.VMEM)
    operands = [*matrices, tokens, *vectors, teacher, valid, seg_ids]
    kernel = functools.partial(step_kernel, extra, token_total)
    if counted is None:
        inputs = len(operands)

        def body(*refs):
            kernel(*refs[:inputs], None, *refs[inputs:])

    else:
        operands.append(counted)
        body = kernel
    return pl.pallas_call(
        body,
        out_shape=(
            jax.ShapeDtypeStruct((rows, width), low),
            jax.ShapeDtypeStruct((rows, width), full),
            jax.ShapeDtypeStruct((pieces, share, PIECE), full),
            jax.ShapeDtypeStruct((32, width), full),
            jax.ShapeDtypeStruct((8, LANES), full),
        ),
        in_specs=[pl.BlockSpec(memory_space=pl.ANY)] * 5 + [vmem] * (len(operands) - 5),
        out_specs=(vmem,) * 5,
        scratch_shapes=[
            pltpu.VMEM((pieces, *blocks), low),
            pltpu.VMEM((4, 2, 2, 24, 2 * LANES), full),
            pltpu.VMEM((16, width), full),
            pltpu.VMEM((8, hidden_width), full),
            pltpu.VMEM((pieces, 4, 2, share, PIECE), low),
            pltpu.VMEM((pieces, 4, share, PIECE), low),
            pltpu.VMEM((pieces, 3, share, PIECE), low),
            pltpu.VMEM((layers, 2, rows, width), low),
            pltpu.VMEM((layers, 3, 2, rows, PIECE), low),
            pltpu.VMEM((layers, 2, rows, PIECE), low),
            pltpu.VMEM((layers, pairs, 2, CHUNKS, 1, 2 * chunk), full),
            pltpu.VMEM((layers, 2, rows, width), low),
            pltpu.VMEM((layers, 2, rows, hidden_width), low),
            pltpu.VMEM((layers, 2, rows, hidden_width), low),
            pltpu.VMEM((layers, 2, rows, width), full),
            pltpu.VMEM((layers, 2, rows, 1), full),
            pltpu.VMEM((rows, width), full),
            pltpu.VMEM((rows, width), low),
            pltpu.VMEM((rows, width), low),
            pltpu.VMEM((rows, width), full),
            pltpu.VMEM((layers, 2, 2, rows, width), low),
            pltpu.VMEM((3, 2, rows, PIECE), low),
            pltpu.VMEM((2, rows, PIECE), low),
            pltpu.VMEM((length, length), full),
            pltpu.VMEM((pairs, LANES, length), low),
            pltpu.VMEM((length, 2 * length), low),
            pltpu.VMEM((length, 2 * length), low),
            pltpu.VMEM((width, length), low),
            pltpu.VMEM((7, 32, width), full),
            pltpu.VMEM((8, LANES), full),
            pltpu.VMEM((8, LANES), full),
            pltpu.VMEM((24, 2 * LANES), full),
            pltpu.VMEM((rows, 1), full),
            dma((pieces, 3)),
            dma((pieces, 3)),
            dma((pieces, 3)),
            dma((pieces, 3)),
            dma((pieces + 1,)),
            dma((6,)),
            dma((6,)),
            dma((8 * layers, CHUNKS)),
            dma((8 * layers, CHUNKS)),
            dma((pieces, 5)),
            dma((pieces, 5)),
            dma((2, 6)),
            dma((2, 6)),
            dma((1,)),
            dma((1,)),
        ],
        compiler_params=pltpu.CompilerParams(
            collective_id=0, has_side_effects=True, vmem_limit_bytes=67_043_328
        ),
        name="encoder_step",
    )(*operands)


def sibling_groups(extra):
    size = lax.axis_size("fsdp")
    return [list(range(first, first + extra)) for first in range(0, size, extra)]


def widen(shard, extra, axis):
    if extra == 1:
        return shard
    return lax.all_gather(
        shard, "fsdp", axis=axis, axis_index_groups=sibling_groups(extra), tiled=True
    )


def sum_siblings(value, extra):
    if extra == 1:
        return value
    return lax.psum(value, "fsdp", axis_index_groups=sibling_groups(extra))


def finish_kernel(
    place_count,
    mixed_hbm,
    tokens_grad_hbm,
    grad_hbm,
    sums_hbm,
    count_hbm,
    mixed_out,
    tokens_grad_out,
    loss_out,
    attn_in_out,
    attn_out_out,
    ff_in_out,
    ff_out_out,
    biases_out,
    gains_out,
    ff_bias_out,
    query_out,
    sums_ref,
    count_ref,
    sem,
):
    layers = attn_in_out.shape[0]
    width = sums_ref.shape[1]
    per_layer = grad_hbm.shape[0] // layers
    ups = (per_layer - 4) // 2
    moves = [
        (sums_hbm, sums_ref),
        (count_hbm, count_ref),
        (mixed_hbm, mixed_out),
        (tokens_grad_hbm, tokens_grad_out),
    ]
    for layer in range(layers):
        base = layer * per_layer
        for j in range(3):
            moves.append((grad_hbm.at[base + j], attn_in_out.at[layer, j]))
        moves.append((grad_hbm.at[base + 3], attn_out_out.at[layer]))
        for j in range(ups):
            lanes = pl.ds(j * PIECE, PIECE)
            moves.append((grad_hbm.at[base + 4 + j], ff_in_out.at[layer, :, lanes]))
            moves.append((grad_hbm.at[base + 4 + ups + j], ff_out_out.at[layer, :, lanes]))
    copies = [
        pltpu.make_async_copy(source, target, sem.at[number])
        for number, (source, target) in enumerate(moves)
    ]
    for copy in copies:
        copy.start()
    copies[0].wait()
    copies[1].wait()
    squares = jnp.sum(sums_ref[pl.ds(24, 1)], axis=1, keepdims=True)
    loss_out[...] = squares / (count_ref[:1, :1] * width)
    place = lax.axis_index("fsdp")
    share = width // place_count
    own = pltpu.roll(sums_ref[:16], (width - place * share) % width, 1)[:, :share]
    up_share = ff_bias_out.shape[1]
    first = place * up_share
    for layer in range(layers):
        for kind in range(biases_out.shape[0]):
            biases_out[kind, pl.ds(layer, 1)] = own[layer * 8 + kind : layer * 8 + kind + 1]
        gains_out[layer] = own[layer * 8 + 5 : layer * 8 + 7]
        query_out[pl.ds(layer, 1)] = own[layer * 8 + 7 : layer * 8 + 8]
        row = jnp.broadcast_to(sums_ref[pl.ds(16 + layer * 4 + first // width, 1)], (8, width))
        ff_bias_out[pl.ds(layer, 1)] = pltpu.roll(row, (width - first % width) % width, 1)[:1, :up_share]
    for copy in copies[2:]:
        copy.wait()


def on_device(
    tokens,
    segments,
    valid,
    teacher,
    attn_in,
    attn_out,
    ff_in,
    ff_out,
    biases,
    gains,
    ff_bias,
    query_bias,
):
    size = lax.axis_size("fsdp")
    extra = size // GROUP
    layers = attn_in.shape[0]
    rows_dev, width = tokens.shape[1], tokens.shape[2]
    length = segments.shape[1]

    matrices = (
        jnp.swapaxes(widen(attn_in, extra, 1), 1, 2),
        widen(attn_out, extra, 1),
        widen(ff_in, extra, 1),
        widen(ff_out, extra, 1),
    )
    vectors = (
        jnp.swapaxes(widen(biases, extra, 2), 0, 1),
        widen(gains, extra, 2),
        widen(ff_bias, extra, 1),
        widen(query_bias, extra, 1),
    )
    counted = None
    if extra > 1:
        own_seg = lax.dynamic_slice_in_dim(segments, lax.axis_index("tp") * rows_dev, rows_dev, 1)
        total = sum_siblings(jnp.sum((valid * (own_seg > 0)).astype(jnp.float32)), extra)
        counted = jnp.broadcast_to(total, (8, LANES))
    mixed, tokens_grad, grads, sums, count = run_step(
        extra,
        float(length * size),
        matrices,
        vectors,
        tokens[0],
        teacher[0],
        valid,
        segments,
        counted,
    )
    if extra > 1:
        grads = lax.psum_scatter(
            grads, "fsdp", scatter_dimension=1, axis_index_groups=sibling_groups(extra), tiled=True
        )
        sums = sum_siblings(sums, extra)
    vmem = pl.BlockSpec(memory_space=pltpu.VMEM)
    full = jnp.float32
    shapes = [
        jax.ShapeDtypeStruct(mixed.shape, jnp.bfloat16),
        jax.ShapeDtypeStruct(tokens_grad.shape, full),
        jax.ShapeDtypeStruct((1, 1), full),
    ]
    turned_in = (layers, 3, attn_in.shape[1], PIECE)
    turned_biases = (biases.shape[1], layers, biases.shape[2])
    for shape in (turned_in, attn_out.shape, ff_in.shape, ff_out.shape, turned_biases):
        shapes.append(jax.ShapeDtypeStruct(shape, full))
    for part in (gains, ff_bias, query_bias):
        shapes.append(jax.ShapeDtypeStruct(part.shape, full))
    mixed, tokens_grad, loss, in_grad, out_grad, up_grad, down_grad, bias_grad, *rest = pl.pallas_call(
        functools.partial(finish_kernel, size),
        out_shape=tuple(shapes),
        in_specs=[pl.BlockSpec(memory_space=pltpu.HBM)] * 5,
        out_specs=(vmem,) * len(shapes),
        scratch_shapes=[
            pltpu.VMEM(sums.shape, full),
            pltpu.VMEM(count.shape, full),
            pltpu.SemaphoreType.DMA((4 + grads.shape[0],)),
        ],
        compiler_params=pltpu.CompilerParams(vmem_limit_bytes=24 * 1024 * 1024),
        name="place_results",
    )(mixed, tokens_grad, grads, sums, count)
    return (
        mixed[None],
        tokens_grad[None],
        loss[0, 0],
        jnp.swapaxes(in_grad, 1, 2),
        out_grad,
        up_grad,
        down_grad,
        jnp.swapaxes(bias_grad, 0, 1),
        *rest,
    )


def solution(mesh):
    in_specs = (
        P("fsdp", "tp", None),
        P("fsdp", None),
        P("fsdp", "tp"),
        P("fsdp", "tp", None),
        P(None, "fsdp", None, "tp"),
        P(None, "fsdp", "tp"),
        P(None, "fsdp", "tp"),
        P(None, "fsdp", "tp"),
        P(None, None, "fsdp"),
        P(None, None, "fsdp"),
        P(None, "fsdp"),
        P(None, "fsdp"),
    )
    out_specs = (
        P("fsdp", "tp", None),
        P("fsdp", "tp", None),
        P(),
        P(None, "fsdp", None, "tp"),
        P(None, "fsdp", "tp"),
        P(None, "fsdp", "tp"),
        P(None, "fsdp", "tp"),
        P(None, None, "fsdp"),
        P(None, None, "fsdp"),
        P(None, "fsdp"),
        P(None, "fsdp"),
    )
    return jax.shard_map(
        on_device, mesh=mesh, in_specs=in_specs, out_specs=out_specs, check_vma=False
    )
```

```python
import functools

import jax
import jax.numpy as jnp
from jax import lax
from jax.experimental import pallas as pl
from jax.experimental.pallas import tpu as pltpu
from jax.sharding import PartitionSpec as P

HEAD_DIM = 64
MESH = pl.DeviceIdType.MESH
PIECE = 384
CHUNKS = 2
LANES = 128
GROUP = 16
WINDOW = 3
ROW_LEAD = 2
COL_LEAD = 1
PUMPS = (
    {
        "projected": (4,),
        "attend": ((1, 5), (2, 6)),
        "norm": ((0, 7), (1, 8)),
        "feed own": (9,),
        "feed": ((0, 10),),
        "fed": (11, 12),
        "sent": (13,),
        "kept": (14,),
        "end": ((0, 15), (1, 16)),
    },
    {
        "own projected": (17, 18),
        "projected": (19,),
        "attend": ((2, 20),),
        "norm": ((0, 21), (1, 22)),
        "feed": ((0, 23), (1, 24)),
    },
)
LAG = 2

epsilon = 1e-05
root_half = 0.7071067811865476
inv_root_tau = 0.3989422804014327
masked = -1e30


def product(left, right):
    return lax.dot_general(left, right, (((1,), (0,)), ((), ())), preferred_element_type=jnp.float32)


def product_nt(left, right):
    return lax.dot_general(left, right, (((1,), (1,)), ((), ())), preferred_element_type=jnp.float32)


def norm_stats(total):
    centred = total - jnp.mean(total, axis=-1, keepdims=True)
    inverse = lax.rsqrt(jnp.mean(centred * centred, axis=-1, keepdims=True) + epsilon)
    return centred * inverse, inverse


def norm_back(grad_out, normed, inverse, gain):
    scaled = grad_out * gain
    return inverse * (
        scaled
        - jnp.mean(scaled, axis=-1, keepdims=True)
        - normed * jnp.mean(scaled * normed, axis=-1, keepdims=True)
    )


def places(grad_rows, rows):
    first = grad_rows
    return first, first + 2 * rows, first + 4 * rows, first + 4 * rows + 64, first + 4 * rows + 72


def step_kernel(
    extra,
    token_total,
    attn_in_ref,
    attn_out_ref,
    ff_in_ref,
    ff_out_ref,
    tokens_ref,
    biases_ref,
    gains_ref,
    ff_bias_ref,
    query_ref,
    teacher_ref,
    valid_ref,
    seg_ref,
    count_in_ref,
    out_ref,
    mats,
    small_all,
    param,
    ff_shift,
    from_core,
    from_col,
    from_row,
    x_low,
    qkv,
    heads,
    log_sum,
    h_low,
    act,
    slope,
    normed,
    inverse,
    stream,
    out_part,
    in_part,
    own_part,
    d_low,
    d_qkv,
    d_heads,
    mask,
    pair_turn,
    probs_all,
    scores_all,
    pair_sums,
    turned,
    sums_in,
    sums_ref,
    count_mine,
    count_theirs,
    small_ref,
    weight_ref,
    z_send,
    z_recv,
    hop_send,
    hop_recv,
    local_sem,
    s_send,
    s_recv,
    x_send,
    x_recv,
    r_send,
    r_recv,
    a_send,
    a_recv,
    c_send,
    c_recv,
):
    pieces = mats.shape[0]
    spots = places(pieces * mats.shape[4], teacher_ref.shape[0])
    layers = x_low.shape[0]
    per_layer = pieces // layers
    half_rows = tokens_ref.shape[0]
    width = tokens_ref.shape[1]
    length = 2 * half_rows
    rows = half_rows // CHUNKS
    pairs = PIECE // LANES
    ups = act.shape[3] // PIECE

    spot = lax.axis_index("fsdp") // extra
    rest = lax.axis_index("fsdp") % extra
    t = lax.axis_index("tp")
    z, y, c = spot // 4, (spot // 2) % 2, spot % 2

    def peer(row, col, core):
        return {"fsdp": ((row * 2 + col) * 2 + core) * extra + rest, "tp": t}

    z_peers = [peer((z + step) % 4, y, c) for step in (1, 2, 3)]
    y_peer = peer(z, 1 - y, c)
    c_peer = peer(z, y, 1 - c)
    x_peer = {"fsdp": lax.axis_index("fsdp"), "tp": 1 - t}
    shards = []
    for layer in range(layers):
        shards += [attn_in_ref.at[layer, j] for j in range(3)]
        for source in (attn_out_ref, ff_in_ref, ff_out_ref):
            shards += [
                source.at[layer, :, pl.ds(j * PIECE, PIECE)] for j in range(source.shape[2] // PIECE)
            ]

    def own_copy(piece):
        return pltpu.make_async_copy(shards[piece], mats.at[piece, z, y, c], local_sem.at[piece])

    own_tokens = pltpu.make_async_copy(tokens_ref, x_low.at[0, t], local_sem.at[pieces])
    own_tokens.start()
    for piece in range(pieces):
        own_copy(piece).start()
    everyone = (*z_peers, y_peer, c_peer, x_peer)
    barrier = pltpu.get_barrier_semaphore()
    for other in everyone:
        pl.semaphore_signal(barrier, inc=1, device_id=other, device_id_type=MESH)
    seg_q = seg_ref[...].astype(jnp.float32)
    half_lanes = pl.ds(pl.multiple_of(t * half_rows, LANES), half_rows)
    counted_rows = valid_ref[...] * (seg_ref[:, half_lanes] > 0).astype(jnp.int32)
    weights = jnp.broadcast_to(counted_rows.astype(jnp.float32), (8, half_rows)).T
    weight_ref[...] = weights[:, :1]
    if count_in_ref is None:
        count_local = jnp.sum(weights[:, :1], axis=0, keepdims=True)
    else:
        count_local = count_in_ref[:1, :1]
    small_ref[...] = jnp.zeros_like(small_ref)
    share = biases_ref.shape[2]
    kinds = biases_ref.shape[0]
    for layer in range(layers):
        for kind in range(kinds):
            line = biases_ref[kind].astype(jnp.float32)[layer : layer + 1]
            small_ref[pl.ds(layer * kinds + kind, 1), pl.ds(0, share)] = line
        small_ref[pl.ds(10 + layer * 2, 2), pl.ds(0, share)] = gains_ref[layer].astype(jnp.float32)
    small_ref[pl.ds(14, layers), pl.ds(0, share)] = query_ref[...].astype(jnp.float32)
    small_ref[pl.ds(16, layers), pl.ds(0, ff_bias_ref.shape[1])] = ff_bias_ref[...].astype(jnp.float32)
    small_ref[pl.ds(18, 6)] = jnp.broadcast_to(count_local, (6, small_ref.shape[1]))
    pl.semaphore_wait(barrier, len(everyone))

    def remote(src, dst, send_sem, recv_sem, device):
        return pltpu.make_async_remote_copy(
            src_ref=src,
            dst_ref=dst,
            send_sem=send_sem,
            recv_sem=recv_sem,
            device_id=device,
            device_id_type=MESH,
        )

    def z_copy(piece, step):
        return remote(
            mats.at[piece, z, y, c],
            mats.at[piece, z, y, c],
            z_send.at[piece, step],
            z_recv.at[piece, step],
            z_peers[step],
        )

    relays = (z == 1) | (z == 2)

    def goes(step):
        if step == 1:
            return None
        return (z != 0) if step == 2 else (z != 3)

    def when(condition, action):
        if condition is None:
            action()
        else:
            pl.when(condition)(action)

    def relay(piece):
        source = jnp.where(z == 2, 0, 3)
        block = mats.at[piece, source, y, c]
        return remote(
            block,
            block,
            z_send.at[piece, 3],
            z_recv.at[piece, jnp.where(z == 2, 2, 0)],
            peer(3 - source, y, c),
        )

    def push(piece):
        for step in range(3):
            when(goes(step), lambda step=step: z_copy(piece, step).start())

    def relay_half(piece):
        z_copy(piece, 1).wait_recv()
        pl.when(relays)(lambda: relay(piece).start())

    def hop_copy(piece, kind):
        column = 1 - y if kind == 2 else y
        block = mats.at[piece, :, column, c]
        return remote(
            block,
            block,
            hop_send.at[piece, kind],
            hop_recv.at[piece, kind],
            y_peer if kind == 0 else c_peer,
        )

    def small_z(step):
        block = small_all.at[z, y, c]
        return remote(small_ref, block, s_send.at[step], s_recv.at[step], z_peers[step])

    def small_hop(kind):
        column = 1 - y if kind == 2 else y
        block = small_all.at[:, column, c]
        return remote(
            block, block, s_send.at[3 + kind], s_recv.at[3 + kind], y_peer if kind == 0 else c_peer
        )

    def first_half(piece):
        z_copy(piece, 0).wait_recv()
        z_copy(piece, 2).wait_recv()
        if isinstance(piece, int):
            if piece + WINDOW < pieces:
                push(piece + WINDOW)
        else:
            pl.when(piece + WINDOW < pieces)(lambda: push(piece + WINDOW))
        hop_copy(piece, 0).start()
        hop_copy(piece, 1).start()

    def second_half(piece):
        hop_copy(piece, 0).wait_recv()
        hop_copy(piece, 2).start()

    def advance(step):
        if isinstance(step, int):
            if step == 0:
                for piece in range(ROW_LEAD):
                    relay_half(piece)
                for piece in range(COL_LEAD):
                    first_half(piece)
            if step + ROW_LEAD < pieces:
                relay_half(step + ROW_LEAD)
            if step + COL_LEAD < pieces:
                first_half(step + COL_LEAD)
            if 0 < step <= pieces:
                second_half(step - 1)
        else:
            pl.when(step + ROW_LEAD < pieces)(lambda: relay_half(step + ROW_LEAD))
            pl.when(step + COL_LEAD < pieces)(lambda: first_half(step + COL_LEAD))
            pl.when(step <= pieces)(lambda: second_half(step - 1))

    def need(first, count=1):
        for piece in range(first, first + count):
            hop_copy(piece, 1).wait_recv()
            hop_copy(piece, 2).wait_recv()

    def chunk_rows(chunk):
        if isinstance(chunk, int):
            return pl.ds(chunk * rows, rows)
        return pl.ds(pl.multiple_of(chunk * rows, rows), rows)

    def put_wide(first, chunk, value):
        for column in range(width // PIECE):
            start = first + column * half_rows + chunk * rows
            if not isinstance(start, int):
                start = pl.multiple_of(start, 8)
            out_ref[pl.ds(start, rows)] = value[:, column * PIECE : (column + 1) * PIECE]

    def give_rows(number, chunk, block):
        place = block.at[t, chunk_rows(chunk)]
        return remote(place, place, x_send.at[number, chunk], x_recv.at[number, chunk], x_peer)

    def give_part(number, chunk):
        return remote(
            out_part.at[chunk_rows(chunk)],
            in_part.at[chunk_rows(chunk)],
            x_send.at[number, chunk],
            x_recv.at[number, chunk],
            x_peer,
        )

    def put_part(number, previous, chunk, value):
        if previous is not None:
            give_part(previous, chunk).wait_send()
        out_part[chunk_rows(chunk)] = value.astype(jnp.bfloat16)
        give_part(number, chunk).start()

    def place_part(index, number, previous, value):
        chunk = index % CHUNKS

        @pl.when(index < CHUNKS)
        def _():
            put_part(number, previous, chunk, value)

        @pl.when(index >= CHUNKS)
        def _():
            own_part[chunk_rows(chunk)] = value

    def core_copy(piece):
        return remote(
            mats.at[piece, :, :, 1 - c],
            from_core.at[piece],
            r_send.at[piece, 0],
            r_recv.at[piece, 0],
            c_peer,
        )

    def col_copy(piece):
        return remote(
            from_core.at[piece, :, 1 - y],
            from_col.at[piece],
            r_send.at[piece, 1],
            r_recv.at[piece, 1],
            y_peer,
        )

    def row_copy(piece, step):
        return remote(
            from_core.at[piece, (z + step + 1) % 4, y],
            from_row.at[piece, step],
            r_send.at[piece, 2 + step],
            r_recv.at[piece, 2 + step],
            z_peers[step],
        )

    def reduce_core(piece):
        core_copy(piece).wait_recv()

        def add_row(row, carry):
            from_core[piece, row] = (
                from_core[piece, row].astype(jnp.float32)
                + mats[piece, row, :, c].astype(jnp.float32)
            ).astype(jnp.bfloat16)
            return carry

        lax.fori_loop(0, 4, add_row, 0)
        col_copy(piece).start()

    def reduce_col(piece):
        col_copy(piece).wait_recv()

        def add_row(row, carry):
            from_core[piece, row, y] = (
                from_core[piece, row, y].astype(jnp.float32) + from_col[piece, row].astype(jnp.float32)
            ).astype(jnp.bfloat16)
            return carry

        lax.fori_loop(0, 4, add_row, 0)
        for step in range(3):
            row_copy(piece, step).start()

    def reduce_row(piece):
        for step in range(3):
            row_copy(piece, step).wait_recv()
        total = from_core[piece, z, y].astype(jnp.float32)
        for step in range(3):
            total = total + from_row[piece, step].astype(jnp.float32)
        out_ref[pl.ds(piece * total.shape[0], total.shape[0])] = total

    def reduce_step(index):
        if isinstance(index, int):
            if index < pieces:
                reduce_core(pieces - 1 - index)
            if 0 <= index - LAG < pieces:
                reduce_col(pieces - 1 - (index - LAG))
            if 0 <= index - 2 * LAG < pieces:
                reduce_row(pieces - 1 - (index - 2 * LAG))
        else:
            pl.when(index < pieces)(lambda: reduce_core(pieces - 1 - index))
            pl.when((index >= LAG) & (index < pieces + LAG))(
                lambda: reduce_col(pieces - 1 - (index - LAG))
            )
            pl.when(index >= 2 * LAG)(lambda: reduce_row(pieces - 1 - (index - 2 * LAG)))

    def put_grad(piece, value):
        mats[piece] = value.astype(jnp.bfloat16).reshape(mats.shape[1:])
        core_copy(piece).start()

    sum_blocks = ((8, 24), (0, 8))

    def sum_copy(phase, step):
        first, count = sum_blocks[phase]
        part = sums_ref.at[pl.ds(first, count)]
        slot = step if step < 3 else 3 + z
        device = (c_peer, y_peer, x_peer)[step] if step < 3 else z_peers[step - 3]
        return remote(
            part,
            sums_in.at[slot, pl.ds(first, count)],
            a_send.at[phase, step],
            a_recv.at[phase, step],
            device,
        )

    def sum_start(phase, step):
        if step < 3:
            sum_copy(phase, step).start()
            return
        first, count = sum_blocks[phase]
        for k in range(3, 6):
            sum_copy(phase, k).start()
        sums_in[3 + z, pl.ds(first, count)] = sums_ref[pl.ds(first, count)]

    def sum_finish(phase, step):
        first, count = sum_blocks[phase]
        block = pl.ds(first, count)
        if step < 3:
            sum_copy(phase, step).wait()
            sums_ref[block] = sums_ref[block] + sums_in[step, block]
            return
        for k in range(3, 6):
            sum_copy(phase, k).wait()
        sums_ref[block] = (sums_in[3, block] + sums_in[4, block]) + (
            sums_in[5, block] + sums_in[6, block]
        )

    def add_sum(row, value, column=None):
        if column is None:
            sums_ref[pl.ds(row, 1)] += value
        else:
            sums_ref[pl.ds(row, 1), column] += value

    def par(row):
        return param[pl.ds(row, 1)]

    def matrix(piece, count=1):
        parts = [mats[piece + j].reshape(width, PIECE) for j in range(count)]
        return parts[0] if count == 1 else jnp.concatenate(parts, axis=1)

    def turn(source):
        def turn_rows(index, carry):
            half, chunk = index // CHUNKS, index % CHUNKS
            columns = pl.ds(pl.multiple_of(index * rows, LANES), rows)
            turned[:, columns] = source[half, chunk_rows(chunk)].T
            return carry

        lax.fori_loop(0, 2 * CHUNKS, turn_rows, 0)

    own_columns = pl.ds(pl.multiple_of(t * PIECE, LANES), PIECE)

    for step in range(3):
        small_z(step).start()
    for piece in range(WINDOW):
        own_copy(piece).wait()
        push(piece)
    for chunk in range(CHUNKS):
        place = x_low.at[0, t, chunk_rows(chunk)]
        remote(
            tokens_ref.at[chunk_rows(chunk)],
            place,
            x_send.at[0, chunk],
            x_recv.at[0, chunk],
            x_peer,
        ).start()
    own_tokens.wait()
    stream[...] = x_low[0, t].astype(jnp.float32)
    small_all[z, y, c] = small_ref[...]
    for piece in range(WINDOW, pieces):
        own_copy(piece).wait()
    seg_k = jnp.broadcast_to(seg_q, (8, length)).T[:, :1]
    allowed = (seg_k > 0) & ((seg_k == seg_q) | (seg_q == 0))
    mask[...] = jnp.where(allowed, 0.0, masked)
    sums_ref[...] = jnp.zeros_like(sums_ref)
    lane = lax.broadcasted_iota(jnp.int32, (1, LANES), 1)
    low_lanes = lane < HEAD_DIM
    low_sub = lax.broadcasted_iota(jnp.int32, (LANES, 1), 0) < HEAD_DIM

    for step in range(3):
        small_z(step).wait_recv()
    small_hop(0).start()
    small_hop(1).start()
    advance(0)
    small_hop(0).wait_recv()
    small_hop(2).start()
    advance(1)
    small_hop(1).wait_recv()
    small_hop(2).wait_recv()
    param[...] = jnp.zeros_like(param)
    ff_shift[...] = jnp.zeros_like(ff_shift)
    counted = jnp.zeros((8, LANES), jnp.float32)
    for place in range(GROUP):
        block = small_all[place // 4, (place // 2) % 2, place % 2]
        offset = place * share
        tile = min(offset // LANES * LANES, width - 2 * LANES)
        shifted = block[:16] if offset == tile else pltpu.roll(block[:16], offset - tile, 1)
        param[pl.ds(0, 16), pl.ds(tile, 2 * LANES)] += shifted
        counted = counted + block[16:24, :LANES]
    hidden_share = ff_shift.shape[1] // (GROUP // 2)
    for place in range(GROUP // 2):
        block = small_all[2 * t + place // 4, (place // 2) % 2, place % 2][16:24]
        offset = place * hidden_share
        tile = offset // LANES * LANES
        if offset != tile:
            block = pltpu.roll(block, offset - tile, 1)
        ff_shift[:, pl.ds(tile, 2 * LANES)] += block
    count_mine[...] = counted
    remote(count_mine, count_theirs, c_send.at[0], c_recv.at[0], x_peer).start()

    def split_heads(pair):
        return jnp.concatenate(
            [jnp.where(low_lanes, pair, 0), jnp.where(low_lanes, 0, pair)], axis=0
        ).astype(pair.dtype)

    def merge_heads(turned_pair):
        size = turned_pair.shape[1] // 2
        return jnp.where(low_sub, turned_pair[:, :size], turned_pair[:, size:]).T

    def pair_lanes(pair):
        return pl.ds(pl.multiple_of(pair * LANES, LANES), LANES)

    def pair_rows(layer, which, pair):
        return qkv[layer, which, :, :, pair_lanes(pair)].reshape(length, LANES)

    def half_of(index):
        return jnp.where(index < CHUNKS, 1 - t, t)

    for layer in range(layers):
        base = layer * per_layer
        ex = 4 * layer
        early = layer == 0

        def project(half, first, count, layer=layer, base=base):
            acc = product(x_low[layer, half], matrix(base + first, count))
            for j in range(first, first + count):
                part = acc[:, (j - first) * PIECE : (j - first + 1) * PIECE]
                if j == 0:
                    part = part + param[pl.ds(14 + layer, 1), own_columns]
                if j == 2:
                    part = part + param[pl.ds(layer * 5, 1), own_columns]
                low = part.astype(jnp.bfloat16)
                if j == 0:
                    low = low * jnp.bfloat16(HEAD_DIM**-0.5)
                qkv[layer, j, half] = low

        def pump(slot, index=None, layer=layer):
            steps = PUMPS[layer].get(slot, ())
            if index is None:
                for step in steps:
                    advance(step)
                return
            for place, step in steps:
                pl.when(index == place)(lambda step=step: advance(step))

        if early:
            for j in range(3):
                if j > 0:
                    advance(j + 1)
                need(base + j)
                project(t, j, 1)
        else:
            need(base, 3)
            project(t, 0, 3)
        pump("own projected")
        for chunk in range(CHUNKS):
            give_rows(ex, chunk, x_low.at[layer]).wait_recv()
        project(1 - t, 0, 3)
        pump("projected")
        for pair in range(pairs):
            pair_turn[pair] = pair_rows(layer, 2, pair).T

        def attend(index, carry, layer=layer, base=base, ex=ex, early=early, pump=pump):
            half, chunk = half_of(index), index % CHUNKS
            where = chunk_rows(chunk)
            columns = pl.ds(pl.multiple_of(half * half_rows + chunk * rows, rows), rows)
            bias = mask[:, columns]
            bias = jnp.concatenate([bias, bias], axis=1)
            pump("attend", index)
            for pair in range(pairs):
                queries = split_heads(qkv[layer, 0, half, where, pair_lanes(pair)])
                scores = product_nt(pair_rows(layer, 1, pair), queries) + bias
                highest = jnp.max(scores, axis=0, keepdims=True)
                exponent = jnp.exp(scores - highest)
                total = jnp.sum(exponent, axis=0, keepdims=True)
                probs = (exponent * (1.0 / total)).astype(jnp.bfloat16)
                log_sum[layer, pair, half, chunk] = highest + jnp.log(total)
                mixed_pair = merge_heads(product(pair_turn[pair], probs))
                heads[layer, half, where, pair_lanes(pair)] = mixed_pair.astype(jnp.bfloat16)
            pl.when(index == 0)(lambda: need(base + 3))
            part = product_nt(heads[layer, half, where], matrix(base + 3))
            place_part(index, ex + 1, None if early else ex - 1, part)
            return carry

        lax.fori_loop(0, 2 * CHUNKS, attend, 0)

        def norm_rows(chunk, carry, layer=layer, ex=ex, pump=pump):
            where = chunk_rows(chunk)
            pump("norm", chunk)
            give_part(ex + 1, chunk).wait_recv()
            total = (
                stream[where] + own_part[where] + in_part[where].astype(jnp.float32) + par(layer * 5 + 1)
            )
            unit, scale = norm_stats(total)
            normed[layer, 0, where] = unit
            inverse[layer, 0, where] = scale
            value = unit * par(10 + layer * 2) + par(layer * 5 + 2)
            stream[where] = value
            h_low[layer, t, where] = value.astype(jnp.bfloat16)
            give_rows(ex + 2, chunk, h_low.at[layer]).start()
            return carry

        lax.fori_loop(0, CHUNKS, norm_rows, 0)

        need(base + 4, 4)

        def feed(half, where, layer=layer, base=base):
            source = h_low[layer, half, where]
            for j in range(0, ups, 2):
                lanes = pl.ds(j * PIECE, 2 * PIECE)
                u = product(source, matrix(base + 4 + j, 2)) + ff_shift[pl.ds(layer, 1), lanes]
                cdf = 0.5 * (1.0 + lax.erf(u * root_half))
                bell = jnp.exp(-0.5 * u * u) * inv_root_tau
                act[layer, half, where, lanes] = (u * cdf).astype(jnp.bfloat16)
                slope[layer, half, where, lanes] = (cdf + u * bell).astype(jnp.bfloat16)

        def feed_peer(chunk, carry, layer=layer, ex=ex, feed=feed, pump=pump):
            pump("feed", chunk)
            give_rows(ex + 2, chunk, h_low.at[layer]).wait_recv()
            feed(1 - t, chunk_rows(chunk))
            return carry

        def down(half, where, layer=layer, base=base):
            return product_nt(act[layer, half, where], matrix(base + 8, ups))

        def down_peer(chunk, carry, down=down, ex=ex):
            put_part(ex + 3, ex + 1, chunk, down(1 - t, chunk_rows(chunk)))
            return carry

        everything = pl.ds(0, half_rows)
        pump("feed own")
        feed(t, everything)
        lax.fori_loop(0, CHUNKS, feed_peer, 0)
        pump("fed")
        need(base + 8, 4)
        lax.fori_loop(0, CHUNKS, down_peer, 0)
        pump("sent")
        own_part[...] = down(t, everything)
        pump("kept")

        if layer == layers - 1:
            remote(count_mine, count_theirs, c_send.at[0], c_recv.at[0], x_peer).wait()
            count_all = (count_mine[...] + count_theirs[...])[2:3, :1]
            out_ref[pl.ds(spots[3], 8)] = jnp.broadcast_to(count_all, (8, PIECE))
            loss_scale = token_total / count_all
        def end_rows(chunk, carry, layer=layer, ex=ex, pump=pump):
            where = chunk_rows(chunk)
            give_part(ex + 3, chunk).wait_recv()
            total = (
                stream[where] + own_part[where] + in_part[where].astype(jnp.float32) + par(layer * 5 + 3)
            )
            unit, scale = norm_stats(total)
            normed[layer, 1, where] = unit
            inverse[layer, 1, where] = scale
            value = unit * par(11 + layer * 2) + par(layer * 5 + 4)
            if layer < layers - 1:
                stream[where] = value
                x_low[layer + 1, t, where] = value.astype(jnp.bfloat16)
                give_rows(ex + 4, chunk, x_low.at[layer + 1]).start()
            else:
                put_wide(spots[1], chunk, value)
                deviation = value - teacher_ref[where].astype(jnp.float32)
                weighted = weight_ref[where] * deviation
                add_sum(24, jnp.sum(weighted * deviation, axis=0, keepdims=True))
                stream[where] = loss_scale * weighted
            pump("end", chunk)
            return carry

        lax.fori_loop(0, CHUNKS, end_rows, 0)

    def finish_gather(piece, carry):
        for k in range(3):
            when(goes(k), lambda k=k: z_copy(piece, k).wait_send())
            hop_copy(piece, k).wait_send()
        pl.when(relays)(lambda: relay(piece).wait_send())
        return carry

    lax.fori_loop(0, pieces, finish_gather, 0)

    for layer in range(layers - 1, -1, -1):
        base = layer * per_layer
        ex = 4 * layers + 4 * (layers - 1 - layer)
        last = layer == layers - 1
        done = 0 if last else per_layer
        sums_base = layer * 8

        def top_rows(chunk, carry, layer=layer, ex=ex, last=last, sums_base=sums_base):
            where = chunk_rows(chunk)
            if not last:
                give_part(ex - 1, chunk).wait_recv()
                stream[where] += own_part[where] + in_part[where].astype(jnp.float32)
            grad_out, unit = stream[where], normed[layer, 1, where]
            below = norm_back(grad_out, unit, inverse[layer, 1, where], par(11 + layer * 2))
            d_low[layer, 0, t, where] = below.astype(jnp.bfloat16)
            give_rows(ex, chunk, d_low.at[layer, 0]).start()
            stream[where] = below
            add_sum(sums_base + 6, jnp.sum(grad_out * unit, axis=0, keepdims=True))
            add_sum(sums_base + 4, jnp.sum(grad_out, axis=0, keepdims=True))
            add_sum(sums_base + 3, jnp.sum(below, axis=0, keepdims=True))
            return carry

        lax.fori_loop(0, CHUNKS, top_rows, 0)
        if not last:
            reduce_step(9)

        def feed_back(half, where, layer=layer, base=base):
            source = d_low[layer, 0, half, where]
            per_row = width // PIECE
            for j in range(0, ups, 2):
                lanes = pl.ds(j * PIECE, 2 * PIECE)
                du = product(source, matrix(base + 8 + j, 2)) * slope[
                    layer, half, where, lanes
                ].astype(jnp.float32)
                total = jnp.sum(du, axis=0, keepdims=True)
                for k in range(j, j + 2):
                    add_sum(
                        16 + layer * 4 + 2 * t + k // per_row,
                        total[:, (k - j) * PIECE : (k - j + 1) * PIECE],
                        pl.ds(k % per_row * PIECE, PIECE),
                    )
                slope[layer, half, where, lanes] = du.astype(jnp.bfloat16)

        def up_back(half, where, layer=layer, base=base):
            return product_nt(slope[layer, half, where], matrix(base + 4, ups))

        def feed_back_peer(chunk, carry, layer=layer, ex=ex, last=last, feed_back=feed_back, up_back=up_back):
            if not last:
                reduce_step(10 + chunk)
            where = chunk_rows(chunk)
            give_rows(ex, chunk, d_low.at[layer, 0]).wait_recv()
            feed_back(1 - t, where)
            put_part(ex + 1, 4 * layers - 1 if last else ex - 1, chunk, up_back(1 - t, where))
            return carry

        feed_back(t, everything)
        own_part[...] = up_back(t, everything)
        lax.fori_loop(0, CHUNKS, feed_back_peer, 0)

        def mid_rows(chunk, layer=layer, ex=ex, sums_base=sums_base):
            where = chunk_rows(chunk)
            give_part(ex + 1, chunk).wait_recv()
            grad_out = stream[where] + own_part[where] + in_part[where].astype(jnp.float32)
            unit = normed[layer, 0, where]
            below = norm_back(grad_out, unit, inverse[layer, 0, where], par(10 + layer * 2))
            d_low[layer, 1, t, where] = below.astype(jnp.bfloat16)
            give_rows(ex + 2, chunk, d_low.at[layer, 1]).start()
            stream[where] = below
            add_sum(sums_base + 5, jnp.sum(grad_out * unit, axis=0, keepdims=True))
            add_sum(sums_base + 2, jnp.sum(grad_out, axis=0, keepdims=True))
            add_sum(sums_base + 1, jnp.sum(below, axis=0, keepdims=True))

        def pair_grad(piece, left, right, j):
            lanes = pl.ds(j * PIECE, 2 * PIECE)
            if not isinstance(j, int):
                lanes = pl.ds(pl.multiple_of(j * PIECE, LANES), 2 * PIECE)
            both = product(left, right[:, :, lanes].reshape(length, 2 * PIECE))
            put_grad(piece + 1, both[:, PIECE:])
            put_grad(piece, both[:, :PIECE])

        def up_grad(j, layer=layer, base=base, pair_grad=pair_grad):
            pair_grad(base + 4 + j, turned[...], slope.at[layer], j)


        def out_grad(layer=layer, base=base):
            turn(d_low.at[layer, 1])
            put_grad(base + 3, product(turned[...], heads[layer].reshape(length, PIECE)))

        def in_grads(layer=layer, base=base):
            turn(x_low.at[layer])
            for j in range(2, -1, -1):
                put_grad(base + j, product(turned[...], d_qkv[j].reshape(length, PIECE)))

        def sum_move(step, last=last):
            if not last:
                if step > 0:
                    sum_finish(0, step - 1)
                sum_start(0, step)

        def attend_back(half, first_step, opening, layer=layer):
            def pair_back(pair, carry):
                lanes = pair_lanes(pair)
                keys_in, values_in = pair_rows(layer, 1, pair), pair_rows(layer, 2, pair)

                def chunk_back(chunk, carry):
                    where = chunk_rows(chunk)
                    columns = pl.ds(pl.multiple_of(half * half_rows + chunk * rows, rows), rows)
                    bias = mask[:, columns]
                    bias = jnp.concatenate([bias, bias], axis=1)
                    queries = split_heads(qkv[layer, 0, half, where, lanes])
                    grads = split_heads(d_heads[half, where, lanes])
                    scores = product_nt(keys_in, queries) + bias
                    probs = jnp.exp(scores - log_sum[layer, pair, half, chunk])
                    d_probs = product_nt(values_in, grads)
                    delta = jnp.sum(probs * d_probs, axis=0, keepdims=True)
                    d_scores = (probs * (d_probs - delta)).astype(jnp.bfloat16)
                    double = pl.ds(pl.multiple_of(chunk * 2 * rows, LANES), 2 * rows)
                    probs_all[:, double] = probs.astype(jnp.bfloat16)
                    scores_all[:, double] = d_scores
                    d_query = merge_heads(product(pair_turn[pair], d_scores)) * HEAD_DIM**-0.5
                    d_qkv[0, half, where, lanes] = d_query.astype(jnp.bfloat16)
                    return carry

                lax.fori_loop(0, CHUNKS, chunk_back, 0)
                query_list, grad_list = [], []
                for chunk in range(CHUNKS):
                    where = chunk_rows(chunk)
                    query_list.append(split_heads(qkv[layer, 0, half, where, lanes]))
                    grad_list.append(split_heads(d_heads[half, where, lanes]))
                d_keys = product(scores_all[...], jnp.concatenate(query_list, axis=0))
                d_values = product(probs_all[...], jnp.concatenate(grad_list, axis=0))
                if opening:
                    pair_sums[pair, 0] = d_keys
                    pair_sums[pair, 1] = d_values
                else:
                    for which, total in ((1, d_keys), (2, d_values)):
                        total = (total + pair_sums[pair, which - 1]).astype(jnp.bfloat16)
                        d_qkv[which, :, :, lanes] = total.reshape(2, half_rows, LANES)
                pl.when(pair != 1)(lambda: reduce_step(first_step + pair // 2))
                return carry

            lax.fori_loop(0, pairs, pair_back, 0)

        sum_move(0)
        turn(d_low.at[layer, 0])
        pair_grad(base + 8 + ups - 2, turned[...], act.at[layer], ups - 2)
        mid_rows(0)
        sum_move(1)
        for j in range(ups - 4, -1, -2):
            pair_grad(base + 8 + j, turned[...], act.at[layer], j)
        reduce_step(done)
        mid_rows(1)
        sum_move(2)
        reduce_step(done + 1)
        turn(h_low.at[layer])
        for j in range(ups - 2, -1, -2):
            up_grad(j)
        reduce_step(done + 2)
        sum_move(3)
        d_heads[t] = product(d_low[layer, 1, t], matrix(base + 3)).astype(jnp.bfloat16)
        for pair in range(pairs):
            pair_turn[pair] = pair_rows(layer, 1, pair).T
        attend_back(t, done + 3, True)
        for chunk in range(CHUNKS):
            give_rows(ex + 2, chunk, d_low.at[layer, 1]).wait_recv()
        d_heads[1 - t] = product(d_low[layer, 1, 1 - t], matrix(base + 3)).astype(jnp.bfloat16)
        attend_back(1 - t, done + 5, False)
        if not last:
            out_grad()

        def query_parts(index, carry, layer=layer, base=base, ex=ex):
            half, chunk = half_of(index), index % CHUNKS
            where = chunk_rows(chunk)
            parts = jnp.concatenate([d_qkv[j, half, where] for j in range(3)], axis=1)
            part = product_nt(parts, matrix(base, 3))
            place_part(index, ex + 3, ex + 1, part)
            return carry

        add_sum(
            sums_base + 7,
            jnp.sum(d_qkv[0].reshape(length, PIECE).astype(jnp.float32), axis=0, keepdims=True),
            own_columns,
        )
        add_sum(
            sums_base,
            jnp.sum(d_qkv[2].reshape(length, PIECE).astype(jnp.float32), axis=0, keepdims=True),
            own_columns,
        )
        if not last:
            sum_start(1, 0)
        lax.fori_loop(0, 2 * CHUNKS, query_parts, 0)
        reduce_step(done + 7)
        if last:
            out_grad()
        in_grads()
        reduce_step(done + 8)
    sum_finish(1, 0)
    sum_start(1, 1)
    ex = 8 * layers - 1
    for chunk in range(CHUNKS):
        where = chunk_rows(chunk)
        give_part(ex, chunk).wait_recv()
        put_wide(spots[0], chunk, stream[where] + own_part[where] + in_part[where].astype(jnp.float32))
    sum_finish(0, 3)
    sum_finish(1, 1)
    sum_start(1, 2)
    reduce_step(pieces - 3)
    sum_finish(1, 2)
    sum_start(1, 3)

    def drain(step, carry):
        reduce_step(step)
        return carry

    lax.fori_loop(pieces - 2, pieces + 2 * LAG, drain, 0)
    sum_finish(1, 3)
    for column in range(width // PIECE):
        out_ref[pl.ds(spots[2] + column * 32, 32)] = sums_ref[:, column * PIECE : (column + 1) * PIECE]

    for step in range(3):
        small_z(step).wait_send()
        small_hop(step).wait_send()
    for chunk in range(CHUNKS):
        give_part(8 * layers - 1, chunk).wait_send()
        for layer in range(layers):
            give_rows(4 * layer, chunk, x_low.at[layer]).wait_send()
            give_rows(4 * layer + 2, chunk, h_low.at[layer]).wait_send()
            number = 4 * layers + 4 * (layers - 1 - layer)
            give_rows(number, chunk, d_low.at[layer, 0]).wait_send()
            give_rows(number + 2, chunk, d_low.at[layer, 1]).wait_send()

    def finish_grads(piece, carry):
        core_copy(piece).wait_send()
        col_copy(piece).wait_send()
        for step in range(3):
            row_copy(piece, step).wait_send()
        return carry

    lax.fori_loop(0, pieces, finish_grads, 0)


def run_step(extra, token_total, matrices, vectors, tokens, teacher, valid, seg_ids, counted):
    attn_in, attn_out, ff_in, ff_out = matrices
    rows, width = tokens.shape
    length = 2 * rows
    layers, share, hidden_width = ff_in.shape
    ups = hidden_width // PIECE
    pieces = layers * (4 + 2 * ups)
    low, full = jnp.bfloat16, jnp.float32
    chunk = rows // CHUNKS
    pairs = PIECE // LANES
    blocks = (4, 2, 2, share, PIECE)
    dma = pltpu.SemaphoreType.DMA
    vmem = pl.BlockSpec(memory_space=pltpu.VMEM)
    operands = [*matrices, tokens, *vectors, teacher, valid, seg_ids]
    kernel = functools.partial(step_kernel, extra, token_total)
    if counted is None:
        inputs = len(operands)

        def body(*refs):
            kernel(*refs[:inputs], None, *refs[inputs:])

    else:
        operands.append(counted)
        body = kernel
    return pl.pallas_call(
        body,
        out_shape=jax.ShapeDtypeStruct((places(pieces * share, rows)[4], PIECE), full),
        in_specs=[pl.BlockSpec(memory_space=pl.ANY)] * 5 + [vmem] * (len(operands) - 5),
        out_specs=vmem,
        scratch_shapes=[
            pltpu.VMEM((pieces, *blocks), low),
            pltpu.VMEM((4, 2, 2, 24, 2 * LANES), full),
            pltpu.VMEM((16, width), full),
            pltpu.VMEM((8, hidden_width), full),
            pltpu.VMEM((pieces, 4, 2, share, PIECE), low),
            pltpu.VMEM((pieces, 4, share, PIECE), low),
            pltpu.VMEM((pieces, 3, share, PIECE), low),
            pltpu.VMEM((layers, 2, rows, width), low),
            pltpu.VMEM((layers, 3, 2, rows, PIECE), low),
            pltpu.VMEM((layers, 2, rows, PIECE), low),
            pltpu.VMEM((layers, pairs, 2, CHUNKS, 1, 2 * chunk), full),
            pltpu.VMEM((layers, 2, rows, width), low),
            pltpu.VMEM((layers, 2, rows, hidden_width), low),
            pltpu.VMEM((layers, 2, rows, hidden_width), low),
            pltpu.VMEM((layers, 2, rows, width), full),
            pltpu.VMEM((layers, 2, rows, 1), full),
            pltpu.VMEM((rows, width), full),
            pltpu.VMEM((rows, width), low),
            pltpu.VMEM((rows, width), low),
            pltpu.VMEM((rows, width), full),
            pltpu.VMEM((layers, 2, 2, rows, width), low),
            pltpu.VMEM((3, 2, rows, PIECE), low),
            pltpu.VMEM((2, rows, PIECE), low),
            pltpu.VMEM((length, length), full),
            pltpu.VMEM((pairs, LANES, length), low),
            pltpu.VMEM((length, length), low),
            pltpu.VMEM((length, length), low),
            pltpu.VMEM((pairs, 2, length, LANES), full),
            pltpu.VMEM((width, length), low),
            pltpu.VMEM((7, 32, width), full),
            pltpu.VMEM((32, width), full),
            pltpu.VMEM((8, LANES), full),
            pltpu.VMEM((8, LANES), full),
            pltpu.VMEM((24, 2 * LANES), full),
            pltpu.VMEM((rows, 1), full),
            dma((pieces, 4)),
            dma((pieces, 3)),
            dma((pieces, 3)),
            dma((pieces, 3)),
            dma((pieces + 1,)),
            dma((6,)),
            dma((6,)),
            dma((8 * layers, CHUNKS)),
            dma((8 * layers, CHUNKS)),
            dma((pieces, 5)),
            dma((pieces, 5)),
            dma((2, 6)),
            dma((2, 6)),
            dma((1,)),
            dma((1,)),
        ],
        compiler_params=pltpu.CompilerParams(
            collective_id=0, has_side_effects=True, vmem_limit_bytes=67_043_328
        ),
        name="encoder_step",
    )(*operands)


def sibling_groups(extra):
    size = lax.axis_size("fsdp")
    return [list(range(first, first + extra)) for first in range(0, size, extra)]


def widen(shard, extra, axis):
    if extra == 1:
        return shard
    return lax.all_gather(
        shard, "fsdp", axis=axis, axis_index_groups=sibling_groups(extra), tiled=True
    )


def sum_siblings(value, extra):
    if extra == 1:
        return value
    return lax.psum(value, "fsdp", axis_index_groups=sibling_groups(extra))


def finish_kernel(
    place_count,
    all_ref,
    mixed_out,
    tokens_grad_out,
    loss_out,
    attn_in_out,
    attn_out_out,
    ff_in_out,
    ff_out_out,
    biases_out,
    gains_out,
    ff_bias_out,
    query_out,
    sums_ref,
):
    layers, share = attn_out_out.shape[0], attn_out_out.shape[1]
    rows, width = mixed_out.shape
    ups = ff_in_out.shape[2] // PIECE
    per_layer = 4 + 2 * ups
    spots = places(layers * per_layer * share, rows)

    def grad(piece):
        return all_ref[pl.ds(piece * share, share)]

    for column in range(width // PIECE):
        lanes = pl.ds(column * PIECE, PIECE)
        tokens_grad_out[:, lanes] = all_ref[pl.ds(spots[0] + column * rows, rows)]
        mixed_out[:, lanes] = all_ref[pl.ds(spots[1] + column * rows, rows)].astype(mixed_out.dtype)
        sums_ref[:, lanes] = all_ref[pl.ds(spots[2] + column * 32, 32)]
    for layer in range(layers):
        base = layer * per_layer
        for j in range(3):
            attn_in_out[layer, j] = grad(base + j)
        attn_out_out[layer] = grad(base + 3)
        for j in range(ups):
            lanes = pl.ds(j * PIECE, PIECE)
            ff_in_out[layer, :, lanes] = grad(base + 4 + j)
            ff_out_out[layer, :, lanes] = grad(base + 4 + ups + j)
    squares = jnp.sum(sums_ref[pl.ds(24, 1)], axis=1, keepdims=True)
    loss_out[...] = squares / (all_ref[pl.ds(spots[3], 8)][:1, :1] * width)
    place = lax.axis_index("fsdp")
    share = width // place_count
    own = pltpu.roll(sums_ref[:16], (width - place * share) % width, 1)[:, :share]
    up_share = ff_bias_out.shape[1]
    first = place * up_share
    for layer in range(layers):
        for kind in range(biases_out.shape[0]):
            biases_out[kind, pl.ds(layer, 1)] = own[layer * 8 + kind : layer * 8 + kind + 1]
        gains_out[layer] = own[layer * 8 + 5 : layer * 8 + 7]
        query_out[pl.ds(layer, 1)] = own[layer * 8 + 7 : layer * 8 + 8]
        row = jnp.broadcast_to(sums_ref[pl.ds(16 + layer * 4 + first // width, 1)], (8, width))
        ff_bias_out[pl.ds(layer, 1)] = pltpu.roll(row, (width - first % width) % width, 1)[:1, :up_share]


def on_device(
    tokens,
    segments,
    valid,
    teacher,
    attn_in,
    attn_out,
    ff_in,
    ff_out,
    biases,
    gains,
    ff_bias,
    query_bias,
):
    size = lax.axis_size("fsdp")
    extra = size // GROUP
    layers = attn_in.shape[0]
    rows_dev, width = tokens.shape[1], tokens.shape[2]
    length = segments.shape[1]

    matrices = (
        jnp.swapaxes(widen(attn_in, extra, 1), 1, 2),
        widen(attn_out, extra, 1),
        widen(ff_in, extra, 1),
        widen(ff_out, extra, 1),
    )
    vectors = (
        jnp.swapaxes(widen(biases, extra, 2), 0, 1),
        widen(gains, extra, 2),
        widen(ff_bias, extra, 1),
        widen(query_bias, extra, 1),
    )
    counted = None
    if extra > 1:
        own_seg = lax.dynamic_slice_in_dim(segments, lax.axis_index("tp") * rows_dev, rows_dev, 1)
        total = sum_siblings(jnp.sum((valid * (own_seg > 0)).astype(jnp.float32)), extra)
        counted = jnp.broadcast_to(total, (8, LANES))
    results = run_step(
        extra,
        float(length * size),
        matrices,
        vectors,
        tokens[0],
        teacher[0],
        valid,
        segments,
        counted,
    )
    if extra > 1:
        share = width // GROUP
        spots = places(results.shape[0] - places(0, rows_dev)[4], rows_dev)
        grads = lax.psum_scatter(
            results[: spots[0]].reshape(-1, share, PIECE),
            "fsdp",
            scatter_dimension=1,
            axis_index_groups=sibling_groups(extra),
            tiled=True,
        )
        sums = sum_siblings(results[spots[2] : spots[3]], extra)
        results = jnp.concatenate(
            [grads.reshape(-1, PIECE), results[spots[0] : spots[2]], sums, results[spots[3] :]], axis=0
        )
    vmem = pl.BlockSpec(memory_space=pltpu.VMEM)
    full = jnp.float32
    shapes = [
        jax.ShapeDtypeStruct((rows_dev, width), jnp.bfloat16),
        jax.ShapeDtypeStruct((rows_dev, width), full),
        jax.ShapeDtypeStruct((1, 1), full),
    ]
    turned_in = (layers, 3, attn_in.shape[1], PIECE)
    turned_biases = (biases.shape[1], layers, biases.shape[2])
    for shape in (turned_in, attn_out.shape, ff_in.shape, ff_out.shape, turned_biases):
        shapes.append(jax.ShapeDtypeStruct(shape, full))
    for part in (gains, ff_bias, query_bias):
        shapes.append(jax.ShapeDtypeStruct(part.shape, full))
    mixed, tokens_grad, loss, in_grad, out_grad, up_grad, down_grad, bias_grad, *rest = pl.pallas_call(
        functools.partial(finish_kernel, size),
        out_shape=tuple(shapes),
        in_specs=[vmem],
        out_specs=(vmem,) * len(shapes),
        scratch_shapes=[pltpu.VMEM((32, width), full)],
        compiler_params=pltpu.CompilerParams(vmem_limit_bytes=24 * 1024 * 1024),
        name="place_results",
    )(results)
    return (
        mixed[None],
        tokens_grad[None],
        loss[0, 0],
        jnp.swapaxes(in_grad, 1, 2),
        out_grad,
        up_grad,
        down_grad,
        jnp.swapaxes(bias_grad, 0, 1),
        *rest,
    )


def solution(mesh):
    in_specs = (
        P("fsdp", "tp", None),
        P("fsdp", None),
        P("fsdp", "tp"),
        P("fsdp", "tp", None),
        P(None, "fsdp", None, "tp"),
        P(None, "fsdp", "tp"),
        P(None, "fsdp", "tp"),
        P(None, "fsdp", "tp"),
        P(None, None, "fsdp"),
        P(None, None, "fsdp"),
        P(None, "fsdp"),
        P(None, "fsdp"),
    )
    out_specs = (
        P("fsdp", "tp", None),
        P("fsdp", "tp", None),
        P(),
        P(None, "fsdp", None, "tp"),
        P(None, "fsdp", "tp"),
        P(None, "fsdp", "tp"),
        P(None, "fsdp", "tp"),
        P(None, None, "fsdp"),
        P(None, None, "fsdp"),
        P(None, "fsdp"),
        P(None, "fsdp"),
    )
    return jax.shard_map(
        on_device, mesh=mesh, in_specs=in_specs, out_specs=out_specs, check_vma=False
    )
```

```python
import functools

import jax
import jax.numpy as jnp
from jax import lax
from jax.experimental import pallas as pl
from jax.experimental.pallas import tpu as pltpu
from jax.sharding import PartitionSpec as P

HEAD_DIM = 64
MESH = pl.DeviceIdType.MESH
PIECE = 384
CHUNKS = 2
LANES = 128
GROUP = 16
WINDOW = 2
ROW_LEAD = 2
COL_LEAD = 1
PUMPS = (
    {
        "projected": (4,),
        "attend": ((1, 5), (2, 6)),
        "norm": ((0, 7), (1, 8)),
        "feed own": (9,),
        "feed": ((0, 10),),
        "fed": (11, 12),
        "sent": (13,),
        "kept": (14,),
        "end": ((0, 15), (1, 16)),
    },
    {
        "own projected": (17, 18),
        "projected": (19,),
        "attend": ((2, 20),),
        "norm": ((0, 21), (1, 22)),
        "feed": ((0, 23),),
        "fed": (24,),
    },
)
LAG = 2

epsilon = 1e-05
root_half = 0.7071067811865476
inv_root_tau = 0.3989422804014327
masked = -1e30


def product(left, right):
    return lax.dot_general(left, right, (((1,), (0,)), ((), ())), preferred_element_type=jnp.float32)


def product_nt(left, right):
    return lax.dot_general(left, right, (((1,), (1,)), ((), ())), preferred_element_type=jnp.float32)


def norm_stats(total):
    centred = total - jnp.mean(total, axis=-1, keepdims=True)
    inverse = lax.rsqrt(jnp.mean(centred * centred, axis=-1, keepdims=True) + epsilon)
    return centred * inverse, inverse


def norm_back(grad_out, normed, inverse, gain):
    scaled = grad_out * gain
    return inverse * (
        scaled
        - jnp.mean(scaled, axis=-1, keepdims=True)
        - normed * jnp.mean(scaled * normed, axis=-1, keepdims=True)
    )


def places(grad_rows, rows):
    first = grad_rows
    return first, first + 2 * rows, first + 4 * rows, first + 4 * rows + 64, first + 4 * rows + 72


def step_kernel(
    extra,
    token_total,
    attn_in_ref,
    attn_out_ref,
    ff_in_ref,
    ff_out_ref,
    tokens_ref,
    biases_ref,
    gains_ref,
    ff_bias_ref,
    query_ref,
    teacher_ref,
    valid_ref,
    seg_ref,
    count_in_ref,
    result_ref,
    out_ref,
    mats,
    small_all,
    param,
    ff_shift,
    from_core,
    from_col,
    from_row,
    x_low,
    qkv,
    heads,
    log_sum,
    h_low,
    act,
    slope,
    normed,
    inverse,
    stream,
    out_part,
    in_part,
    own_part,
    d_low,
    d_qkv,
    d_heads,
    mask,
    pair_turn,
    probs_all,
    scores_all,
    pair_sums,
    turned,
    sums_in,
    sums_ref,
    count_mine,
    count_theirs,
    small_ref,
    weight_ref,
    z_send,
    z_recv,
    hop_send,
    hop_recv,
    local_sem,
    s_send,
    s_recv,
    x_send,
    x_recv,
    r_send,
    r_recv,
    a_send,
    a_recv,
    c_send,
    c_recv,
    out_sem,
):
    pieces = mats.shape[0]
    spots = places(pieces * mats.shape[4], teacher_ref.shape[0])
    layers = x_low.shape[0]
    per_layer = pieces // layers
    half_rows = tokens_ref.shape[0]
    width = tokens_ref.shape[1]
    length = 2 * half_rows
    rows = half_rows // CHUNKS
    pairs = PIECE // LANES
    ups = act.shape[3] // PIECE

    spot = lax.axis_index("fsdp") // extra
    rest = lax.axis_index("fsdp") % extra
    t = lax.axis_index("tp")
    z, y, c = spot // 4, (spot // 2) % 2, spot % 2

    def peer(row, col, core):
        return {"fsdp": ((row * 2 + col) * 2 + core) * extra + rest, "tp": t}

    z_peers = [peer((z + step) % 4, y, c) for step in (1, 2, 3)]
    y_peer = peer(z, 1 - y, c)
    c_peer = peer(z, y, 1 - c)
    x_peer = {"fsdp": lax.axis_index("fsdp"), "tp": 1 - t}
    shards = []
    for layer in range(layers):
        shards += [attn_in_ref.at[layer, j] for j in range(3)]
        for source in (attn_out_ref, ff_in_ref, ff_out_ref):
            shards += [
                source.at[layer, :, pl.ds(j * PIECE, PIECE)] for j in range(source.shape[2] // PIECE)
            ]

    def own_copy(piece):
        return pltpu.make_async_copy(shards[piece], mats.at[piece, z, y, c], local_sem.at[piece])

    own_tokens = pltpu.make_async_copy(tokens_ref, x_low.at[0, t], local_sem.at[pieces])
    own_tokens.start()
    for piece in range(pieces):
        own_copy(piece).start()
    everyone = (*z_peers, y_peer, c_peer, x_peer)
    barrier = pltpu.get_barrier_semaphore()
    for other in everyone:
        pl.semaphore_signal(barrier, inc=1, device_id=other, device_id_type=MESH)
    seg_q = seg_ref[...].astype(jnp.float32)
    half_lanes = pl.ds(pl.multiple_of(t * half_rows, LANES), half_rows)
    counted_rows = valid_ref[...] * (seg_ref[:, half_lanes] > 0).astype(jnp.int32)
    weights = jnp.broadcast_to(counted_rows.astype(jnp.float32), (8, half_rows)).T
    weight_ref[...] = weights[:, :1]
    if count_in_ref is None:
        count_local = jnp.sum(weights[:, :1], axis=0, keepdims=True)
    else:
        count_local = count_in_ref[:1, :1]
    small_ref[...] = jnp.zeros_like(small_ref)
    share = biases_ref.shape[2]
    kinds = biases_ref.shape[0]
    for layer in range(layers):
        for kind in range(kinds):
            line = biases_ref[kind].astype(jnp.float32)[layer : layer + 1]
            small_ref[pl.ds(layer * kinds + kind, 1), pl.ds(0, share)] = line
        small_ref[pl.ds(10 + layer * 2, 2), pl.ds(0, share)] = gains_ref[layer].astype(jnp.float32)
    small_ref[pl.ds(14, layers), pl.ds(0, share)] = query_ref[...].astype(jnp.float32)
    small_ref[pl.ds(16, layers), pl.ds(0, ff_bias_ref.shape[1])] = ff_bias_ref[...].astype(jnp.float32)
    small_ref[pl.ds(18, 6)] = jnp.broadcast_to(count_local, (6, small_ref.shape[1]))
    pl.semaphore_wait(barrier, len(everyone))

    def remote(src, dst, send_sem, recv_sem, device):
        return pltpu.make_async_remote_copy(
            src_ref=src,
            dst_ref=dst,
            send_sem=send_sem,
            recv_sem=recv_sem,
            device_id=device,
            device_id_type=MESH,
        )

    def z_copy(piece, step):
        return remote(
            mats.at[piece, z, y, c],
            mats.at[piece, z, y, c],
            z_send.at[piece, step],
            z_recv.at[piece, step],
            z_peers[step],
        )

    relays = (z == 1) | (z == 2)

    def goes(step):
        if step == 1:
            return None
        return (z != 0) if step == 2 else (z != 3)

    def when(condition, action):
        if condition is None:
            action()
        else:
            pl.when(condition)(action)

    def relay(piece):
        source = jnp.where(z == 2, 0, 3)
        block = mats.at[piece, source, y, c]
        return remote(
            block,
            block,
            z_send.at[piece, 3],
            z_recv.at[piece, jnp.where(z == 2, 2, 0)],
            peer(3 - source, y, c),
        )

    def push(piece):
        for step in range(3):
            when(goes(step), lambda step=step: z_copy(piece, step).start())

    def relay_half(piece):
        z_copy(piece, 1).wait_recv()
        pl.when(relays)(lambda: relay(piece).start())
        if isinstance(piece, int):
            if piece + WINDOW < pieces:
                push(piece + WINDOW)
        else:
            pl.when(piece + WINDOW < pieces)(lambda: push(piece + WINDOW))

    def hop_copy(piece, kind):
        column = 1 - y if kind == 2 else y
        block = mats.at[piece, :, column, c]
        return remote(
            block,
            block,
            hop_send.at[piece, kind],
            hop_recv.at[piece, kind],
            y_peer if kind == 0 else c_peer,
        )

    def small_z(step):
        block = small_all.at[z, y, c]
        return remote(small_ref, block, s_send.at[step], s_recv.at[step], z_peers[step])

    def small_hop(kind):
        column = 1 - y if kind == 2 else y
        block = small_all.at[:, column, c]
        return remote(
            block, block, s_send.at[3 + kind], s_recv.at[3 + kind], y_peer if kind == 0 else c_peer
        )

    def first_half(piece):
        z_copy(piece, 0).wait_recv()
        z_copy(piece, 2).wait_recv()
        hop_copy(piece, 0).start()
        hop_copy(piece, 1).start()

    def second_half(piece):
        hop_copy(piece, 0).wait_recv()
        hop_copy(piece, 2).start()

    def advance(step):
        if isinstance(step, int):
            if step == 0:
                for piece in range(ROW_LEAD):
                    relay_half(piece)
                for piece in range(COL_LEAD):
                    first_half(piece)
            if step + ROW_LEAD < pieces:
                relay_half(step + ROW_LEAD)
            if step + COL_LEAD < pieces:
                first_half(step + COL_LEAD)
            if 0 < step <= pieces:
                second_half(step - 1)
        else:
            pl.when(step + ROW_LEAD < pieces)(lambda: relay_half(step + ROW_LEAD))
            pl.when(step + COL_LEAD < pieces)(lambda: first_half(step + COL_LEAD))
            pl.when(step <= pieces)(lambda: second_half(step - 1))

    def need(first, count=1):
        for piece in range(first, first + count):
            hop_copy(piece, 1).wait_recv()
            hop_copy(piece, 2).wait_recv()

    def chunk_rows(chunk):
        if isinstance(chunk, int):
            return pl.ds(chunk * rows, rows)
        return pl.ds(pl.multiple_of(chunk * rows, rows), rows)

    def put_wide(first, chunk, value):
        for column in range(width // PIECE):
            start = first + column * half_rows + chunk * rows
            if not isinstance(start, int):
                start = pl.multiple_of(start, 8)
            out_ref[pl.ds(start, rows)] = value[:, column * PIECE : (column + 1) * PIECE]

    def give_rows(number, chunk, block):
        place = block.at[t, chunk_rows(chunk)]
        return remote(place, place, x_send.at[number, chunk], x_recv.at[number, chunk], x_peer)

    def give_part(number, chunk):
        return remote(
            out_part.at[chunk_rows(chunk)],
            in_part.at[chunk_rows(chunk)],
            x_send.at[number, chunk],
            x_recv.at[number, chunk],
            x_peer,
        )

    def put_part(number, previous, chunk, value):
        if previous is not None:
            give_part(previous, chunk).wait_send()
        out_part[chunk_rows(chunk)] = value.astype(jnp.bfloat16)
        give_part(number, chunk).start()

    def place_part(index, number, previous, value):
        chunk = index % CHUNKS

        @pl.when(index < CHUNKS)
        def _():
            put_part(number, previous, chunk, value)

        @pl.when(index >= CHUNKS)
        def _():
            own_part[chunk_rows(chunk)] = value

    def core_copy(piece):
        return remote(
            mats.at[piece, :, :, 1 - c],
            from_core.at[piece],
            r_send.at[piece, 0],
            r_recv.at[piece, 0],
            c_peer,
        )

    def col_copy(piece):
        return remote(
            from_core.at[piece, :, 1 - y],
            from_col.at[piece],
            r_send.at[piece, 1],
            r_recv.at[piece, 1],
            y_peer,
        )

    def row_copy(piece, step):
        return remote(
            from_core.at[piece, (z + step + 1) % 4, y],
            from_row.at[piece, step],
            r_send.at[piece, 2 + step],
            r_recv.at[piece, 2 + step],
            z_peers[step],
        )

    def reduce_core(piece):
        core_copy(piece).wait_recv()

        def add_row(row, carry):
            from_core[piece, row] = (
                from_core[piece, row].astype(jnp.float32)
                + mats[piece, row, :, c].astype(jnp.float32)
            ).astype(jnp.bfloat16)
            return carry

        lax.fori_loop(0, 4, add_row, 0)
        col_copy(piece).start()

    def reduce_col(piece):
        col_copy(piece).wait_recv()

        def add_row(row, carry):
            from_core[piece, row, y] = (
                from_core[piece, row, y].astype(jnp.float32) + from_col[piece, row].astype(jnp.float32)
            ).astype(jnp.bfloat16)
            return carry

        lax.fori_loop(0, 4, add_row, 0)
        for step in range(3):
            row_copy(piece, step).start()

    def reduce_row(piece):
        for step in range(3):
            row_copy(piece, step).wait_recv()
        total = from_core[piece, z, y].astype(jnp.float32)
        for step in range(3):
            total = total + from_row[piece, step].astype(jnp.float32)
        out_ref[pl.ds(piece * total.shape[0], total.shape[0])] = total

    def reduce_step(index):
        if isinstance(index, int):
            if index < pieces:
                reduce_core(pieces - 1 - index)
            if 0 <= index - LAG < pieces:
                reduce_col(pieces - 1 - (index - LAG))
            if 0 <= index - 2 * LAG < pieces:
                reduce_row(pieces - 1 - (index - 2 * LAG))
        else:
            pl.when(index < pieces)(lambda: reduce_core(pieces - 1 - index))
            pl.when((index >= LAG) & (index < pieces + LAG))(
                lambda: reduce_col(pieces - 1 - (index - LAG))
            )
            pl.when(index >= 2 * LAG)(lambda: reduce_row(pieces - 1 - (index - 2 * LAG)))

    def put_grad(piece, value):
        mats[piece] = value.astype(jnp.bfloat16).reshape(mats.shape[1:])
        core_copy(piece).start()

    sum_blocks = ((8, 24), (0, 8))

    def sum_copy(phase, step):
        first, count = sum_blocks[phase]
        part = sums_ref.at[pl.ds(first, count)]
        slot = step if step < 3 else 3 + z
        device = (c_peer, y_peer, x_peer)[step] if step < 3 else z_peers[step - 3]
        return remote(
            part,
            sums_in.at[slot, pl.ds(first, count)],
            a_send.at[phase, step],
            a_recv.at[phase, step],
            device,
        )

    def sum_start(phase, step):
        if step < 3:
            sum_copy(phase, step).start()
            return
        first, count = sum_blocks[phase]
        for k in range(3, 6):
            sum_copy(phase, k).start()
        sums_in[3 + z, pl.ds(first, count)] = sums_ref[pl.ds(first, count)]

    def sum_finish(phase, step):
        first, count = sum_blocks[phase]
        block = pl.ds(first, count)
        if step < 3:
            sum_copy(phase, step).wait()
            sums_ref[block] = sums_ref[block] + sums_in[step, block]
            return
        for k in range(3, 6):
            sum_copy(phase, k).wait()
        sums_ref[block] = (sums_in[3, block] + sums_in[4, block]) + (
            sums_in[5, block] + sums_in[6, block]
        )

    def add_sum(row, value, column=None):
        if column is None:
            sums_ref[pl.ds(row, 1)] += value
        else:
            sums_ref[pl.ds(row, 1), column] += value

    def par(row):
        return param[pl.ds(row, 1)]

    def matrix(piece, count=1):
        parts = [mats[piece + j].reshape(width, PIECE) for j in range(count)]
        return parts[0] if count == 1 else jnp.concatenate(parts, axis=1)

    def turn(source):
        def turn_rows(index, carry):
            half, chunk = index // CHUNKS, index % CHUNKS
            columns = pl.ds(pl.multiple_of(index * rows, LANES), rows)
            turned[:, columns] = source[half, chunk_rows(chunk)].T
            return carry

        lax.fori_loop(0, 2 * CHUNKS, turn_rows, 0)

    own_columns = pl.ds(pl.multiple_of(t * PIECE, LANES), PIECE)

    for step in range(3):
        small_z(step).start()
    for piece in range(WINDOW):
        own_copy(piece).wait()
        push(piece)
    for chunk in range(CHUNKS):
        place = x_low.at[0, t, chunk_rows(chunk)]
        remote(
            tokens_ref.at[chunk_rows(chunk)],
            place,
            x_send.at[0, chunk],
            x_recv.at[0, chunk],
            x_peer,
        ).start()
    own_tokens.wait()
    stream[...] = x_low[0, t].astype(jnp.float32)
    small_all[z, y, c] = small_ref[...]
    for piece in range(WINDOW, pieces):
        own_copy(piece).wait()
    seg_k = jnp.broadcast_to(seg_q, (8, length)).T[:, :1]
    allowed = (seg_k > 0) & ((seg_k == seg_q) | (seg_q == 0))
    mask[...] = jnp.where(allowed, 0.0, masked)
    sums_ref[...] = jnp.zeros_like(sums_ref)
    lane = lax.broadcasted_iota(jnp.int32, (1, LANES), 1)
    low_lanes = lane < HEAD_DIM
    low_sub = lax.broadcasted_iota(jnp.int32, (LANES, 1), 0) < HEAD_DIM

    for step in range(3):
        small_z(step).wait_recv()
    small_hop(0).start()
    small_hop(1).start()
    advance(0)
    small_hop(0).wait_recv()
    small_hop(2).start()
    advance(1)
    small_hop(1).wait_recv()
    small_hop(2).wait_recv()
    param[...] = jnp.zeros_like(param)
    ff_shift[...] = jnp.zeros_like(ff_shift)
    counted = jnp.zeros((8, LANES), jnp.float32)
    for place in range(GROUP):
        block = small_all[place // 4, (place // 2) % 2, place % 2]
        offset = place * share
        tile = min(offset // LANES * LANES, width - 2 * LANES)
        shifted = block[:16] if offset == tile else pltpu.roll(block[:16], offset - tile, 1)
        param[pl.ds(0, 16), pl.ds(tile, 2 * LANES)] += shifted
        counted = counted + block[16:24, :LANES]
    hidden_share = ff_shift.shape[1] // (GROUP // 2)
    for place in range(GROUP // 2):
        block = small_all[2 * t + place // 4, (place // 2) % 2, place % 2][16:24]
        offset = place * hidden_share
        tile = offset // LANES * LANES
        if offset != tile:
            block = pltpu.roll(block, offset - tile, 1)
        ff_shift[:, pl.ds(tile, 2 * LANES)] += block
    count_mine[...] = counted
    remote(count_mine, count_theirs, c_send.at[0], c_recv.at[0], x_peer).start()

    def split_heads(pair):
        return jnp.concatenate(
            [jnp.where(low_lanes, pair, 0), jnp.where(low_lanes, 0, pair)], axis=0
        ).astype(pair.dtype)

    def merge_heads(turned_pair):
        size = turned_pair.shape[1] // 2
        return jnp.where(low_sub, turned_pair[:, :size], turned_pair[:, size:]).T

    def pair_lanes(pair):
        return pl.ds(pl.multiple_of(pair * LANES, LANES), LANES)

    def pair_rows(layer, which, pair):
        return qkv[layer, which, :, :, pair_lanes(pair)].reshape(length, LANES)

    def half_of(index):
        return jnp.where(index < CHUNKS, 1 - t, t)

    for layer in range(layers):
        base = layer * per_layer
        ex = 4 * layer
        early = layer == 0

        def project(half, first, count, layer=layer, base=base):
            acc = product(x_low[layer, half], matrix(base + first, count))
            for j in range(first, first + count):
                part = acc[:, (j - first) * PIECE : (j - first + 1) * PIECE]
                if j == 0:
                    part = part + param[pl.ds(14 + layer, 1), own_columns]
                if j == 2:
                    part = part + param[pl.ds(layer * 5, 1), own_columns]
                low = part.astype(jnp.bfloat16)
                if j == 0:
                    low = low * jnp.bfloat16(HEAD_DIM**-0.5)
                qkv[layer, j, half] = low

        def pump(slot, index=None, layer=layer):
            steps = PUMPS[layer].get(slot, ())
            if index is None:
                for step in steps:
                    advance(step)
                return
            for place, step in steps:
                pl.when(index == place)(lambda step=step: advance(step))

        if early:
            for j in range(3):
                if j > 0:
                    advance(j + 1)
                need(base + j)
                project(t, j, 1)
        else:
            need(base, 3)
            project(t, 0, 3)
        pump("own projected")
        for chunk in range(CHUNKS):
            give_rows(ex, chunk, x_low.at[layer]).wait_recv()
        project(1 - t, 0, 3)
        pump("projected")
        for pair in range(pairs):
            pair_turn[pair] = pair_rows(layer, 2, pair).T

        def attend(index, carry, layer=layer, base=base, ex=ex, early=early, pump=pump):
            half, chunk = half_of(index), index % CHUNKS
            where = chunk_rows(chunk)
            columns = pl.ds(pl.multiple_of(half * half_rows + chunk * rows, rows), rows)
            bias = mask[:, columns]
            bias = jnp.concatenate([bias, bias], axis=1)
            pump("attend", index)
            for pair in range(pairs):
                queries = split_heads(qkv[layer, 0, half, where, pair_lanes(pair)])
                scores = product_nt(pair_rows(layer, 1, pair), queries) + bias
                highest = jnp.max(scores, axis=0, keepdims=True)
                exponent = jnp.exp(scores - highest)
                total = jnp.sum(exponent, axis=0, keepdims=True)
                probs = (exponent * (1.0 / total)).astype(jnp.bfloat16)
                log_sum[layer, pair, half, chunk] = highest + jnp.log(total)
                mixed_pair = merge_heads(product(pair_turn[pair], probs))
                heads[layer, half, where, pair_lanes(pair)] = mixed_pair.astype(jnp.bfloat16)
            pl.when(index == 0)(lambda: need(base + 3))
            part = product_nt(heads[layer, half, where], matrix(base + 3))
            place_part(index, ex + 1, None if early else ex - 1, part)
            return carry

        lax.fori_loop(0, 2 * CHUNKS, attend, 0)

        def norm_rows(chunk, carry, layer=layer, ex=ex, pump=pump):
            where = chunk_rows(chunk)
            pump("norm", chunk)
            give_part(ex + 1, chunk).wait_recv()
            total = (
                stream[where] + own_part[where] + in_part[where].astype(jnp.float32) + par(layer * 5 + 1)
            )
            unit, scale = norm_stats(total)
            normed[layer, 0, where] = unit
            inverse[layer, 0, where] = scale
            value = unit * par(10 + layer * 2) + par(layer * 5 + 2)
            stream[where] = value
            h_low[layer, t, where] = value.astype(jnp.bfloat16)
            give_rows(ex + 2, chunk, h_low.at[layer]).start()
            return carry

        lax.fori_loop(0, CHUNKS, norm_rows, 0)

        need(base + 4, 4)

        def feed(half, where, layer=layer, base=base):
            source = h_low[layer, half, where]
            for j in range(0, ups, 2):
                lanes = pl.ds(j * PIECE, 2 * PIECE)
                u = product(source, matrix(base + 4 + j, 2)) + ff_shift[pl.ds(layer, 1), lanes]
                cdf = 0.5 * (1.0 + lax.erf(u * root_half))
                bell = jnp.exp(-0.5 * u * u) * inv_root_tau
                act[layer, half, where, lanes] = (u * cdf).astype(jnp.bfloat16)
                slope[layer, half, where, lanes] = (cdf + u * bell).astype(jnp.bfloat16)

        def down(half, where, layer=layer, base=base):
            return product_nt(act[layer, half, where], matrix(base + 8, ups))

        def feed_peer(chunk, carry, layer=layer, base=base, ex=ex, feed=feed, down=down, pump=pump):
            pump("feed", chunk)
            give_rows(ex + 2, chunk, h_low.at[layer]).wait_recv()
            feed(1 - t, chunk_rows(chunk))
            if layer > 0:

                @pl.when(chunk == 0)
                def _():
                    pump("fed")
                    need(base + 8, 4)

                put_part(ex + 3, ex + 1, chunk, down(1 - t, chunk_rows(chunk)))
            return carry

        def down_peer(chunk, carry, down=down, ex=ex):
            put_part(ex + 3, ex + 1, chunk, down(1 - t, chunk_rows(chunk)))
            return carry

        everything = pl.ds(0, half_rows)
        pump("feed own")
        feed(t, everything)
        lax.fori_loop(0, CHUNKS, feed_peer, 0)
        if layer == 0:
            pump("fed")
            need(base + 8, 4)
            lax.fori_loop(0, CHUNKS, down_peer, 0)
        pump("sent")
        own_part[...] = down(t, everything)
        pump("kept")

        if layer == layers - 1:
            remote(count_mine, count_theirs, c_send.at[0], c_recv.at[0], x_peer).wait()
            count_all = (count_mine[...] + count_theirs[...])[2:3, :1]
            out_ref[pl.ds(spots[3], 8)] = jnp.broadcast_to(count_all, (8, PIECE))
            loss_scale = token_total / count_all
        def end_rows(chunk, carry, layer=layer, ex=ex, pump=pump):
            where = chunk_rows(chunk)
            give_part(ex + 3, chunk).wait_recv()
            total = (
                stream[where] + own_part[where] + in_part[where].astype(jnp.float32) + par(layer * 5 + 3)
            )
            unit, scale = norm_stats(total)
            normed[layer, 1, where] = unit
            inverse[layer, 1, where] = scale
            value = unit * par(11 + layer * 2) + par(layer * 5 + 4)
            if layer < layers - 1:
                stream[where] = value
                x_low[layer + 1, t, where] = value.astype(jnp.bfloat16)
                give_rows(ex + 4, chunk, x_low.at[layer + 1]).start()
            else:
                put_wide(spots[1], chunk, value)
                deviation = value - teacher_ref[where].astype(jnp.float32)
                weighted = weight_ref[where] * deviation
                add_sum(24, jnp.sum(weighted * deviation, axis=0, keepdims=True))
                stream[where] = loss_scale * weighted
            pump("end", chunk)
            return carry

        lax.fori_loop(0, CHUNKS, end_rows, 0)

    def finish_gather(piece, carry):
        for k in range(3):
            when(goes(k), lambda k=k: z_copy(piece, k).wait_send())
            hop_copy(piece, k).wait_send()
        pl.when(relays)(lambda: relay(piece).wait_send())
        return carry

    lax.fori_loop(0, pieces, finish_gather, 0)

    for layer in range(layers - 1, -1, -1):
        base = layer * per_layer
        ex = 4 * layers + 4 * (layers - 1 - layer)
        last = layer == layers - 1
        done = 0 if last else per_layer
        sums_base = layer * 8

        def top_rows(chunk, carry, layer=layer, ex=ex, last=last, sums_base=sums_base):
            where = chunk_rows(chunk)
            if not last:
                give_part(ex - 1, chunk).wait_recv()
                stream[where] += own_part[where] + in_part[where].astype(jnp.float32)
            grad_out, unit = stream[where], normed[layer, 1, where]
            below = norm_back(grad_out, unit, inverse[layer, 1, where], par(11 + layer * 2))
            d_low[layer, 0, t, where] = below.astype(jnp.bfloat16)
            give_rows(ex, chunk, d_low.at[layer, 0]).start()
            stream[where] = below
            add_sum(sums_base + 6, jnp.sum(grad_out * unit, axis=0, keepdims=True))
            add_sum(sums_base + 4, jnp.sum(grad_out, axis=0, keepdims=True))
            add_sum(sums_base + 3, jnp.sum(below, axis=0, keepdims=True))
            return carry

        lax.fori_loop(0, CHUNKS, top_rows, 0)
        if not last:
            reduce_step(9)

        def feed_back(half, where, layer=layer, base=base):
            source = d_low[layer, 0, half, where]
            per_row = width // PIECE
            for j in range(0, ups, 2):
                lanes = pl.ds(j * PIECE, 2 * PIECE)
                du = product(source, matrix(base + 8 + j, 2)) * slope[
                    layer, half, where, lanes
                ].astype(jnp.float32)
                total = jnp.sum(du, axis=0, keepdims=True)
                for k in range(j, j + 2):
                    add_sum(
                        16 + layer * 4 + 2 * t + k // per_row,
                        total[:, (k - j) * PIECE : (k - j + 1) * PIECE],
                        pl.ds(k % per_row * PIECE, PIECE),
                    )
                slope[layer, half, where, lanes] = du.astype(jnp.bfloat16)

        def up_back(half, where, layer=layer, base=base):
            return product_nt(slope[layer, half, where], matrix(base + 4, ups))

        def feed_back_peer(chunk, carry, layer=layer, ex=ex, last=last, feed_back=feed_back, up_back=up_back):
            if not last:
                reduce_step(10 + chunk)
            where = chunk_rows(chunk)
            give_rows(ex, chunk, d_low.at[layer, 0]).wait_recv()
            feed_back(1 - t, where)
            put_part(ex + 1, 4 * layers - 1 if last else ex - 1, chunk, up_back(1 - t, where))
            return carry

        feed_back(t, everything)
        own_part[...] = up_back(t, everything)
        lax.fori_loop(0, CHUNKS, feed_back_peer, 0)

        def mid_rows(chunk, layer=layer, ex=ex, sums_base=sums_base):
            where = chunk_rows(chunk)
            give_part(ex + 1, chunk).wait_recv()
            grad_out = stream[where] + own_part[where] + in_part[where].astype(jnp.float32)
            unit = normed[layer, 0, where]
            below = norm_back(grad_out, unit, inverse[layer, 0, where], par(10 + layer * 2))
            d_low[layer, 1, t, where] = below.astype(jnp.bfloat16)
            give_rows(ex + 2, chunk, d_low.at[layer, 1]).start()
            stream[where] = below
            add_sum(sums_base + 5, jnp.sum(grad_out * unit, axis=0, keepdims=True))
            add_sum(sums_base + 2, jnp.sum(grad_out, axis=0, keepdims=True))
            add_sum(sums_base + 1, jnp.sum(below, axis=0, keepdims=True))

        def pair_grad(piece, left, right, j):
            lanes = pl.ds(j * PIECE, 2 * PIECE)
            if not isinstance(j, int):
                lanes = pl.ds(pl.multiple_of(j * PIECE, LANES), 2 * PIECE)
            both = product(left, right[:, :, lanes].reshape(length, 2 * PIECE))
            put_grad(piece + 1, both[:, PIECE:])
            put_grad(piece, both[:, :PIECE])

        def up_grad(j, layer=layer, base=base, pair_grad=pair_grad):
            pair_grad(base + 4 + j, turned[...], slope.at[layer], j)


        def out_grad(layer=layer, base=base):
            turn(d_low.at[layer, 1])
            put_grad(base + 3, product(turned[...], heads[layer].reshape(length, PIECE)))

        def in_grads(layer=layer, base=base):
            turn(x_low.at[layer])

            def one(index, carry):
                j = 2 - index
                put_grad(base + j, product(turned[...], d_qkv[j].reshape(length, PIECE)))
                return carry

            lax.fori_loop(0, 3, one, 0)

        def sum_move(step, last=last):
            if not last:
                if step > 0:
                    sum_finish(0, step - 1)
                sum_start(0, step)

        def attend_back(turn_number, carry, layer=layer, base=base, ex=ex, done=done):
            half = jnp.where(turn_number == 0, t, 1 - t)

            @pl.when(turn_number == 1)
            def _():
                for chunk in range(CHUNKS):
                    give_rows(ex + 2, chunk, d_low.at[layer, 1]).wait_recv()

            d_heads[half] = product(d_low[layer, 1, half], matrix(base + 3)).astype(jnp.bfloat16)

            def pair_back(pair, carry):
                lanes = pair_lanes(pair)
                keys_in, values_in = pair_rows(layer, 1, pair), pair_rows(layer, 2, pair)

                def chunk_back(chunk, carry):
                    where = chunk_rows(chunk)
                    columns = pl.ds(pl.multiple_of(half * half_rows + chunk * rows, rows), rows)
                    bias = mask[:, columns]
                    bias = jnp.concatenate([bias, bias], axis=1)
                    queries = split_heads(qkv[layer, 0, half, where, lanes])
                    grads = split_heads(d_heads[half, where, lanes])
                    scores = product_nt(keys_in, queries) + bias
                    probs = jnp.exp(scores - log_sum[layer, pair, half, chunk])
                    d_probs = product_nt(values_in, grads)
                    delta = jnp.sum(probs * d_probs, axis=0, keepdims=True)
                    d_scores = (probs * (d_probs - delta)).astype(jnp.bfloat16)
                    double = pl.ds(pl.multiple_of(chunk * 2 * rows, LANES), 2 * rows)
                    probs_all[:, double] = probs.astype(jnp.bfloat16)
                    scores_all[:, double] = d_scores
                    d_query = merge_heads(product(pair_turn[pair], d_scores)) * HEAD_DIM**-0.5
                    d_qkv[0, half, where, lanes] = d_query.astype(jnp.bfloat16)
                    return carry

                lax.fori_loop(0, CHUNKS, chunk_back, 0)
                query_list, grad_list = [], []
                for chunk in range(CHUNKS):
                    where = chunk_rows(chunk)
                    query_list.append(split_heads(qkv[layer, 0, half, where, lanes]))
                    grad_list.append(split_heads(d_heads[half, where, lanes]))
                d_keys = product(scores_all[...], jnp.concatenate(query_list, axis=0))
                d_values = product(probs_all[...], jnp.concatenate(grad_list, axis=0))

                @pl.when(turn_number == 0)
                def _():
                    pair_sums[pair, 0] = d_keys
                    pair_sums[pair, 1] = d_values

                @pl.when(turn_number == 1)
                def _():
                    for which, total in ((1, d_keys), (2, d_values)):
                        total = (total + pair_sums[pair, which - 1]).astype(jnp.bfloat16)
                        d_qkv[which, :, :, lanes] = total.reshape(2, half_rows, LANES)

                pl.when(pair != 1)(lambda: reduce_step(done + 3 + 2 * turn_number + pair // 2))
                return carry

            lax.fori_loop(0, pairs, pair_back, 0)
            return carry

        sum_move(0)
        turn(d_low.at[layer, 0])
        pair_grad(base + 8 + ups - 2, turned[...], act.at[layer], ups - 2)
        mid_rows(0)
        sum_move(1)
        for j in range(ups - 4, -1, -2):
            pair_grad(base + 8 + j, turned[...], act.at[layer], j)
        reduce_step(done)
        mid_rows(1)
        sum_move(2)
        reduce_step(done + 1)
        turn(h_low.at[layer])

        def up_grads(index, carry, up_grad=up_grad):
            up_grad(ups - 2 - 2 * index)
            return carry

        lax.fori_loop(0, ups // 2, up_grads, 0)
        reduce_step(done + 2)
        sum_move(3)
        for pair in range(pairs):
            pair_turn[pair] = pair_rows(layer, 1, pair).T
        lax.fori_loop(0, 2, attend_back, 0)
        if not last:
            out_grad()

        def query_rows(half, where, base=base):
            parts = jnp.concatenate([d_qkv[j, half, where] for j in range(3)], axis=1)
            return product_nt(parts, matrix(base, 3))

        def query_peer(chunk, carry, ex=ex, query_rows=query_rows):
            put_part(ex + 3, ex + 1, chunk, query_rows(1 - t, chunk_rows(chunk)))
            return carry

        add_sum(
            sums_base + 7,
            jnp.sum(d_qkv[0].reshape(length, PIECE).astype(jnp.float32), axis=0, keepdims=True),
            own_columns,
        )
        add_sum(
            sums_base,
            jnp.sum(d_qkv[2].reshape(length, PIECE).astype(jnp.float32), axis=0, keepdims=True),
            own_columns,
        )
        if not last:
            sum_start(1, 0)
        lax.fori_loop(0, CHUNKS, query_peer, 0)
        own_part[...] = query_rows(t, everything)
        reduce_step(done + 7)
        if last:
            out_grad()
        in_grads()
        reduce_step(done + 8)
    def store(first, count, number):
        block = pl.ds(first, count)
        return pltpu.make_async_copy(out_ref.at[block], result_ref.at[block], out_sem.at[number])

    later = per_layer * mats.shape[4]
    stores = (
        store(later, spots[0] - later, 0),
        store(spots[0], spots[4] - spots[0], 1),
        store(0, later, 2),
    )
    stores[0].start()
    for step in range(3):
        sum_finish(1, step)
        sum_start(1, step + 1)
        reduce_step(pieces - 3 + step)
    ex = 8 * layers - 1
    for chunk in range(CHUNKS):
        where = chunk_rows(chunk)
        give_part(ex, chunk).wait_recv()
        put_wide(spots[0], chunk, stream[where] + own_part[where] + in_part[where].astype(jnp.float32))
    sum_finish(0, 3)
    sum_finish(1, 3)
    for column in range(width // PIECE):
        out_ref[pl.ds(spots[2] + column * 32, 32)] = sums_ref[:, column * PIECE : (column + 1) * PIECE]
    stores[1].start()

    def drain(step, carry):
        reduce_step(step)
        return carry

    lax.fori_loop(pieces, pieces + 2 * LAG, drain, 0)
    stores[2].start()

    for step in range(3):
        small_z(step).wait_send()
        small_hop(step).wait_send()
    for chunk in range(CHUNKS):
        give_part(8 * layers - 1, chunk).wait_send()
        for layer in range(layers):
            give_rows(4 * layer, chunk, x_low.at[layer]).wait_send()
            give_rows(4 * layer + 2, chunk, h_low.at[layer]).wait_send()
            number = 4 * layers + 4 * (layers - 1 - layer)
            give_rows(number, chunk, d_low.at[layer, 0]).wait_send()
            give_rows(number + 2, chunk, d_low.at[layer, 1]).wait_send()

    def finish_grads(piece, carry):
        core_copy(piece).wait_send()
        col_copy(piece).wait_send()
        for step in range(3):
            row_copy(piece, step).wait_send()
        return carry

    lax.fori_loop(0, pieces, finish_grads, 0)
    for copy in stores:
        copy.wait()


def run_step(extra, token_total, matrices, vectors, tokens, teacher, valid, seg_ids, counted):
    attn_in, attn_out, ff_in, ff_out = matrices
    rows, width = tokens.shape
    length = 2 * rows
    layers, share, hidden_width = ff_in.shape
    ups = hidden_width // PIECE
    pieces = layers * (4 + 2 * ups)
    low, full = jnp.bfloat16, jnp.float32
    chunk = rows // CHUNKS
    pairs = PIECE // LANES
    blocks = (4, 2, 2, share, PIECE)
    dma = pltpu.SemaphoreType.DMA
    vmem = pl.BlockSpec(memory_space=pltpu.VMEM)
    operands = [*matrices, tokens, *vectors, teacher, valid, seg_ids]
    kernel = functools.partial(step_kernel, extra, token_total)
    if counted is None:
        inputs = len(operands)

        def body(*refs):
            kernel(*refs[:inputs], None, *refs[inputs:])

    else:
        operands.append(counted)
        body = kernel
    return pl.pallas_call(
        body,
        out_shape=jax.ShapeDtypeStruct((places(pieces * share, rows)[4], PIECE), full),
        in_specs=[pl.BlockSpec(memory_space=pl.ANY)] * 5 + [vmem] * (len(operands) - 5),
        out_specs=pl.BlockSpec(memory_space=pl.ANY),
        scratch_shapes=[
            pltpu.VMEM((places(pieces * share, rows)[4], PIECE), full),
            pltpu.VMEM((pieces, *blocks), low),
            pltpu.VMEM((4, 2, 2, 24, 2 * LANES), full),
            pltpu.VMEM((16, width), full),
            pltpu.VMEM((8, hidden_width), full),
            pltpu.VMEM((pieces, 4, 2, share, PIECE), low),
            pltpu.VMEM((pieces, 4, share, PIECE), low),
            pltpu.VMEM((pieces, 3, share, PIECE), low),
            pltpu.VMEM((layers, 2, rows, width), low),
            pltpu.VMEM((layers, 3, 2, rows, PIECE), low),
            pltpu.VMEM((layers, 2, rows, PIECE), low),
            pltpu.VMEM((layers, pairs, 2, CHUNKS, 1, 2 * chunk), full),
            pltpu.VMEM((layers, 2, rows, width), low),
            pltpu.VMEM((layers, 2, rows, hidden_width), low),
            pltpu.VMEM((layers, 2, rows, hidden_width), low),
            pltpu.VMEM((layers, 2, rows, width), full),
            pltpu.VMEM((layers, 2, rows, 1), full),
            pltpu.VMEM((rows, width), full),
            pltpu.VMEM((rows, width), low),
            pltpu.VMEM((rows, width), low),
            pltpu.VMEM((rows, width), full),
            pltpu.VMEM((layers, 2, 2, rows, width), low),
            pltpu.VMEM((3, 2, rows, PIECE), low),
            pltpu.VMEM((2, rows, PIECE), low),
            pltpu.VMEM((length, length), full),
            pltpu.VMEM((pairs, LANES, length), low),
            pltpu.VMEM((length, length), low),
            pltpu.VMEM((length, length), low),
            pltpu.VMEM((pairs, 2, length, LANES), full),
            pltpu.VMEM((width, length), low),
            pltpu.VMEM((7, 32, width), full),
            pltpu.VMEM((32, width), full),
            pltpu.VMEM((8, LANES), full),
            pltpu.VMEM((8, LANES), full),
            pltpu.VMEM((24, 2 * LANES), full),
            pltpu.VMEM((rows, 1), full),
            dma((pieces, 4)),
            dma((pieces, 3)),
            dma((pieces, 3)),
            dma((pieces, 3)),
            dma((pieces + 1,)),
            dma((6,)),
            dma((6,)),
            dma((8 * layers, CHUNKS)),
            dma((8 * layers, CHUNKS)),
            dma((pieces, 5)),
            dma((pieces, 5)),
            dma((2, 6)),
            dma((2, 6)),
            dma((1,)),
            dma((1,)),
            dma((3,)),
        ],
        compiler_params=pltpu.CompilerParams(
            collective_id=0, has_side_effects=True, vmem_limit_bytes=67_043_328
        ),
        name="encoder_step",
    )(*operands)


def sibling_groups(extra):
    size = lax.axis_size("fsdp")
    return [list(range(first, first + extra)) for first in range(0, size, extra)]


def widen(shard, extra, axis):
    if extra == 1:
        return shard
    return lax.all_gather(
        shard, "fsdp", axis=axis, axis_index_groups=sibling_groups(extra), tiled=True
    )


def sum_siblings(value, extra):
    if extra == 1:
        return value
    return lax.psum(value, "fsdp", axis_index_groups=sibling_groups(extra))


def finish_kernel(
    place_count,
    all_ref,
    mixed_out,
    tokens_grad_out,
    loss_out,
    attn_in_out,
    attn_out_out,
    ff_in_out,
    ff_out_out,
    biases_out,
    gains_out,
    ff_bias_out,
    query_out,
    sums_ref,
):
    layers, share = attn_out_out.shape[0], attn_out_out.shape[1]
    rows, width = mixed_out.shape
    ups = ff_in_out.shape[2] // PIECE
    per_layer = 4 + 2 * ups
    spots = places(layers * per_layer * share, rows)

    def grad(piece):
        return all_ref[pl.ds(piece * share, share)]

    for column in range(width // PIECE):
        lanes = pl.ds(column * PIECE, PIECE)
        tokens_grad_out[:, lanes] = all_ref[pl.ds(spots[0] + column * rows, rows)]
        mixed_out[:, lanes] = all_ref[pl.ds(spots[1] + column * rows, rows)].astype(mixed_out.dtype)
        sums_ref[:, lanes] = all_ref[pl.ds(spots[2] + column * 32, 32)]
    for layer in range(layers):
        base = layer * per_layer
        for j in range(3):
            attn_in_out[layer, j] = grad(base + j)
        attn_out_out[layer] = grad(base + 3)
        for j in range(ups):
            lanes = pl.ds(j * PIECE, PIECE)
            ff_in_out[layer, :, lanes] = grad(base + 4 + j)
            ff_out_out[layer, :, lanes] = grad(base + 4 + ups + j)
    squares = jnp.sum(sums_ref[pl.ds(24, 1)], axis=1, keepdims=True)
    loss_out[...] = squares / (all_ref[pl.ds(spots[3], 8)][:1, :1] * width)
    place = lax.axis_index("fsdp")
    share = width // place_count
    own = pltpu.roll(sums_ref[:16], (width - place * share) % width, 1)[:, :share]
    up_share = ff_bias_out.shape[1]
    first = place * up_share
    for layer in range(layers):
        for kind in range(biases_out.shape[0]):
            biases_out[kind, pl.ds(layer, 1)] = own[layer * 8 + kind : layer * 8 + kind + 1]
        gains_out[layer] = own[layer * 8 + 5 : layer * 8 + 7]
        query_out[pl.ds(layer, 1)] = own[layer * 8 + 7 : layer * 8 + 8]
        row = jnp.broadcast_to(sums_ref[pl.ds(16 + layer * 4 + first // width, 1)], (8, width))
        ff_bias_out[pl.ds(layer, 1)] = pltpu.roll(row, (width - first % width) % width, 1)[:1, :up_share]


def on_device(
    tokens,
    segments,
    valid,
    teacher,
    attn_in,
    attn_out,
    ff_in,
    ff_out,
    biases,
    gains,
    ff_bias,
    query_bias,
):
    size = lax.axis_size("fsdp")
    extra = size // GROUP
    layers = attn_in.shape[0]
    rows_dev, width = tokens.shape[1], tokens.shape[2]
    length = segments.shape[1]

    matrices = (
        jnp.swapaxes(widen(attn_in, extra, 1), 1, 2),
        widen(attn_out, extra, 1),
        widen(ff_in, extra, 1),
        widen(ff_out, extra, 1),
    )
    vectors = (
        jnp.swapaxes(widen(biases, extra, 2), 0, 1),
        widen(gains, extra, 2),
        widen(ff_bias, extra, 1),
        widen(query_bias, extra, 1),
    )
    counted = None
    if extra > 1:
        own_seg = lax.dynamic_slice_in_dim(segments, lax.axis_index("tp") * rows_dev, rows_dev, 1)
        total = sum_siblings(jnp.sum((valid * (own_seg > 0)).astype(jnp.float32)), extra)
        counted = jnp.broadcast_to(total, (8, LANES))
    results = run_step(
        extra,
        float(length * size),
        matrices,
        vectors,
        tokens[0],
        teacher[0],
        valid,
        segments,
        counted,
    )
    if extra > 1:
        share = width // GROUP
        spots = places(results.shape[0] - places(0, rows_dev)[4], rows_dev)
        grads = lax.psum_scatter(
            results[: spots[0]].reshape(-1, share, PIECE),
            "fsdp",
            scatter_dimension=1,
            axis_index_groups=sibling_groups(extra),
            tiled=True,
        )
        sums = sum_siblings(results[spots[2] : spots[3]], extra)
        results = jnp.concatenate(
            [grads.reshape(-1, PIECE), results[spots[0] : spots[2]], sums, results[spots[3] :]], axis=0
        )
    vmem = pl.BlockSpec(memory_space=pltpu.VMEM)
    full = jnp.float32
    shapes = [
        jax.ShapeDtypeStruct((rows_dev, width), jnp.bfloat16),
        jax.ShapeDtypeStruct((rows_dev, width), full),
        jax.ShapeDtypeStruct((1, 1), full),
    ]
    turned_in = (layers, 3, attn_in.shape[1], PIECE)
    turned_biases = (biases.shape[1], layers, biases.shape[2])
    for shape in (turned_in, attn_out.shape, ff_in.shape, ff_out.shape, turned_biases):
        shapes.append(jax.ShapeDtypeStruct(shape, full))
    for part in (gains, ff_bias, query_bias):
        shapes.append(jax.ShapeDtypeStruct(part.shape, full))
    mixed, tokens_grad, loss, in_grad, out_grad, up_grad, down_grad, bias_grad, *rest = pl.pallas_call(
        functools.partial(finish_kernel, size),
        out_shape=tuple(shapes),
        in_specs=[vmem],
        out_specs=(vmem,) * len(shapes),
        scratch_shapes=[pltpu.VMEM((32, width), full)],
        compiler_params=pltpu.CompilerParams(vmem_limit_bytes=24 * 1024 * 1024),
        name="place_results",
    )(results)
    return (
        mixed[None],
        tokens_grad[None],
        loss[0, 0],
        jnp.swapaxes(in_grad, 1, 2),
        out_grad,
        up_grad,
        down_grad,
        jnp.swapaxes(bias_grad, 0, 1),
        *rest,
    )


def solution(mesh):
    in_specs = (
        P("fsdp", "tp", None),
        P("fsdp", None),
        P("fsdp", "tp"),
        P("fsdp", "tp", None),
        P(None, "fsdp", None, "tp"),
        P(None, "fsdp", "tp"),
        P(None, "fsdp", "tp"),
        P(None, "fsdp", "tp"),
        P(None, None, "fsdp"),
        P(None, None, "fsdp"),
        P(None, "fsdp"),
        P(None, "fsdp"),
    )
    out_specs = (
        P("fsdp", "tp", None),
        P("fsdp", "tp", None),
        P(),
        P(None, "fsdp", None, "tp"),
        P(None, "fsdp", "tp"),
        P(None, "fsdp", "tp"),
        P(None, "fsdp", "tp"),
        P(None, None, "fsdp"),
        P(None, None, "fsdp"),
        P(None, "fsdp"),
        P(None, "fsdp"),
    )
    return jax.shard_map(
        on_device, mesh=mesh, in_specs=in_specs, out_specs=out_specs, check_vma=False
    )
```

```python
import functools

import jax
import jax.numpy as jnp
from jax import lax
from jax.experimental import pallas as pl
from jax.experimental.pallas import tpu as pltpu
from jax.sharding import PartitionSpec as P

HEAD_DIM = 64
MESH = pl.DeviceIdType.MESH
PIECE = 384
CHUNKS = 2
LANES = 128
GROUP = 16
WINDOW = 2
ROW_LEAD = 2
COL_LEAD = 1
PUMPS = (
    {
        "projected": (4,),
        "attend": ((1, 5), (2, 6)),
        "norm": ((0, 7), (1, 8)),
        "feed own": (9,),
        "feed": ((0, 10),),
        "fed": (11, 12),
        "sent": (13,),
        "kept": (14,),
        "end": ((0, 15), (1, 16)),
    },
    {
        "own projected": (17, 18),
        "projected": (19,),
        "attend": ((2, 20),),
        "norm": ((0, 21), (1, 22)),
        "feed": ((0, 23),),
        "fed": (24,),
    },
)
LAG = 2
LATE = 6

epsilon = 1e-05
root_half = 0.7071067811865476
inv_root_tau = 0.3989422804014327
masked = -1e30


def product(left, right):
    return lax.dot_general(left, right, (((1,), (0,)), ((), ())), preferred_element_type=jnp.float32)


def product_nt(left, right):
    return lax.dot_general(left, right, (((1,), (1,)), ((), ())), preferred_element_type=jnp.float32)


def norm_stats(total):
    centred = total - jnp.mean(total, axis=-1, keepdims=True)
    inverse = lax.rsqrt(jnp.mean(centred * centred, axis=-1, keepdims=True) + epsilon)
    return centred * inverse, inverse


def norm_back(grad_out, normed, inverse, gain):
    scaled = grad_out * gain
    return inverse * (
        scaled
        - jnp.mean(scaled, axis=-1, keepdims=True)
        - normed * jnp.mean(scaled * normed, axis=-1, keepdims=True)
    )


def places(grad_rows, rows):
    first = grad_rows
    return first, first + 2 * rows, first + 4 * rows, first + 4 * rows + 64, first + 4 * rows + 72


def step_kernel(
    extra,
    token_total,
    attn_in_ref,
    attn_out_ref,
    ff_in_ref,
    ff_out_ref,
    tokens_ref,
    biases_ref,
    gains_ref,
    ff_bias_ref,
    query_ref,
    teacher_ref,
    valid_ref,
    seg_ref,
    count_in_ref,
    result_ref,
    out_ref,
    mats,
    small_all,
    param,
    ff_shift,
    from_core,
    from_col,
    from_row,
    x_low,
    qkv,
    heads,
    log_sum,
    h_low,
    act,
    slope,
    normed,
    inverse,
    stream,
    out_part,
    in_part,
    own_part,
    d_low,
    d_qkv,
    d_heads,
    mask,
    pair_turn,
    probs_all,
    scores_all,
    pair_sums,
    turned,
    sums_in,
    sums_ref,
    count_mine,
    count_theirs,
    small_ref,
    weight_ref,
    z_send,
    z_recv,
    hop_send,
    hop_recv,
    local_sem,
    s_send,
    s_recv,
    x_send,
    x_recv,
    r_send,
    r_recv,
    a_send,
    a_recv,
    c_send,
    c_recv,
    out_sem,
):
    pieces = mats.shape[0]
    spots = places(pieces * mats.shape[4], teacher_ref.shape[0])
    layers = x_low.shape[0]
    per_layer = pieces // layers
    half_rows = tokens_ref.shape[0]
    width = tokens_ref.shape[1]
    length = 2 * half_rows
    rows = half_rows // CHUNKS
    pairs = PIECE // LANES
    ups = act.shape[3] // PIECE

    spot = lax.axis_index("fsdp") // extra
    rest = lax.axis_index("fsdp") % extra
    t = lax.axis_index("tp")
    z, y, c = spot // 4, (spot // 2) % 2, spot % 2

    def peer(row, col, core):
        return {"fsdp": ((row * 2 + col) * 2 + core) * extra + rest, "tp": t}

    z_peers = [peer((z + step) % 4, y, c) for step in (1, 2, 3)]
    y_peer = peer(z, 1 - y, c)
    c_peer = peer(z, y, 1 - c)
    x_peer = {"fsdp": lax.axis_index("fsdp"), "tp": 1 - t}
    shards = []
    for layer in range(layers):
        shards += [attn_in_ref.at[layer, j] for j in range(3)]
        for source in (attn_out_ref, ff_in_ref, ff_out_ref):
            shards += [
                source.at[layer, :, pl.ds(j * PIECE, PIECE)] for j in range(source.shape[2] // PIECE)
            ]

    def own_copy(piece):
        return pltpu.make_async_copy(shards[piece], mats.at[piece, z, y, c], local_sem.at[piece])

    own_tokens = pltpu.make_async_copy(tokens_ref, x_low.at[0, t], local_sem.at[pieces])
    own_tokens.start()
    for piece in range(pieces):
        own_copy(piece).start()
    everyone = (*z_peers, y_peer, c_peer, x_peer)
    barrier = pltpu.get_barrier_semaphore()
    for other in everyone:
        pl.semaphore_signal(barrier, inc=1, device_id=other, device_id_type=MESH)
    seg_q = seg_ref[...].astype(jnp.float32)
    half_lanes = pl.ds(pl.multiple_of(t * half_rows, LANES), half_rows)
    counted_rows = valid_ref[...] * (seg_ref[:, half_lanes] > 0).astype(jnp.int32)
    weights = jnp.broadcast_to(counted_rows.astype(jnp.float32), (8, half_rows)).T
    weight_ref[...] = weights[:, :1]
    if count_in_ref is None:
        count_local = jnp.sum(weights[:, :1], axis=0, keepdims=True)
    else:
        count_local = count_in_ref[:1, :1]
    small_ref[...] = jnp.zeros_like(small_ref)
    share = biases_ref.shape[2]
    kinds = biases_ref.shape[0]
    for layer in range(layers):
        for kind in range(kinds):
            line = biases_ref[kind].astype(jnp.float32)[layer : layer + 1]
            small_ref[pl.ds(layer * kinds + kind, 1), pl.ds(0, share)] = line
        small_ref[pl.ds(10 + layer * 2, 2), pl.ds(0, share)] = gains_ref[layer].astype(jnp.float32)
    small_ref[pl.ds(14, layers), pl.ds(0, share)] = query_ref[...].astype(jnp.float32)
    small_ref[pl.ds(16, layers), pl.ds(0, ff_bias_ref.shape[1])] = ff_bias_ref[...].astype(jnp.float32)
    small_ref[pl.ds(18, 6)] = jnp.broadcast_to(count_local, (6, small_ref.shape[1]))
    pl.semaphore_wait(barrier, len(everyone))

    def remote(src, dst, send_sem, recv_sem, device):
        return pltpu.make_async_remote_copy(
            src_ref=src,
            dst_ref=dst,
            send_sem=send_sem,
            recv_sem=recv_sem,
            device_id=device,
            device_id_type=MESH,
        )

    def z_copy(piece, step):
        return remote(
            mats.at[piece, z, y, c],
            mats.at[piece, z, y, c],
            z_send.at[piece, step],
            z_recv.at[piece, step],
            z_peers[step],
        )

    relays = (z == 1) | (z == 2)

    def goes(step):
        if step == 1:
            return None
        return (z != 0) if step == 2 else (z != 3)

    def when(condition, action):
        if condition is None:
            action()
        else:
            pl.when(condition)(action)

    def relay(piece):
        source = jnp.where(z == 2, 0, 3)
        block = mats.at[piece, source, y, c]
        return remote(
            block,
            block,
            z_send.at[piece, 3],
            z_recv.at[piece, jnp.where(z == 2, 2, 0)],
            peer(3 - source, y, c),
        )

    def push(piece):
        for step in range(3):
            when(goes(step), lambda step=step: z_copy(piece, step).start())

    def relay_half(piece):
        z_copy(piece, 1).wait_recv()
        pl.when(relays)(lambda: relay(piece).start())
        if isinstance(piece, int):
            if piece + WINDOW < pieces:
                push(piece + WINDOW)
        else:
            pl.when(piece + WINDOW < pieces)(lambda: push(piece + WINDOW))

    def hop_copy(piece, kind):
        column = 1 - y if kind == 2 else y
        block = mats.at[piece, :, column, c]
        return remote(
            block,
            block,
            hop_send.at[piece, kind],
            hop_recv.at[piece, kind],
            y_peer if kind == 0 else c_peer,
        )

    def small_z(step):
        block = small_all.at[z, y, c]
        return remote(small_ref, block, s_send.at[step], s_recv.at[step], z_peers[step])

    def small_hop(kind):
        column = 1 - y if kind == 2 else y
        block = small_all.at[:, column, c]
        return remote(
            block, block, s_send.at[3 + kind], s_recv.at[3 + kind], y_peer if kind == 0 else c_peer
        )

    def first_half(piece):
        z_copy(piece, 0).wait_recv()
        z_copy(piece, 2).wait_recv()
        hop_copy(piece, 0).start()
        hop_copy(piece, 1).start()

    def second_half(piece):
        hop_copy(piece, 0).wait_recv()
        hop_copy(piece, 2).start()

    def advance(step):
        if isinstance(step, int):
            if step == 0:
                for piece in range(ROW_LEAD):
                    relay_half(piece)
                for piece in range(COL_LEAD):
                    first_half(piece)
            if step + ROW_LEAD < pieces:
                relay_half(step + ROW_LEAD)
            if step + COL_LEAD < pieces:
                first_half(step + COL_LEAD)
            if 0 < step <= pieces:
                second_half(step - 1)
        else:
            pl.when(step + ROW_LEAD < pieces)(lambda: relay_half(step + ROW_LEAD))
            pl.when(step + COL_LEAD < pieces)(lambda: first_half(step + COL_LEAD))
            pl.when(step <= pieces)(lambda: second_half(step - 1))

    def need(first, count=1):
        for piece in range(first, first + count):
            hop_copy(piece, 1).wait_recv()
            hop_copy(piece, 2).wait_recv()

    def chunk_rows(chunk):
        if isinstance(chunk, int):
            return pl.ds(chunk * rows, rows)
        return pl.ds(pl.multiple_of(chunk * rows, rows), rows)

    def put_wide(first, chunk, value):
        for column in range(width // PIECE):
            start = first + column * half_rows + chunk * rows
            if not isinstance(start, int):
                start = pl.multiple_of(start, 8)
            out_ref[pl.ds(start, rows)] = value[:, column * PIECE : (column + 1) * PIECE]

    def give_rows(number, chunk, block):
        place = block.at[t, chunk_rows(chunk)]
        return remote(place, place, x_send.at[number, chunk], x_recv.at[number, chunk], x_peer)

    def give_part(number, chunk):
        return remote(
            out_part.at[chunk_rows(chunk)],
            in_part.at[chunk_rows(chunk)],
            x_send.at[number, chunk],
            x_recv.at[number, chunk],
            x_peer,
        )

    def put_part(number, previous, chunk, value):
        if previous is not None:
            give_part(previous, chunk).wait_send()
        out_part[chunk_rows(chunk)] = value.astype(jnp.bfloat16)
        give_part(number, chunk).start()

    def place_part(index, number, previous, value):
        chunk = index % CHUNKS

        @pl.when(index < CHUNKS)
        def _():
            put_part(number, previous, chunk, value)

        @pl.when(index >= CHUNKS)
        def _():
            own_part[chunk_rows(chunk)] = value

    def core_copy(piece):
        return remote(
            mats.at[piece, :, :, 1 - c],
            from_core.at[piece],
            r_send.at[piece, 0],
            r_recv.at[piece, 0],
            c_peer,
        )

    def col_copy(piece):
        return remote(
            from_core.at[piece, :, 1 - y],
            from_col.at[piece],
            r_send.at[piece, 1],
            r_recv.at[piece, 1],
            y_peer,
        )

    def row_copy(piece, step):
        return remote(
            from_core.at[piece, (z + step + 1) % 4, y],
            from_row.at[piece, step],
            r_send.at[piece, 2 + step],
            r_recv.at[piece, 2 + step],
            z_peers[step],
        )

    def reduce_core(piece):
        core_copy(piece).wait_recv()

        def add_row(row, carry):
            from_core[piece, row] = from_core[piece, row] + mats[piece, row, :, c]
            return carry

        lax.fori_loop(0, 4, add_row, 0)
        col_copy(piece).start()

    def reduce_col(piece):
        col_copy(piece).wait_recv()

        def add_row(row, carry):
            from_core[piece, row, y] = from_core[piece, row, y] + from_col[piece, row]
            return carry

        lax.fori_loop(0, 4, add_row, 0)
        for step in range(3):
            row_copy(piece, step).start()

    def reduce_row(piece):
        for step in range(3):
            row_copy(piece, step).wait_recv()
        total = from_core[piece, z, y].astype(jnp.float32)
        for step in range(3):
            total = total + from_row[piece, step].astype(jnp.float32)
        out_ref[pl.ds(piece * total.shape[0], total.shape[0])] = total

    def reduce_step(index):
        if isinstance(index, int):
            if index < pieces:
                reduce_core(pieces - 1 - index)
            if 0 <= index - LAG < pieces:
                reduce_col(pieces - 1 - (index - LAG))
            if 0 <= index - LATE < pieces:
                reduce_row(pieces - 1 - (index - LATE))
        else:
            pl.when(index < pieces)(lambda: reduce_core(pieces - 1 - index))
            pl.when((index >= LAG) & (index < pieces + LAG))(
                lambda: reduce_col(pieces - 1 - (index - LAG))
            )
            pl.when(index >= LATE)(lambda: reduce_row(pieces - 1 - (index - LATE)))

    def put_grad(piece, value):
        mats[piece] = value.astype(jnp.bfloat16).reshape(mats.shape[1:])
        core_copy(piece).start()

    sum_blocks = ((8, 24), (0, 8))

    def sum_copy(phase, step):
        first, count = sum_blocks[phase]
        part = sums_ref.at[pl.ds(first, count)]
        slot = step if step < 3 else 3 + z
        device = (c_peer, y_peer, x_peer)[step] if step < 3 else z_peers[step - 3]
        return remote(
            part,
            sums_in.at[slot, pl.ds(first, count)],
            a_send.at[phase, step],
            a_recv.at[phase, step],
            device,
        )

    def sum_start(phase, step):
        if step < 3:
            sum_copy(phase, step).start()
            return
        first, count = sum_blocks[phase]
        for k in range(3, 6):
            sum_copy(phase, k).start()
        sums_in[3 + z, pl.ds(first, count)] = sums_ref[pl.ds(first, count)]

    def sum_finish(phase, step):
        first, count = sum_blocks[phase]
        block = pl.ds(first, count)
        if step < 3:
            sum_copy(phase, step).wait()
            sums_ref[block] = sums_ref[block] + sums_in[step, block]
            return
        for k in range(3, 6):
            sum_copy(phase, k).wait()
        sums_ref[block] = (sums_in[3, block] + sums_in[4, block]) + (
            sums_in[5, block] + sums_in[6, block]
        )

    def add_sum(row, value, column=None):
        if column is None:
            sums_ref[pl.ds(row, 1)] += value
        else:
            sums_ref[pl.ds(row, 1), column] += value

    def par(row):
        return param[pl.ds(row, 1)]

    def matrix(piece, count=1):
        parts = [mats[piece + j].reshape(width, PIECE) for j in range(count)]
        return parts[0] if count == 1 else jnp.concatenate(parts, axis=1)

    def turn(source):
        def turn_rows(index, carry):
            half, chunk = index // CHUNKS, index % CHUNKS
            columns = pl.ds(pl.multiple_of(index * rows, LANES), rows)
            turned[:, columns] = source[half, chunk_rows(chunk)].T
            return carry

        lax.fori_loop(0, 2 * CHUNKS, turn_rows, 0)

    own_columns = pl.ds(pl.multiple_of(t * PIECE, LANES), PIECE)

    for step in range(3):
        small_z(step).start()
    for piece in range(WINDOW):
        own_copy(piece).wait()
        push(piece)
    for chunk in range(CHUNKS):
        place = x_low.at[0, t, chunk_rows(chunk)]
        remote(
            tokens_ref.at[chunk_rows(chunk)],
            place,
            x_send.at[0, chunk],
            x_recv.at[0, chunk],
            x_peer,
        ).start()
    own_tokens.wait()
    stream[...] = x_low[0, t].astype(jnp.float32)
    small_all[z, y, c] = small_ref[...]
    for piece in range(WINDOW, pieces):
        own_copy(piece).wait()
    seg_k = jnp.broadcast_to(seg_q, (8, length)).T[:, :1]
    allowed = (seg_k > 0) & ((seg_k == seg_q) | (seg_q == 0))
    mask[...] = jnp.where(allowed, 0.0, masked)
    sums_ref[...] = jnp.zeros_like(sums_ref)
    lane = lax.broadcasted_iota(jnp.int32, (1, LANES), 1)
    low_lanes = lane < HEAD_DIM
    low_sub = lax.broadcasted_iota(jnp.int32, (LANES, 1), 0) < HEAD_DIM

    for step in range(3):
        small_z(step).wait_recv()
    small_hop(0).start()
    small_hop(1).start()
    advance(0)
    small_hop(0).wait_recv()
    small_hop(2).start()
    advance(1)
    small_hop(1).wait_recv()
    small_hop(2).wait_recv()
    param[...] = jnp.zeros_like(param)
    ff_shift[...] = jnp.zeros_like(ff_shift)
    counted = jnp.zeros((8, LANES), jnp.float32)
    for place in range(GROUP):
        block = small_all[place // 4, (place // 2) % 2, place % 2]
        offset = place * share
        tile = min(offset // LANES * LANES, width - 2 * LANES)
        shifted = block[:16] if offset == tile else pltpu.roll(block[:16], offset - tile, 1)
        param[pl.ds(0, 16), pl.ds(tile, 2 * LANES)] += shifted
        counted = counted + block[16:24, :LANES]
    hidden_share = ff_shift.shape[1] // (GROUP // 2)
    for place in range(GROUP // 2):
        block = small_all[2 * t + place // 4, (place // 2) % 2, place % 2][16:24]
        offset = place * hidden_share
        tile = offset // LANES * LANES
        if offset != tile:
            block = pltpu.roll(block, offset - tile, 1)
        ff_shift[:, pl.ds(tile, 2 * LANES)] += block
    count_mine[...] = counted
    remote(count_mine, count_theirs, c_send.at[0], c_recv.at[0], x_peer).start()

    def split_heads(pair):
        return jnp.concatenate(
            [jnp.where(low_lanes, pair, 0), jnp.where(low_lanes, 0, pair)], axis=0
        ).astype(pair.dtype)

    def merge_heads(turned_pair):
        size = turned_pair.shape[1] // 2
        return jnp.where(low_sub, turned_pair[:, :size], turned_pair[:, size:]).T

    def pair_lanes(pair):
        return pl.ds(pl.multiple_of(pair * LANES, LANES), LANES)

    def pair_rows(layer, which, pair):
        return qkv[layer, which, :, :, pair_lanes(pair)].reshape(length, LANES)

    def half_of(index):
        return jnp.where(index < CHUNKS, 1 - t, t)

    for layer in range(layers):
        base = layer * per_layer
        ex = 4 * layer
        early = layer == 0

        def project(half, first, count, layer=layer, base=base):
            acc = product(x_low[layer, half], matrix(base + first, count))
            for j in range(first, first + count):
                part = acc[:, (j - first) * PIECE : (j - first + 1) * PIECE]
                if j == 0:
                    part = part + param[pl.ds(14 + layer, 1), own_columns]
                if j == 2:
                    part = part + param[pl.ds(layer * 5, 1), own_columns]
                low = part.astype(jnp.bfloat16)
                if j == 0:
                    low = low * jnp.bfloat16(HEAD_DIM**-0.5)
                qkv[layer, j, half] = low

        def pump(slot, index=None, layer=layer):
            steps = PUMPS[layer].get(slot, ())
            if index is None:
                for step in steps:
                    advance(step)
                return
            for place, step in steps:
                pl.when(index == place)(lambda step=step: advance(step))

        if early:
            for j in range(3):
                if j > 0:
                    advance(j + 1)
                need(base + j)
                project(t, j, 1)
        else:
            need(base, 3)
            project(t, 0, 3)
        pump("own projected")
        for chunk in range(CHUNKS):
            give_rows(ex, chunk, x_low.at[layer]).wait_recv()
        project(1 - t, 0, 3)
        pump("projected")
        for pair in range(pairs):
            pair_turn[pair] = pair_rows(layer, 2, pair).T

        def attend(index, carry, layer=layer, base=base, ex=ex, early=early, pump=pump):
            half, chunk = half_of(index), index % CHUNKS
            where = chunk_rows(chunk)
            columns = pl.ds(pl.multiple_of(half * half_rows + chunk * rows, rows), rows)
            bias = mask[:, columns]
            bias = jnp.concatenate([bias, bias], axis=1)
            pump("attend", index)
            for pair in range(pairs):
                queries = split_heads(qkv[layer, 0, half, where, pair_lanes(pair)])
                scores = product_nt(pair_rows(layer, 1, pair), queries) + bias
                highest = jnp.max(scores, axis=0, keepdims=True)
                exponent = jnp.exp(scores - highest)
                total = jnp.sum(exponent, axis=0, keepdims=True)
                probs = (exponent * (1.0 / total)).astype(jnp.bfloat16)
                log_sum[layer, pair, half, chunk] = highest + jnp.log(total)
                mixed_pair = merge_heads(product(pair_turn[pair], probs))
                heads[layer, half, where, pair_lanes(pair)] = mixed_pair.astype(jnp.bfloat16)
            pl.when(index == 0)(lambda: need(base + 3))
            part = product_nt(heads[layer, half, where], matrix(base + 3))
            place_part(index, ex + 1, None if early else ex - 1, part)
            return carry

        lax.fori_loop(0, 2 * CHUNKS, attend, 0)

        def norm_rows(chunk, carry, layer=layer, ex=ex, pump=pump):
            where = chunk_rows(chunk)
            pump("norm", chunk)
            give_part(ex + 1, chunk).wait_recv()
            total = (
                stream[where] + own_part[where] + in_part[where].astype(jnp.float32) + par(layer * 5 + 1)
            )
            unit, scale = norm_stats(total)
            normed[layer, 0, where] = unit
            inverse[layer, 0, where] = scale
            value = unit * par(10 + layer * 2) + par(layer * 5 + 2)
            stream[where] = value
            h_low[layer, t, where] = value.astype(jnp.bfloat16)
            give_rows(ex + 2, chunk, h_low.at[layer]).start()
            return carry

        lax.fori_loop(0, CHUNKS, norm_rows, 0)

        need(base + 4, 4)

        def feed(half, where, layer=layer, base=base):
            source = h_low[layer, half, where]
            for j in range(0, ups, 2):
                lanes = pl.ds(j * PIECE, 2 * PIECE)
                u = product(source, matrix(base + 4 + j, 2)) + ff_shift[pl.ds(layer, 1), lanes]
                cdf = 0.5 * (1.0 + lax.erf(u * root_half))
                bell = jnp.exp(-0.5 * u * u) * inv_root_tau
                act[layer, half, where, lanes] = (u * cdf).astype(jnp.bfloat16)
                slope[layer, half, where, lanes] = (cdf + u * bell).astype(jnp.bfloat16)

        def down(half, where, layer=layer, base=base):
            return product_nt(act[layer, half, where], matrix(base + 8, ups))

        def feed_peer(chunk, carry, layer=layer, base=base, ex=ex, feed=feed, down=down, pump=pump):
            pump("feed", chunk)
            give_rows(ex + 2, chunk, h_low.at[layer]).wait_recv()
            feed(1 - t, chunk_rows(chunk))
            if layer > 0:

                @pl.when(chunk == 0)
                def _():
                    pump("fed")
                    need(base + 8, 4)

                put_part(ex + 3, ex + 1, chunk, down(1 - t, chunk_rows(chunk)))
            return carry

        def down_peer(chunk, carry, down=down, ex=ex):
            put_part(ex + 3, ex + 1, chunk, down(1 - t, chunk_rows(chunk)))
            return carry

        everything = pl.ds(0, half_rows)
        pump("feed own")
        feed(t, everything)
        lax.fori_loop(0, CHUNKS, feed_peer, 0)
        if layer == 0:
            pump("fed")
            need(base + 8, 4)
            lax.fori_loop(0, CHUNKS, down_peer, 0)
        pump("sent")
        own_part[...] = down(t, everything)
        pump("kept")

        if layer == layers - 1:
            remote(count_mine, count_theirs, c_send.at[0], c_recv.at[0], x_peer).wait()
            count_all = (count_mine[...] + count_theirs[...])[2:3, :1]
            out_ref[pl.ds(spots[3], 8)] = jnp.broadcast_to(count_all, (8, PIECE))
            loss_scale = token_total / count_all
        def end_rows(chunk, carry, layer=layer, ex=ex, pump=pump):
            where = chunk_rows(chunk)
            give_part(ex + 3, chunk).wait_recv()
            total = (
                stream[where] + own_part[where] + in_part[where].astype(jnp.float32) + par(layer * 5 + 3)
            )
            unit, scale = norm_stats(total)
            normed[layer, 1, where] = unit
            inverse[layer, 1, where] = scale
            value = unit * par(11 + layer * 2) + par(layer * 5 + 4)
            if layer < layers - 1:
                stream[where] = value
                x_low[layer + 1, t, where] = value.astype(jnp.bfloat16)
                give_rows(ex + 4, chunk, x_low.at[layer + 1]).start()
            else:
                put_wide(spots[1], chunk, value)
                deviation = value - teacher_ref[where].astype(jnp.float32)
                weighted = weight_ref[where] * deviation
                add_sum(24, jnp.sum(weighted * deviation, axis=0, keepdims=True))
                stream[where] = loss_scale * weighted
            pump("end", chunk)
            return carry

        lax.fori_loop(0, CHUNKS, end_rows, 0)

    def finish_gather(piece, carry):
        for k in range(3):
            when(goes(k), lambda k=k: z_copy(piece, k).wait_send())
            hop_copy(piece, k).wait_send()
        pl.when(relays)(lambda: relay(piece).wait_send())
        return carry

    lax.fori_loop(0, pieces, finish_gather, 0)

    for layer in range(layers - 1, -1, -1):
        base = layer * per_layer
        ex = 4 * layers + 4 * (layers - 1 - layer)
        last = layer == layers - 1
        done = 0 if last else per_layer
        sums_base = layer * 8

        def top_rows(chunk, carry, layer=layer, ex=ex, last=last, sums_base=sums_base):
            where = chunk_rows(chunk)
            if not last:
                give_part(ex - 1, chunk).wait_recv()
                stream[where] += own_part[where] + in_part[where].astype(jnp.float32)
            grad_out, unit = stream[where], normed[layer, 1, where]
            below = norm_back(grad_out, unit, inverse[layer, 1, where], par(11 + layer * 2))
            d_low[layer, 0, t, where] = below.astype(jnp.bfloat16)
            give_rows(ex, chunk, d_low.at[layer, 0]).start()
            stream[where] = below
            add_sum(sums_base + 6, jnp.sum(grad_out * unit, axis=0, keepdims=True))
            add_sum(sums_base + 4, jnp.sum(grad_out, axis=0, keepdims=True))
            add_sum(sums_base + 3, jnp.sum(below, axis=0, keepdims=True))
            return carry

        lax.fori_loop(0, CHUNKS, top_rows, 0)
        if not last:
            reduce_step(9)

        def feed_back(half, where, layer=layer, base=base):
            source = d_low[layer, 0, half, where]
            per_row = width // PIECE
            for j in range(0, ups, 2):
                lanes = pl.ds(j * PIECE, 2 * PIECE)
                du = product(source, matrix(base + 8 + j, 2)) * slope[
                    layer, half, where, lanes
                ].astype(jnp.float32)
                total = jnp.sum(du, axis=0, keepdims=True)
                for k in range(j, j + 2):
                    add_sum(
                        16 + layer * 4 + 2 * t + k // per_row,
                        total[:, (k - j) * PIECE : (k - j + 1) * PIECE],
                        pl.ds(k % per_row * PIECE, PIECE),
                    )
                slope[layer, half, where, lanes] = du.astype(jnp.bfloat16)

        def up_back(half, where, layer=layer, base=base):
            return product_nt(slope[layer, half, where], matrix(base + 4, ups))

        def feed_back_peer(chunk, carry, layer=layer, ex=ex, last=last, feed_back=feed_back, up_back=up_back):
            if not last:
                reduce_step(10 + chunk)
            where = chunk_rows(chunk)
            give_rows(ex, chunk, d_low.at[layer, 0]).wait_recv()
            feed_back(1 - t, where)
            put_part(ex + 1, 4 * layers - 1 if last else ex - 1, chunk, up_back(1 - t, where))
            return carry

        feed_back(t, everything)
        own_part[...] = up_back(t, everything)
        lax.fori_loop(0, CHUNKS, feed_back_peer, 0)

        def mid_rows(chunk, layer=layer, ex=ex, sums_base=sums_base):
            where = chunk_rows(chunk)
            give_part(ex + 1, chunk).wait_recv()
            grad_out = stream[where] + own_part[where] + in_part[where].astype(jnp.float32)
            unit = normed[layer, 0, where]
            below = norm_back(grad_out, unit, inverse[layer, 0, where], par(10 + layer * 2))
            d_low[layer, 1, t, where] = below.astype(jnp.bfloat16)
            give_rows(ex + 2, chunk, d_low.at[layer, 1]).start()
            stream[where] = below
            add_sum(sums_base + 5, jnp.sum(grad_out * unit, axis=0, keepdims=True))
            add_sum(sums_base + 2, jnp.sum(grad_out, axis=0, keepdims=True))
            add_sum(sums_base + 1, jnp.sum(below, axis=0, keepdims=True))

        def pair_grad(piece, left, right, j):
            lanes = pl.ds(j * PIECE, 2 * PIECE)
            if not isinstance(j, int):
                lanes = pl.ds(pl.multiple_of(j * PIECE, LANES), 2 * PIECE)
            both = product(left, right[:, :, lanes].reshape(length, 2 * PIECE))
            put_grad(piece + 1, both[:, PIECE:])
            put_grad(piece, both[:, :PIECE])

        def up_grad(j, layer=layer, base=base, pair_grad=pair_grad):
            pair_grad(base + 4 + j, turned[...], slope.at[layer], j)


        def out_grad(layer=layer, base=base):
            turn(d_low.at[layer, 1])
            put_grad(base + 3, product(turned[...], heads[layer].reshape(length, PIECE)))

        def in_grads(layer=layer, base=base):
            turn(x_low.at[layer])

            def one(index, carry):
                j = 2 - index
                put_grad(base + j, product(turned[...], d_qkv[j].reshape(length, PIECE)))
                return carry

            lax.fori_loop(0, 3, one, 0)

        def sum_move(step, last=last):
            if not last:
                if step > 0:
                    sum_finish(0, step - 1)
                sum_start(0, step)

        def attend_back(turn_number, carry, layer=layer, base=base, ex=ex, done=done):
            half = jnp.where(turn_number == 0, t, 1 - t)

            @pl.when(turn_number == 1)
            def _():
                for chunk in range(CHUNKS):
                    give_rows(ex + 2, chunk, d_low.at[layer, 1]).wait_recv()

            d_heads[half] = product(d_low[layer, 1, half], matrix(base + 3)).astype(jnp.bfloat16)

            def pair_back(pair, carry):
                lanes = pair_lanes(pair)
                keys_in, values_in = pair_rows(layer, 1, pair), pair_rows(layer, 2, pair)

                def chunk_back(chunk, carry):
                    where = chunk_rows(chunk)
                    columns = pl.ds(pl.multiple_of(half * half_rows + chunk * rows, rows), rows)
                    bias = mask[:, columns]
                    bias = jnp.concatenate([bias, bias], axis=1)
                    queries = split_heads(qkv[layer, 0, half, where, lanes])
                    grads = split_heads(d_heads[half, where, lanes])
                    scores = product_nt(keys_in, queries) + bias
                    probs = jnp.exp(scores - log_sum[layer, pair, half, chunk])
                    d_probs = product_nt(values_in, grads)
                    delta = jnp.sum(probs * d_probs, axis=0, keepdims=True)
                    d_scores = (probs * (d_probs - delta)).astype(jnp.bfloat16)
                    double = pl.ds(chunk * 2 * rows, 2 * rows)
                    probs_all[:, double] = probs.astype(jnp.bfloat16)
                    scores_all[:, double] = d_scores
                    d_query = merge_heads(product(pair_turn[pair], d_scores)) * HEAD_DIM**-0.5
                    d_qkv[0, half, where, lanes] = d_query.astype(jnp.bfloat16)
                    return carry

                for chunk in range(CHUNKS):
                    chunk_back(chunk, 0)
                query_list, grad_list = [], []
                for chunk in range(CHUNKS):
                    where = chunk_rows(chunk)
                    query_list.append(split_heads(qkv[layer, 0, half, where, lanes]))
                    grad_list.append(split_heads(d_heads[half, where, lanes]))
                d_keys = product(scores_all[...], jnp.concatenate(query_list, axis=0))
                d_values = product(probs_all[...], jnp.concatenate(grad_list, axis=0))

                @pl.when(turn_number == 0)
                def _():
                    pair_sums[pair, 0] = d_keys
                    pair_sums[pair, 1] = d_values

                @pl.when(turn_number == 1)
                def _():
                    for which, total in ((1, d_keys), (2, d_values)):
                        total = (total + pair_sums[pair, which - 1]).astype(jnp.bfloat16)
                        d_qkv[which, :, :, lanes] = total.reshape(2, half_rows, LANES)

                pl.when(pair != 1)(lambda: reduce_step(done + 3 + 2 * turn_number + pair // 2))
                return carry

            lax.fori_loop(0, pairs, pair_back, 0)
            return carry

        sum_move(0)
        turn(d_low.at[layer, 0])
        pair_grad(base + 8 + ups - 2, turned[...], act.at[layer], ups - 2)
        mid_rows(0)
        sum_move(1)
        for j in range(ups - 4, -1, -2):
            pair_grad(base + 8 + j, turned[...], act.at[layer], j)
        reduce_step(done)
        mid_rows(1)
        sum_move(2)
        reduce_step(done + 1)
        turn(h_low.at[layer])

        def up_grads(index, carry, up_grad=up_grad):
            up_grad(ups - 2 - 2 * index)
            return carry

        lax.fori_loop(0, ups // 2, up_grads, 0)
        reduce_step(done + 2)
        sum_move(3)
        for pair in range(pairs):
            pair_turn[pair] = pair_rows(layer, 1, pair).T
        lax.fori_loop(0, 2, attend_back, 0)
        if not last:
            out_grad()

        def query_rows(half, where, base=base):
            parts = jnp.concatenate([d_qkv[j, half, where] for j in range(3)], axis=1)
            return product_nt(parts, matrix(base, 3))

        def query_peer(chunk, carry, ex=ex, query_rows=query_rows):
            put_part(ex + 3, ex + 1, chunk, query_rows(1 - t, chunk_rows(chunk)))
            return carry

        add_sum(
            sums_base + 7,
            jnp.sum(d_qkv[0].reshape(length, PIECE).astype(jnp.float32), axis=0, keepdims=True),
            own_columns,
        )
        add_sum(
            sums_base,
            jnp.sum(d_qkv[2].reshape(length, PIECE).astype(jnp.float32), axis=0, keepdims=True),
            own_columns,
        )
        if not last:
            sum_start(1, 0)
        lax.fori_loop(0, CHUNKS, query_peer, 0)
        own_part[...] = query_rows(t, everything)
        reduce_step(done + 7)
        if last:
            out_grad()
        in_grads()
        reduce_step(done + 8)
    def store(first, count, number):
        block = pl.ds(first, count)
        return pltpu.make_async_copy(out_ref.at[block], result_ref.at[block], out_sem.at[number])

    later = per_layer * mats.shape[4]
    stores = (
        store(later, spots[0] - later, 0),
        store(spots[0], spots[4] - spots[0], 1),
        store(0, later, 2),
    )
    stores[0].start()
    for step in range(3):
        sum_finish(1, step)
        sum_start(1, step + 1)
        reduce_step(pieces - 3 + step)
    ex = 8 * layers - 1
    for chunk in range(CHUNKS):
        where = chunk_rows(chunk)
        give_part(ex, chunk).wait_recv()
        put_wide(spots[0], chunk, stream[where] + own_part[where] + in_part[where].astype(jnp.float32))
    sum_finish(0, 3)
    sum_finish(1, 3)
    for column in range(width // PIECE):
        out_ref[pl.ds(spots[2] + column * 32, 32)] = sums_ref[:, column * PIECE : (column + 1) * PIECE]
    stores[1].start()

    def drain(step, carry):
        reduce_step(step)
        return carry

    lax.fori_loop(pieces, pieces + LATE, drain, 0)
    stores[2].start()

    for step in range(3):
        small_z(step).wait_send()
        small_hop(step).wait_send()
    for chunk in range(CHUNKS):
        give_part(8 * layers - 1, chunk).wait_send()
        for layer in range(layers):
            give_rows(4 * layer, chunk, x_low.at[layer]).wait_send()
            give_rows(4 * layer + 2, chunk, h_low.at[layer]).wait_send()
            number = 4 * layers + 4 * (layers - 1 - layer)
            give_rows(number, chunk, d_low.at[layer, 0]).wait_send()
            give_rows(number + 2, chunk, d_low.at[layer, 1]).wait_send()

    def finish_grads(piece, carry):
        core_copy(piece).wait_send()
        col_copy(piece).wait_send()
        for step in range(3):
            row_copy(piece, step).wait_send()
        return carry

    lax.fori_loop(0, pieces, finish_grads, 0)
    for copy in stores:
        copy.wait()


def run_step(extra, token_total, matrices, vectors, tokens, teacher, valid, seg_ids, counted):
    attn_in, attn_out, ff_in, ff_out = matrices
    rows, width = tokens.shape
    length = 2 * rows
    layers, share, hidden_width = ff_in.shape
    ups = hidden_width // PIECE
    pieces = layers * (4 + 2 * ups)
    low, full = jnp.bfloat16, jnp.float32
    chunk = rows // CHUNKS
    pairs = PIECE // LANES
    blocks = (4, 2, 2, share, PIECE)
    dma = pltpu.SemaphoreType.DMA
    vmem = pl.BlockSpec(memory_space=pltpu.VMEM)
    operands = [*matrices, tokens, *vectors, teacher, valid, seg_ids]
    kernel = functools.partial(step_kernel, extra, token_total)
    if counted is None:
        inputs = len(operands)

        def body(*refs):
            kernel(*refs[:inputs], None, *refs[inputs:])

    else:
        operands.append(counted)
        body = kernel
    return pl.pallas_call(
        body,
        out_shape=jax.ShapeDtypeStruct((places(pieces * share, rows)[4], PIECE), full),
        in_specs=[pl.BlockSpec(memory_space=pl.ANY)] * 5 + [vmem] * (len(operands) - 5),
        out_specs=pl.BlockSpec(memory_space=pl.ANY),
        scratch_shapes=[
            pltpu.VMEM((places(pieces * share, rows)[4], PIECE), full),
            pltpu.VMEM((pieces, *blocks), low),
            pltpu.VMEM((4, 2, 2, 24, 2 * LANES), full),
            pltpu.VMEM((16, width), full),
            pltpu.VMEM((8, hidden_width), full),
            pltpu.VMEM((pieces, 4, 2, share, PIECE), low),
            pltpu.VMEM((pieces, 4, share, PIECE), low),
            pltpu.VMEM((pieces, 3, share, PIECE), low),
            pltpu.VMEM((layers, 2, rows, width), low),
            pltpu.VMEM((layers, 3, 2, rows, PIECE), low),
            pltpu.VMEM((layers, 2, rows, PIECE), low),
            pltpu.VMEM((layers, pairs, 2, CHUNKS, 1, 2 * chunk), full),
            pltpu.VMEM((layers, 2, rows, width), low),
            pltpu.VMEM((layers, 2, rows, hidden_width), low),
            pltpu.VMEM((layers, 2, rows, hidden_width), low),
            pltpu.VMEM((layers, 2, rows, width), full),
            pltpu.VMEM((layers, 2, rows, 1), full),
            pltpu.VMEM((rows, width), full),
            pltpu.VMEM((rows, width), low),
            pltpu.VMEM((rows, width), low),
            pltpu.VMEM((rows, width), full),
            pltpu.VMEM((layers, 2, 2, rows, width), low),
            pltpu.VMEM((3, 2, rows, PIECE), low),
            pltpu.VMEM((2, rows, PIECE), low),
            pltpu.VMEM((length, length), full),
            pltpu.VMEM((pairs, LANES, length), low),
            pltpu.VMEM((length, length), low),
            pltpu.VMEM((length, length), low),
            pltpu.VMEM((pairs, 2, length, LANES), full),
            pltpu.VMEM((width, length), low),
            pltpu.VMEM((7, 32, width), full),
            pltpu.VMEM((32, width), full),
            pltpu.VMEM((8, LANES), full),
            pltpu.VMEM((8, LANES), full),
            pltpu.VMEM((24, 2 * LANES), full),
            pltpu.VMEM((rows, 1), full),
            dma((pieces, 4)),
            dma((pieces, 3)),
            dma((pieces, 3)),
            dma((pieces, 3)),
            dma((pieces + 1,)),
            dma((6,)),
            dma((6,)),
            dma((8 * layers, CHUNKS)),
            dma((8 * layers, CHUNKS)),
            dma((pieces, 5)),
            dma((pieces, 5)),
            dma((2, 6)),
            dma((2, 6)),
            dma((1,)),
            dma((1,)),
            dma((3,)),
        ],
        compiler_params=pltpu.CompilerParams(
            collective_id=0, has_side_effects=True, vmem_limit_bytes=67_043_328
        ),
        name="encoder_step",
    )(*operands)


def sibling_groups(extra):
    size = lax.axis_size("fsdp")
    return [list(range(first, first + extra)) for first in range(0, size, extra)]


def widen(shard, extra, axis):
    if extra == 1:
        return shard
    return lax.all_gather(
        shard, "fsdp", axis=axis, axis_index_groups=sibling_groups(extra), tiled=True
    )


def sum_siblings(value, extra):
    if extra == 1:
        return value
    return lax.psum(value, "fsdp", axis_index_groups=sibling_groups(extra))


def finish_kernel(
    place_count,
    all_ref,
    mixed_out,
    tokens_grad_out,
    loss_out,
    attn_in_out,
    attn_out_out,
    ff_in_out,
    ff_out_out,
    biases_out,
    gains_out,
    ff_bias_out,
    query_out,
    sums_ref,
):
    layers, share = attn_out_out.shape[0], attn_out_out.shape[1]
    rows, width = mixed_out.shape
    ups = ff_in_out.shape[2] // PIECE
    per_layer = 4 + 2 * ups
    spots = places(layers * per_layer * share, rows)

    def grad(piece):
        return all_ref[pl.ds(piece * share, share)]

    for column in range(width // PIECE):
        lanes = pl.ds(column * PIECE, PIECE)
        tokens_grad_out[:, lanes] = all_ref[pl.ds(spots[0] + column * rows, rows)]
        mixed_out[:, lanes] = all_ref[pl.ds(spots[1] + column * rows, rows)].astype(mixed_out.dtype)
        sums_ref[:, lanes] = all_ref[pl.ds(spots[2] + column * 32, 32)]
    for layer in range(layers):
        base = layer * per_layer
        for j in range(3):
            attn_in_out[layer, j] = grad(base + j)
        attn_out_out[layer] = grad(base + 3)
        for j in range(ups):
            lanes = pl.ds(j * PIECE, PIECE)
            ff_in_out[layer, :, lanes] = grad(base + 4 + j)
            ff_out_out[layer, :, lanes] = grad(base + 4 + ups + j)
    squares = jnp.sum(sums_ref[pl.ds(24, 1)], axis=1, keepdims=True)
    loss_out[...] = squares / (all_ref[pl.ds(spots[3], 8)][:1, :1] * width)
    place = lax.axis_index("fsdp")
    share = width // place_count
    own = pltpu.roll(sums_ref[:16], (width - place * share) % width, 1)[:, :share]
    up_share = ff_bias_out.shape[1]
    first = place * up_share
    for layer in range(layers):
        for kind in range(biases_out.shape[0]):
            biases_out[kind, pl.ds(layer, 1)] = own[layer * 8 + kind : layer * 8 + kind + 1]
        gains_out[layer] = own[layer * 8 + 5 : layer * 8 + 7]
        query_out[pl.ds(layer, 1)] = own[layer * 8 + 7 : layer * 8 + 8]
        row = jnp.broadcast_to(sums_ref[pl.ds(16 + layer * 4 + first // width, 1)], (8, width))
        ff_bias_out[pl.ds(layer, 1)] = pltpu.roll(row, (width - first % width) % width, 1)[:1, :up_share]


def on_device(
    tokens,
    segments,
    valid,
    teacher,
    attn_in,
    attn_out,
    ff_in,
    ff_out,
    biases,
    gains,
    ff_bias,
    query_bias,
):
    size = lax.axis_size("fsdp")
    extra = size // GROUP
    layers = attn_in.shape[0]
    rows_dev, width = tokens.shape[1], tokens.shape[2]
    length = segments.shape[1]

    matrices = (
        jnp.swapaxes(widen(attn_in, extra, 1), 1, 2),
        widen(attn_out, extra, 1),
        widen(ff_in, extra, 1),
        widen(ff_out, extra, 1),
    )
    vectors = (
        jnp.swapaxes(widen(biases, extra, 2), 0, 1),
        widen(gains, extra, 2),
        widen(ff_bias, extra, 1),
        widen(query_bias, extra, 1),
    )
    counted = None
    if extra > 1:
        own_seg = lax.dynamic_slice_in_dim(segments, lax.axis_index("tp") * rows_dev, rows_dev, 1)
        total = sum_siblings(jnp.sum((valid * (own_seg > 0)).astype(jnp.float32)), extra)
        counted = jnp.broadcast_to(total, (8, LANES))
    results = run_step(
        extra,
        float(length * size),
        matrices,
        vectors,
        tokens[0],
        teacher[0],
        valid,
        segments,
        counted,
    )
    if extra > 1:
        share = width // GROUP
        spots = places(results.shape[0] - places(0, rows_dev)[4], rows_dev)
        grads = lax.psum_scatter(
            results[: spots[0]].reshape(-1, share, PIECE),
            "fsdp",
            scatter_dimension=1,
            axis_index_groups=sibling_groups(extra),
            tiled=True,
        )
        sums = sum_siblings(results[spots[2] : spots[3]], extra)
        results = jnp.concatenate(
            [grads.reshape(-1, PIECE), results[spots[0] : spots[2]], sums, results[spots[3] :]], axis=0
        )
    vmem = pl.BlockSpec(memory_space=pltpu.VMEM)
    full = jnp.float32
    shapes = [
        jax.ShapeDtypeStruct((rows_dev, width), jnp.bfloat16),
        jax.ShapeDtypeStruct((rows_dev, width), full),
        jax.ShapeDtypeStruct((1, 1), full),
    ]
    turned_in = (layers, 3, attn_in.shape[1], PIECE)
    turned_biases = (biases.shape[1], layers, biases.shape[2])
    for shape in (turned_in, attn_out.shape, ff_in.shape, ff_out.shape, turned_biases):
        shapes.append(jax.ShapeDtypeStruct(shape, full))
    for part in (gains, ff_bias, query_bias):
        shapes.append(jax.ShapeDtypeStruct(part.shape, full))
    mixed, tokens_grad, loss, in_grad, out_grad, up_grad, down_grad, bias_grad, *rest = pl.pallas_call(
        functools.partial(finish_kernel, size),
        out_shape=tuple(shapes),
        in_specs=[vmem],
        out_specs=(vmem,) * len(shapes),
        scratch_shapes=[pltpu.VMEM((32, width), full)],
        compiler_params=pltpu.CompilerParams(vmem_limit_bytes=24 * 1024 * 1024),
        name="place_results",
    )(results)
    return (
        mixed[None],
        tokens_grad[None],
        loss[0, 0],
        jnp.swapaxes(in_grad, 1, 2),
        out_grad,
        up_grad,
        down_grad,
        jnp.swapaxes(bias_grad, 0, 1),
        *rest,
    )


def solution(mesh):
    in_specs = (
        P("fsdp", "tp", None),
        P("fsdp", None),
        P("fsdp", "tp"),
        P("fsdp", "tp", None),
        P(None, "fsdp", None, "tp"),
        P(None, "fsdp", "tp"),
        P(None, "fsdp", "tp"),
        P(None, "fsdp", "tp"),
        P(None, None, "fsdp"),
        P(None, None, "fsdp"),
        P(None, "fsdp"),
        P(None, "fsdp"),
    )
    out_specs = (
        P("fsdp", "tp", None),
        P("fsdp", "tp", None),
        P(),
        P(None, "fsdp", None, "tp"),
        P(None, "fsdp", "tp"),
        P(None, "fsdp", "tp"),
        P(None, "fsdp", "tp"),
        P(None, None, "fsdp"),
        P(None, None, "fsdp"),
        P(None, "fsdp"),
        P(None, "fsdp"),
    )
    return jax.shard_map(
        on_device, mesh=mesh, in_specs=in_specs, out_specs=out_specs, check_vma=False
    )
```

```python
import functools

import jax
import jax.numpy as jnp
from jax import lax
from jax.experimental import pallas as pl
from jax.experimental.pallas import tpu as pltpu
from jax.sharding import PartitionSpec as P

HEAD_DIM = 64
MESH = pl.DeviceIdType.MESH
PIECE = 384
CHUNKS = 2
LANES = 128
GROUP = 16
WINDOW = 2
ROW_LEAD = 1
COL_LEAD = 1
PUMPS = (
    {
        "projected": (4,),
        "attend": ((2, 5), (3, 6)),
        "norm": ((0, 7), (1, 8), (1, 9)),
        "feed own": (10,),
        "feed": ((0, 11),),
        "fed": (12,),
        "sent": (13,),
        "kept": (14, 15),
        "end": ((0, 16),),
    },
    {
        "own projected": (17, 18),
        "attend": ((1, 19), (3, 20)),
        "norm": ((0, 21), (1, 22)),
        "feed own": (23,),
        "fed": (24,),
    },
)
LAG = 2
LATE = 6

epsilon = 1e-05
root_half = 0.7071067811865476
inv_root_tau = 0.3989422804014327
masked = -1e30


def product(left, right):
    return lax.dot_general(left, right, (((1,), (0,)), ((), ())), preferred_element_type=jnp.float32)


def product_nt(left, right):
    return lax.dot_general(left, right, (((1,), (1,)), ((), ())), preferred_element_type=jnp.float32)


def norm_stats(total):
    centred = total - jnp.mean(total, axis=-1, keepdims=True)
    inverse = lax.rsqrt(jnp.mean(centred * centred, axis=-1, keepdims=True) + epsilon)
    return centred * inverse, inverse


def norm_back(grad_out, normed, inverse, gain):
    scaled = grad_out * gain
    return inverse * (
        scaled
        - jnp.mean(scaled, axis=-1, keepdims=True)
        - normed * jnp.mean(scaled * normed, axis=-1, keepdims=True)
    )


def places(grad_rows, rows):
    first = grad_rows
    return first, first + 2 * rows, first + 4 * rows, first + 4 * rows + 64, first + 4 * rows + 72


def step_kernel(
    extra,
    token_total,
    attn_in_ref,
    attn_out_ref,
    ff_in_ref,
    ff_out_ref,
    tokens_ref,
    biases_ref,
    gains_ref,
    ff_bias_ref,
    query_ref,
    teacher_ref,
    valid_ref,
    seg_ref,
    count_in_ref,
    result_ref,
    out_ref,
    mats,
    small_all,
    param,
    ff_shift,
    from_core,
    from_col,
    from_row,
    x_low,
    qkv,
    heads,
    log_sum,
    h_low,
    act,
    slope,
    normed,
    inverse,
    stream,
    out_part,
    in_part,
    own_part,
    d_low,
    d_qkv,
    d_heads,
    mask,
    pair_turn,
    probs_all,
    scores_all,
    pair_sums,
    turned,
    sums_in,
    sums_ref,
    count_mine,
    count_theirs,
    small_ref,
    weight_ref,
    z_send,
    z_recv,
    hop_send,
    hop_recv,
    local_sem,
    s_send,
    s_recv,
    x_send,
    x_recv,
    r_send,
    r_recv,
    a_send,
    a_recv,
    c_send,
    c_recv,
    out_sem,
):
    pieces = mats.shape[0]
    spots = places(pieces * mats.shape[4], teacher_ref.shape[0])
    layers = x_low.shape[0]
    per_layer = pieces // layers
    half_rows = tokens_ref.shape[0]
    width = tokens_ref.shape[1]
    length = 2 * half_rows
    rows = half_rows // CHUNKS
    pairs = PIECE // LANES
    ups = act.shape[3] // PIECE

    spot = lax.axis_index("fsdp") // extra
    rest = lax.axis_index("fsdp") % extra
    t = lax.axis_index("tp")
    z, y, c = spot // 4, (spot // 2) % 2, spot % 2

    def peer(row, col, core):
        return {"fsdp": ((row * 2 + col) * 2 + core) * extra + rest, "tp": t}

    z_peers = [peer((z + step) % 4, y, c) for step in (1, 2, 3)]
    y_peer = peer(z, 1 - y, c)
    c_peer = peer(z, y, 1 - c)
    x_peer = {"fsdp": lax.axis_index("fsdp"), "tp": 1 - t}
    shards = []
    for layer in range(layers):
        shards += [attn_in_ref.at[layer, j] for j in range(3)]
        for source in (attn_out_ref, ff_in_ref, ff_out_ref):
            shards += [
                source.at[layer, :, pl.ds(j * PIECE, PIECE)] for j in range(source.shape[2] // PIECE)
            ]

    def own_copy(piece):
        return pltpu.make_async_copy(shards[piece], mats.at[piece, z, y, c], local_sem.at[piece])

    own_tokens = pltpu.make_async_copy(tokens_ref, x_low.at[0, t], local_sem.at[pieces])
    own_tokens.start()
    for piece in range(pieces):
        own_copy(piece).start()
    everyone = (*z_peers, y_peer, c_peer, x_peer)
    barrier = pltpu.get_barrier_semaphore()
    for other in everyone:
        pl.semaphore_signal(barrier, inc=1, device_id=other, device_id_type=MESH)
    seg_q = seg_ref[...].astype(jnp.float32)
    half_lanes = pl.ds(pl.multiple_of(t * half_rows, LANES), half_rows)
    counted_rows = valid_ref[...] * (seg_ref[:, half_lanes] > 0).astype(jnp.int32)
    weights = jnp.broadcast_to(counted_rows.astype(jnp.float32), (8, half_rows)).T
    weight_ref[...] = weights[:, :1]
    if count_in_ref is None:
        count_local = jnp.sum(weights[:, :1], axis=0, keepdims=True)
    else:
        count_local = count_in_ref[:1, :1]
    small_ref[...] = jnp.zeros_like(small_ref)
    share = biases_ref.shape[2]
    kinds = biases_ref.shape[0]
    for layer in range(layers):
        for kind in range(kinds):
            line = biases_ref[kind].astype(jnp.float32)[layer : layer + 1]
            small_ref[pl.ds(layer * kinds + kind, 1), pl.ds(0, share)] = line
        small_ref[pl.ds(10 + layer * 2, 2), pl.ds(0, share)] = gains_ref[layer].astype(jnp.float32)
    small_ref[pl.ds(14, layers), pl.ds(0, share)] = query_ref[...].astype(jnp.float32)
    small_ref[pl.ds(16, layers), pl.ds(0, ff_bias_ref.shape[1])] = ff_bias_ref[...].astype(jnp.float32)
    small_ref[pl.ds(18, 6)] = jnp.broadcast_to(count_local, (6, small_ref.shape[1]))
    pl.semaphore_wait(barrier, len(everyone))

    def remote(src, dst, send_sem, recv_sem, device):
        return pltpu.make_async_remote_copy(
            src_ref=src,
            dst_ref=dst,
            send_sem=send_sem,
            recv_sem=recv_sem,
            device_id=device,
            device_id_type=MESH,
        )

    def z_copy(piece, step):
        return remote(
            mats.at[piece, z, y, c],
            mats.at[piece, z, y, c],
            z_send.at[piece, step],
            z_recv.at[piece, step],
            z_peers[step],
        )

    relays = (z == 1) | (z == 2)

    def goes(step):
        if step == 1:
            return None
        return (z != 0) if step == 2 else (z != 3)

    def when(condition, action):
        if condition is None:
            action()
        else:
            pl.when(condition)(action)

    def relay(piece):
        source = jnp.where(z == 2, 0, 3)
        block = mats.at[piece, source, y, c]
        return remote(
            block,
            block,
            z_send.at[piece, 3],
            z_recv.at[piece, jnp.where(z == 2, 2, 0)],
            peer(3 - source, y, c),
        )

    def push(piece):
        for step in range(3):
            when(goes(step), lambda step=step: z_copy(piece, step).start())

    def relay_half(piece):
        z_copy(piece, 1).wait_recv()
        pl.when(relays)(lambda: relay(piece).start())
        if isinstance(piece, int):
            if piece + WINDOW < pieces:
                push(piece + WINDOW)
        else:
            pl.when(piece + WINDOW < pieces)(lambda: push(piece + WINDOW))

    def hop_copy(piece, kind):
        column = 1 - y if kind == 2 else y
        block = mats.at[piece, :, column, c]
        return remote(
            block,
            block,
            hop_send.at[piece, kind],
            hop_recv.at[piece, kind],
            y_peer if kind == 0 else c_peer,
        )

    def small_z(step):
        block = small_all.at[z, y, c]
        return remote(small_ref, block, s_send.at[step], s_recv.at[step], z_peers[step])

    def small_hop(kind):
        column = 1 - y if kind == 2 else y
        block = small_all.at[:, column, c]
        return remote(
            block, block, s_send.at[3 + kind], s_recv.at[3 + kind], y_peer if kind == 0 else c_peer
        )

    def first_half(piece):
        z_copy(piece, 0).wait_recv()
        z_copy(piece, 2).wait_recv()
        hop_copy(piece, 0).start()
        hop_copy(piece, 1).start()

    def second_half(piece):
        hop_copy(piece, 0).wait_recv()
        hop_copy(piece, 2).start()

    def advance(step):
        if isinstance(step, int):
            if step == 0:
                for piece in range(ROW_LEAD):
                    relay_half(piece)
                for piece in range(COL_LEAD):
                    first_half(piece)
            if step + ROW_LEAD < pieces:
                relay_half(step + ROW_LEAD)
            if step + COL_LEAD < pieces:
                first_half(step + COL_LEAD)
            if 0 < step <= pieces:
                second_half(step - 1)
        else:
            pl.when(step + ROW_LEAD < pieces)(lambda: relay_half(step + ROW_LEAD))
            pl.when(step + COL_LEAD < pieces)(lambda: first_half(step + COL_LEAD))
            pl.when(step <= pieces)(lambda: second_half(step - 1))

    def need(first, count=1):
        for piece in range(first, first + count):
            hop_copy(piece, 1).wait_recv()
            hop_copy(piece, 2).wait_recv()

    def chunk_rows(chunk):
        if isinstance(chunk, int):
            return pl.ds(chunk * rows, rows)
        return pl.ds(pl.multiple_of(chunk * rows, rows), rows)

    def put_wide(first, chunk, value):
        for column in range(width // PIECE):
            start = first + column * half_rows + chunk * rows
            if not isinstance(start, int):
                start = pl.multiple_of(start, 8)
            out_ref[pl.ds(start, rows)] = value[:, column * PIECE : (column + 1) * PIECE]

    def give_rows(number, chunk, block):
        place = block.at[t, chunk_rows(chunk)]
        return remote(place, place, x_send.at[number, chunk], x_recv.at[number, chunk], x_peer)

    def give_part(number, chunk):
        return remote(
            out_part.at[chunk_rows(chunk)],
            in_part.at[chunk_rows(chunk)],
            x_send.at[number, chunk],
            x_recv.at[number, chunk],
            x_peer,
        )

    def put_part(number, previous, chunk, value):
        if previous is not None:
            give_part(previous, chunk).wait_send()
        out_part[chunk_rows(chunk)] = value.astype(jnp.bfloat16)
        give_part(number, chunk).start()

    def place_part(index, number, previous, value):
        chunk = index % CHUNKS

        @pl.when(index < CHUNKS)
        def _():
            put_part(number, previous, chunk, value)

        @pl.when(index >= CHUNKS)
        def _():
            own_part[chunk_rows(chunk)] = value

    def core_copy(piece):
        return remote(
            mats.at[piece, :, :, 1 - c],
            from_core.at[piece],
            r_send.at[piece, 0],
            r_recv.at[piece, 0],
            c_peer,
        )

    def col_copy(piece):
        return remote(
            from_core.at[piece, :, 1 - y],
            from_col.at[piece],
            r_send.at[piece, 1],
            r_recv.at[piece, 1],
            y_peer,
        )

    def row_copy(piece, step):
        return remote(
            from_core.at[piece, (z + step + 1) % 4, y],
            from_row.at[piece, step],
            r_send.at[piece, 2 + step],
            r_recv.at[piece, 2 + step],
            z_peers[step],
        )

    def reduce_core(piece):
        core_copy(piece).wait_recv()

        def add_row(row, carry):
            from_core[piece, row] = from_core[piece, row] + mats[piece, row, :, c]
            return carry

        lax.fori_loop(0, 4, add_row, 0)
        col_copy(piece).start()

    def reduce_col(piece):
        col_copy(piece).wait_recv()

        def add_row(row, carry):
            from_core[piece, row, y] = from_core[piece, row, y] + from_col[piece, row]
            return carry

        lax.fori_loop(0, 4, add_row, 0)
        for step in range(3):
            row_copy(piece, step).start()

    def reduce_row(piece):
        for step in range(3):
            row_copy(piece, step).wait_recv()
        total = from_core[piece, z, y].astype(jnp.float32)
        for step in range(3):
            total = total + from_row[piece, step].astype(jnp.float32)
        out_ref[pl.ds(piece * total.shape[0], total.shape[0])] = total

    def reduce_step(index):
        if isinstance(index, int):
            if index < pieces:
                reduce_core(pieces - 1 - index)
            if 0 <= index - LAG < pieces:
                reduce_col(pieces - 1 - (index - LAG))
            if 0 <= index - LATE < pieces:
                reduce_row(pieces - 1 - (index - LATE))
        else:
            pl.when(index < pieces)(lambda: reduce_core(pieces - 1 - index))
            pl.when((index >= LAG) & (index < pieces + LAG))(
                lambda: reduce_col(pieces - 1 - (index - LAG))
            )
            pl.when(index >= LATE)(lambda: reduce_row(pieces - 1 - (index - LATE)))

    def put_grad(piece, value):
        mats[piece] = value.astype(jnp.bfloat16).reshape(mats.shape[1:])
        core_copy(piece).start()

    sum_blocks = ((8, 24), (0, 8))

    def sum_copy(phase, step):
        first, count = sum_blocks[phase]
        part = sums_ref.at[pl.ds(first, count)]
        slot = step if step < 3 else 3 + z
        device = (c_peer, y_peer, x_peer)[step] if step < 3 else z_peers[step - 3]
        return remote(
            part,
            sums_in.at[slot, pl.ds(first, count)],
            a_send.at[phase, step],
            a_recv.at[phase, step],
            device,
        )

    def sum_start(phase, step):
        if step < 3:
            sum_copy(phase, step).start()
            return
        first, count = sum_blocks[phase]
        for k in range(3, 6):
            sum_copy(phase, k).start()
        sums_in[3 + z, pl.ds(first, count)] = sums_ref[pl.ds(first, count)]

    def sum_finish(phase, step):
        first, count = sum_blocks[phase]
        block = pl.ds(first, count)
        if step < 3:
            sum_copy(phase, step).wait()
            sums_ref[block] = sums_ref[block] + sums_in[step, block]
            return
        for k in range(3, 6):
            sum_copy(phase, k).wait()
        sums_ref[block] = (sums_in[3, block] + sums_in[4, block]) + (
            sums_in[5, block] + sums_in[6, block]
        )

    def add_sum(row, value, column=None):
        if column is None:
            sums_ref[pl.ds(row, 1)] += value
        else:
            sums_ref[pl.ds(row, 1), column] += value

    def par(row):
        return param[pl.ds(row, 1)]

    def matrix(piece, count=1):
        parts = [mats[piece + j].reshape(width, PIECE) for j in range(count)]
        return parts[0] if count == 1 else jnp.concatenate(parts, axis=1)

    def turn(source):
        def turn_rows(index, carry):
            half, chunk = index // CHUNKS, index % CHUNKS
            columns = pl.ds(pl.multiple_of(index * rows, LANES), rows)
            turned[:, columns] = source[half, chunk_rows(chunk)].T
            return carry

        lax.fori_loop(0, 2 * CHUNKS, turn_rows, 0)

    own_columns = pl.ds(pl.multiple_of(t * PIECE, LANES), PIECE)

    for step in range(3):
        small_z(step).start()
    for piece in range(WINDOW):
        own_copy(piece).wait()
        push(piece)
    for chunk in range(CHUNKS):
        place = x_low.at[0, t, chunk_rows(chunk)]
        remote(
            tokens_ref.at[chunk_rows(chunk)],
            place,
            x_send.at[0, chunk],
            x_recv.at[0, chunk],
            x_peer,
        ).start()
    own_tokens.wait()
    stream[...] = x_low[0, t].astype(jnp.float32)
    small_all[z, y, c] = small_ref[...]
    for piece in range(WINDOW, pieces):
        own_copy(piece).wait()
    seg_k = jnp.broadcast_to(seg_q, (8, length)).T[:, :1]
    allowed = (seg_k > 0) & ((seg_k == seg_q) | (seg_q == 0))
    mask[...] = jnp.where(allowed, 0.0, masked)
    sums_ref[...] = jnp.zeros_like(sums_ref)
    lane = lax.broadcasted_iota(jnp.int32, (1, LANES), 1)
    low_lanes = lane < HEAD_DIM
    low_sub = lax.broadcasted_iota(jnp.int32, (LANES, 1), 0) < HEAD_DIM

    for step in range(3):
        small_z(step).wait_recv()
    small_hop(0).start()
    small_hop(1).start()
    advance(0)
    small_hop(0).wait_recv()
    small_hop(2).start()
    advance(1)
    small_hop(1).wait_recv()
    small_hop(2).wait_recv()
    param[...] = jnp.zeros_like(param)
    ff_shift[...] = jnp.zeros_like(ff_shift)
    counted = jnp.zeros((8, LANES), jnp.float32)
    for place in range(GROUP):
        block = small_all[place // 4, (place // 2) % 2, place % 2]
        offset = place * share
        tile = min(offset // LANES * LANES, width - 2 * LANES)
        shifted = block[:16] if offset == tile else pltpu.roll(block[:16], offset - tile, 1)
        param[pl.ds(0, 16), pl.ds(tile, 2 * LANES)] += shifted
        counted = counted + block[16:24, :LANES]
    hidden_share = ff_shift.shape[1] // (GROUP // 2)
    for place in range(GROUP // 2):
        block = small_all[2 * t + place // 4, (place // 2) % 2, place % 2][16:24]
        offset = place * hidden_share
        tile = offset // LANES * LANES
        if offset != tile:
            block = pltpu.roll(block, offset - tile, 1)
        ff_shift[:, pl.ds(tile, 2 * LANES)] += block
    count_mine[...] = counted
    remote(count_mine, count_theirs, c_send.at[0], c_recv.at[0], x_peer).start()

    def split_heads(pair):
        return jnp.concatenate(
            [jnp.where(low_lanes, pair, 0), jnp.where(low_lanes, 0, pair)], axis=0
        ).astype(pair.dtype)

    def merge_heads(turned_pair):
        size = turned_pair.shape[1] // 2
        return jnp.where(low_sub, turned_pair[:, :size], turned_pair[:, size:]).T

    def pair_lanes(pair):
        return pl.ds(pl.multiple_of(pair * LANES, LANES), LANES)

    def pair_rows(layer, which, pair):
        return qkv[layer, which, :, :, pair_lanes(pair)].reshape(length, LANES)

    def half_of(index):
        return jnp.where(index < CHUNKS, 1 - t, t)

    for layer in range(layers):
        base = layer * per_layer
        ex = 4 * layer
        early = layer == 0

        def project(half, first, count, layer=layer, base=base):
            acc = product(x_low[layer, half], matrix(base + first, count))
            for j in range(first, first + count):
                part = acc[:, (j - first) * PIECE : (j - first + 1) * PIECE]
                if j == 0:
                    part = part + param[pl.ds(14 + layer, 1), own_columns]
                if j == 2:
                    part = part + param[pl.ds(layer * 5, 1), own_columns]
                low = part.astype(jnp.bfloat16)
                if j == 0:
                    low = low * jnp.bfloat16(HEAD_DIM**-0.5)
                qkv[layer, j, half] = low

        def pump(slot, index=None, layer=layer):
            steps = PUMPS[layer].get(slot, ())
            if index is None:
                for step in steps:
                    advance(step)
                return
            for place, step in steps:
                pl.when(index == place)(lambda step=step: advance(step))

        if early:
            for j in range(3):
                if j > 0:
                    advance(j + 1)
                need(base + j)
                project(t, j, 1)
        else:
            need(base, 3)
            project(t, 0, 3)
        pump("own projected")
        for chunk in range(CHUNKS):
            give_rows(ex, chunk, x_low.at[layer]).wait_recv()
        project(1 - t, 0, 3)
        pump("projected")
        for pair in range(pairs):
            pair_turn[pair] = pair_rows(layer, 2, pair).T

        def attend(index, carry, layer=layer, base=base, ex=ex, early=early, pump=pump):
            half, chunk = half_of(index), index % CHUNKS
            where = chunk_rows(chunk)
            columns = pl.ds(pl.multiple_of(half * half_rows + chunk * rows, rows), rows)
            bias = mask[:, columns]
            bias = jnp.concatenate([bias, bias], axis=1)
            pump("attend", index)
            for pair in range(pairs):
                queries = split_heads(qkv[layer, 0, half, where, pair_lanes(pair)])
                scores = product_nt(pair_rows(layer, 1, pair), queries) + bias
                highest = jnp.max(scores, axis=0, keepdims=True)
                exponent = jnp.exp(scores - highest)
                total = jnp.sum(exponent, axis=0, keepdims=True)
                probs = (exponent * (1.0 / total)).astype(jnp.bfloat16)
                log_sum[layer, pair, half, chunk] = highest + jnp.log(total)
                mixed_pair = merge_heads(product(pair_turn[pair], probs))
                heads[layer, half, where, pair_lanes(pair)] = mixed_pair.astype(jnp.bfloat16)
            pl.when(index == 0)(lambda: need(base + 3))
            part = product_nt(heads[layer, half, where], matrix(base + 3))
            place_part(index, ex + 1, None if early else ex - 1, part)
            return carry

        lax.fori_loop(0, 2 * CHUNKS, attend, 0)

        def norm_rows(chunk, carry, layer=layer, ex=ex, pump=pump):
            where = chunk_rows(chunk)
            pump("norm", chunk)
            give_part(ex + 1, chunk).wait_recv()
            total = (
                stream[where] + own_part[where] + in_part[where].astype(jnp.float32) + par(layer * 5 + 1)
            )
            unit, scale = norm_stats(total)
            normed[layer, 0, where] = unit
            inverse[layer, 0, where] = scale
            value = unit * par(10 + layer * 2) + par(layer * 5 + 2)
            stream[where] = value
            h_low[layer, t, where] = value.astype(jnp.bfloat16)
            give_rows(ex + 2, chunk, h_low.at[layer]).start()
            return carry

        lax.fori_loop(0, CHUNKS, norm_rows, 0)

        need(base + 4, 4)

        def feed(half, where, layer=layer, base=base):
            source = h_low[layer, half, where]
            for j in range(0, ups, 2):
                lanes = pl.ds(j * PIECE, 2 * PIECE)
                u = product(source, matrix(base + 4 + j, 2)) + ff_shift[pl.ds(layer, 1), lanes]
                cdf = 0.5 * (1.0 + lax.erf(u * root_half))
                bell = jnp.exp(-0.5 * u * u) * inv_root_tau
                act[layer, half, where, lanes] = (u * cdf).astype(jnp.bfloat16)
                slope[layer, half, where, lanes] = (cdf + u * bell).astype(jnp.bfloat16)

        def down(half, where, layer=layer, base=base):
            return product_nt(act[layer, half, where], matrix(base + 8, ups))

        def feed_peer(chunk, carry, layer=layer, base=base, ex=ex, feed=feed, down=down, pump=pump):
            pump("feed", chunk)
            give_rows(ex + 2, chunk, h_low.at[layer]).wait_recv()
            feed(1 - t, chunk_rows(chunk))
            if layer > 0:

                @pl.when(chunk == 0)
                def _():
                    pump("fed")
                    need(base + 8, 4)

                put_part(ex + 3, ex + 1, chunk, down(1 - t, chunk_rows(chunk)))
            return carry

        def down_peer(chunk, carry, down=down, ex=ex):
            put_part(ex + 3, ex + 1, chunk, down(1 - t, chunk_rows(chunk)))
            return carry

        everything = pl.ds(0, half_rows)
        pump("feed own")
        feed(t, everything)
        lax.fori_loop(0, CHUNKS, feed_peer, 0)
        if layer == 0:
            pump("fed")
            need(base + 8, 4)
            lax.fori_loop(0, CHUNKS, down_peer, 0)
        pump("sent")
        own_part[...] = down(t, everything)
        pump("kept")

        if layer == layers - 1:
            remote(count_mine, count_theirs, c_send.at[0], c_recv.at[0], x_peer).wait()
            count_all = (count_mine[...] + count_theirs[...])[2:3, :1]
            out_ref[pl.ds(spots[3], 8)] = jnp.broadcast_to(count_all, (8, PIECE))
            loss_scale = token_total / count_all
        def end_rows(chunk, carry, layer=layer, ex=ex, pump=pump):
            where = chunk_rows(chunk)
            give_part(ex + 3, chunk).wait_recv()
            total = (
                stream[where] + own_part[where] + in_part[where].astype(jnp.float32) + par(layer * 5 + 3)
            )
            unit, scale = norm_stats(total)
            normed[layer, 1, where] = unit
            inverse[layer, 1, where] = scale
            value = unit * par(11 + layer * 2) + par(layer * 5 + 4)
            if layer < layers - 1:
                stream[where] = value
                x_low[layer + 1, t, where] = value.astype(jnp.bfloat16)
                give_rows(ex + 4, chunk, x_low.at[layer + 1]).start()
            else:
                put_wide(spots[1], chunk, value)
                deviation = value - teacher_ref[where].astype(jnp.float32)
                weighted = weight_ref[where] * deviation
                add_sum(24, jnp.sum(weighted * deviation, axis=0, keepdims=True))
                stream[where] = loss_scale * weighted
            pump("end", chunk)
            return carry

        lax.fori_loop(0, CHUNKS, end_rows, 0)

    def finish_gather(piece, carry):
        for k in range(3):
            when(goes(k), lambda k=k: z_copy(piece, k).wait_send())
            hop_copy(piece, k).wait_send()
        pl.when(relays)(lambda: relay(piece).wait_send())
        return carry

    lax.fori_loop(0, pieces, finish_gather, 0)

    for layer in range(layers - 1, -1, -1):
        base = layer * per_layer
        ex = 4 * layers + 4 * (layers - 1 - layer)
        last = layer == layers - 1
        done = 0 if last else per_layer
        sums_base = layer * 8

        def top_rows(chunk, carry, layer=layer, ex=ex, last=last, sums_base=sums_base):
            where = chunk_rows(chunk)
            if not last:
                give_part(ex - 1, chunk).wait_recv()
                stream[where] += own_part[where] + in_part[where].astype(jnp.float32)
            grad_out, unit = stream[where], normed[layer, 1, where]
            below = norm_back(grad_out, unit, inverse[layer, 1, where], par(11 + layer * 2))
            d_low[layer, 0, t, where] = below.astype(jnp.bfloat16)
            give_rows(ex, chunk, d_low.at[layer, 0]).start()
            stream[where] = below
            add_sum(sums_base + 6, jnp.sum(grad_out * unit, axis=0, keepdims=True))
            add_sum(sums_base + 4, jnp.sum(grad_out, axis=0, keepdims=True))
            add_sum(sums_base + 3, jnp.sum(below, axis=0, keepdims=True))
            return carry

        lax.fori_loop(0, CHUNKS, top_rows, 0)
        if not last:
            reduce_step(9)

        def feed_back(half, where, layer=layer, base=base):
            source = d_low[layer, 0, half, where]
            per_row = width // PIECE
            for j in range(0, ups, 2):
                lanes = pl.ds(j * PIECE, 2 * PIECE)
                du = product(source, matrix(base + 8 + j, 2)) * slope[
                    layer, half, where, lanes
                ].astype(jnp.float32)
                total = jnp.sum(du, axis=0, keepdims=True)
                for k in range(j, j + 2):
                    add_sum(
                        16 + layer * 4 + 2 * t + k // per_row,
                        total[:, (k - j) * PIECE : (k - j + 1) * PIECE],
                        pl.ds(k % per_row * PIECE, PIECE),
                    )
                slope[layer, half, where, lanes] = du.astype(jnp.bfloat16)

        def up_back(half, where, layer=layer, base=base):
            return product_nt(slope[layer, half, where], matrix(base + 4, ups))

        def feed_back_peer(chunk, carry, layer=layer, ex=ex, last=last, feed_back=feed_back, up_back=up_back):
            if not last:
                reduce_step(10 + chunk)
            where = chunk_rows(chunk)
            give_rows(ex, chunk, d_low.at[layer, 0]).wait_recv()
            feed_back(1 - t, where)
            put_part(ex + 1, 4 * layers - 1 if last else ex - 1, chunk, up_back(1 - t, where))
            return carry

        feed_back(t, everything)
        own_part[...] = up_back(t, everything)
        lax.fori_loop(0, CHUNKS, feed_back_peer, 0)

        def mid_rows(chunk, layer=layer, ex=ex, sums_base=sums_base):
            where = chunk_rows(chunk)
            give_part(ex + 1, chunk).wait_recv()
            grad_out = stream[where] + own_part[where] + in_part[where].astype(jnp.float32)
            unit = normed[layer, 0, where]
            below = norm_back(grad_out, unit, inverse[layer, 0, where], par(10 + layer * 2))
            d_low[layer, 1, t, where] = below.astype(jnp.bfloat16)
            give_rows(ex + 2, chunk, d_low.at[layer, 1]).start()
            stream[where] = below
            add_sum(sums_base + 5, jnp.sum(grad_out * unit, axis=0, keepdims=True))
            add_sum(sums_base + 2, jnp.sum(grad_out, axis=0, keepdims=True))
            add_sum(sums_base + 1, jnp.sum(below, axis=0, keepdims=True))

        def pair_grad(piece, left, right, j):
            lanes = pl.ds(j * PIECE, 2 * PIECE)
            if not isinstance(j, int):
                lanes = pl.ds(pl.multiple_of(j * PIECE, LANES), 2 * PIECE)
            both = product(left, right[:, :, lanes].reshape(length, 2 * PIECE))
            put_grad(piece + 1, both[:, PIECE:])
            put_grad(piece, both[:, :PIECE])

        def up_grad(j, layer=layer, base=base, pair_grad=pair_grad):
            pair_grad(base + 4 + j, turned[...], slope.at[layer], j)


        def out_grad(layer=layer, base=base):
            turn(d_low.at[layer, 1])
            put_grad(base + 3, product(turned[...], heads[layer].reshape(length, PIECE)))

        def in_grads(layer=layer, base=base):
            turn(x_low.at[layer])

            def one(index, carry):
                j = 2 - index
                put_grad(base + j, product(turned[...], d_qkv[j].reshape(length, PIECE)))
                return carry

            lax.fori_loop(0, 3, one, 0)

        def sum_move(step, last=last):
            if not last:
                if step > 0:
                    sum_finish(0, step - 1)
                sum_start(0, step)

        def attend_back(turn_number, carry, layer=layer, base=base, ex=ex, done=done):
            half = jnp.where(turn_number == 0, t, 1 - t)

            @pl.when(turn_number == 1)
            def _():
                for chunk in range(CHUNKS):
                    give_rows(ex + 2, chunk, d_low.at[layer, 1]).wait_recv()

            d_heads[half] = product(d_low[layer, 1, half], matrix(base + 3)).astype(jnp.bfloat16)

            def pair_back(pair, carry):
                lanes = pair_lanes(pair)
                keys_in, values_in = pair_rows(layer, 1, pair), pair_rows(layer, 2, pair)

                def chunk_back(chunk, carry):
                    where = chunk_rows(chunk)
                    columns = pl.ds(pl.multiple_of(half * half_rows + chunk * rows, rows), rows)
                    bias = mask[:, columns]
                    bias = jnp.concatenate([bias, bias], axis=1)
                    queries = split_heads(qkv[layer, 0, half, where, lanes])
                    grads = split_heads(d_heads[half, where, lanes])
                    scores = product_nt(keys_in, queries) + bias
                    probs = jnp.exp(scores - log_sum[layer, pair, half, chunk])
                    d_probs = product_nt(values_in, grads)
                    delta = jnp.sum(probs * d_probs, axis=0, keepdims=True)
                    d_scores = (probs * (d_probs - delta)).astype(jnp.bfloat16)
                    double = pl.ds(chunk * 2 * rows, 2 * rows)
                    probs_all[:, double] = probs.astype(jnp.bfloat16)
                    scores_all[:, double] = d_scores
                    d_query = merge_heads(product(pair_turn[pair], d_scores)) * HEAD_DIM**-0.5
                    d_qkv[0, half, where, lanes] = d_query.astype(jnp.bfloat16)
                    return carry

                for chunk in range(CHUNKS):
                    chunk_back(chunk, 0)
                query_list, grad_list = [], []
                for chunk in range(CHUNKS):
                    where = chunk_rows(chunk)
                    query_list.append(split_heads(qkv[layer, 0, half, where, lanes]))
                    grad_list.append(split_heads(d_heads[half, where, lanes]))
                d_keys = product(scores_all[...], jnp.concatenate(query_list, axis=0))
                d_values = product(probs_all[...], jnp.concatenate(grad_list, axis=0))

                @pl.when(turn_number == 0)
                def _():
                    pair_sums[pair, 0] = d_keys
                    pair_sums[pair, 1] = d_values

                @pl.when(turn_number == 1)
                def _():
                    for which, total in ((1, d_keys), (2, d_values)):
                        total = (total + pair_sums[pair, which - 1]).astype(jnp.bfloat16)
                        d_qkv[which, :, :, lanes] = total.reshape(2, half_rows, LANES)

                pl.when(pair != 1)(lambda: reduce_step(done + 3 + 2 * turn_number + pair // 2))
                return carry

            lax.fori_loop(0, pairs, pair_back, 0)
            return carry

        sum_move(0)
        turn(d_low.at[layer, 0])
        pair_grad(base + 8 + ups - 2, turned[...], act.at[layer], ups - 2)
        mid_rows(0)
        sum_move(1)
        for j in range(ups - 4, -1, -2):
            pair_grad(base + 8 + j, turned[...], act.at[layer], j)
        reduce_step(done)
        mid_rows(1)
        sum_move(2)
        reduce_step(done + 1)
        turn(h_low.at[layer])

        def up_grads(index, carry, up_grad=up_grad):
            up_grad(ups - 2 - 2 * index)
            return carry

        lax.fori_loop(0, ups // 2, up_grads, 0)
        reduce_step(done + 2)
        sum_move(3)
        for pair in range(pairs):
            pair_turn[pair] = pair_rows(layer, 1, pair).T
        lax.fori_loop(0, 2, attend_back, 0)
        if not last:
            out_grad()

        def query_rows(half, where, base=base):
            parts = jnp.concatenate([d_qkv[j, half, where] for j in range(3)], axis=1)
            return product_nt(parts, matrix(base, 3))

        def query_peer(chunk, carry, ex=ex, query_rows=query_rows):
            put_part(ex + 3, ex + 1, chunk, query_rows(1 - t, chunk_rows(chunk)))
            return carry

        add_sum(
            sums_base + 7,
            jnp.sum(d_qkv[0].reshape(length, PIECE).astype(jnp.float32), axis=0, keepdims=True),
            own_columns,
        )
        add_sum(
            sums_base,
            jnp.sum(d_qkv[2].reshape(length, PIECE).astype(jnp.float32), axis=0, keepdims=True),
            own_columns,
        )
        if not last:
            sum_start(1, 0)
        lax.fori_loop(0, CHUNKS, query_peer, 0)
        own_part[...] = query_rows(t, everything)
        reduce_step(done + 7)
        if last:
            out_grad()
        in_grads()
        reduce_step(done + 8)
    def store(first, count, number):
        block = pl.ds(first, count)
        return pltpu.make_async_copy(out_ref.at[block], result_ref.at[block], out_sem.at[number])

    later = per_layer * mats.shape[4]
    stores = (
        store(later, spots[0] - later, 0),
        store(spots[0], spots[4] - spots[0], 1),
        store(0, later, 2),
    )
    stores[0].start()
    for step in range(3):
        sum_finish(1, step)
        sum_start(1, step + 1)
        reduce_step(pieces - 3 + step)
    ex = 8 * layers - 1
    for chunk in range(CHUNKS):
        where = chunk_rows(chunk)
        give_part(ex, chunk).wait_recv()
        put_wide(spots[0], chunk, stream[where] + own_part[where] + in_part[where].astype(jnp.float32))
    sum_finish(0, 3)
    sum_finish(1, 3)
    for column in range(width // PIECE):
        out_ref[pl.ds(spots[2] + column * 32, 32)] = sums_ref[:, column * PIECE : (column + 1) * PIECE]
    stores[1].start()

    def drain(step, carry):
        reduce_step(step)
        return carry

    lax.fori_loop(pieces, pieces + LATE, drain, 0)
    stores[2].start()

    for step in range(3):
        small_z(step).wait_send()
        small_hop(step).wait_send()
    for chunk in range(CHUNKS):
        give_part(8 * layers - 1, chunk).wait_send()
        for layer in range(layers):
            give_rows(4 * layer, chunk, x_low.at[layer]).wait_send()
            give_rows(4 * layer + 2, chunk, h_low.at[layer]).wait_send()
            number = 4 * layers + 4 * (layers - 1 - layer)
            give_rows(number, chunk, d_low.at[layer, 0]).wait_send()
            give_rows(number + 2, chunk, d_low.at[layer, 1]).wait_send()

    def finish_grads(piece, carry):
        core_copy(piece).wait_send()
        col_copy(piece).wait_send()
        for step in range(3):
            row_copy(piece, step).wait_send()
        return carry

    lax.fori_loop(0, pieces, finish_grads, 0)
    for copy in stores:
        copy.wait()


def run_step(extra, token_total, matrices, vectors, tokens, teacher, valid, seg_ids, counted):
    attn_in, attn_out, ff_in, ff_out = matrices
    rows, width = tokens.shape
    length = 2 * rows
    layers, share, hidden_width = ff_in.shape
    ups = hidden_width // PIECE
    pieces = layers * (4 + 2 * ups)
    low, full = jnp.bfloat16, jnp.float32
    chunk = rows // CHUNKS
    pairs = PIECE // LANES
    blocks = (4, 2, 2, share, PIECE)
    dma = pltpu.SemaphoreType.DMA
    vmem = pl.BlockSpec(memory_space=pltpu.VMEM)
    operands = [*matrices, tokens, *vectors, teacher, valid, seg_ids]
    kernel = functools.partial(step_kernel, extra, token_total)
    if counted is None:
        inputs = len(operands)

        def body(*refs):
            kernel(*refs[:inputs], None, *refs[inputs:])

    else:
        operands.append(counted)
        body = kernel
    return pl.pallas_call(
        body,
        out_shape=jax.ShapeDtypeStruct((places(pieces * share, rows)[4], PIECE), full),
        in_specs=[pl.BlockSpec(memory_space=pl.ANY)] * 5 + [vmem] * (len(operands) - 5),
        out_specs=pl.BlockSpec(memory_space=pl.ANY),
        scratch_shapes=[
            pltpu.VMEM((places(pieces * share, rows)[4], PIECE), full),
            pltpu.VMEM((pieces, *blocks), low),
            pltpu.VMEM((4, 2, 2, 24, 2 * LANES), full),
            pltpu.VMEM((16, width), full),
            pltpu.VMEM((8, hidden_width), full),
            pltpu.VMEM((pieces, 4, 2, share, PIECE), low),
            pltpu.VMEM((pieces, 4, share, PIECE), low),
            pltpu.VMEM((pieces, 3, share, PIECE), low),
            pltpu.VMEM((layers, 2, rows, width), low),
            pltpu.VMEM((layers, 3, 2, rows, PIECE), low),
            pltpu.VMEM((layers, 2, rows, PIECE), low),
            pltpu.VMEM((layers, pairs, 2, CHUNKS, 1, 2 * chunk), full),
            pltpu.VMEM((layers, 2, rows, width), low),
            pltpu.VMEM((layers, 2, rows, hidden_width), low),
            pltpu.VMEM((layers, 2, rows, hidden_width), low),
            pltpu.VMEM((layers, 2, rows, width), full),
            pltpu.VMEM((layers, 2, rows, 1), full),
            pltpu.VMEM((rows, width), full),
            pltpu.VMEM((rows, width), low),
            pltpu.VMEM((rows, width), low),
            pltpu.VMEM((rows, width), full),
            pltpu.VMEM((layers, 2, 2, rows, width), low),
            pltpu.VMEM((3, 2, rows, PIECE), low),
            pltpu.VMEM((2, rows, PIECE), low),
            pltpu.VMEM((length, length), full),
            pltpu.VMEM((pairs, LANES, length), low),
            pltpu.VMEM((length, length), low),
            pltpu.VMEM((length, length), low),
            pltpu.VMEM((pairs, 2, length, LANES), full),
            pltpu.VMEM((width, length), low),
            pltpu.VMEM((7, 32, width), full),
            pltpu.VMEM((32, width), full),
            pltpu.VMEM((8, LANES), full),
            pltpu.VMEM((8, LANES), full),
            pltpu.VMEM((24, 2 * LANES), full),
            pltpu.VMEM((rows, 1), full),
            dma((pieces, 4)),
            dma((pieces, 3)),
            dma((pieces, 3)),
            dma((pieces, 3)),
            dma((pieces + 1,)),
            dma((6,)),
            dma((6,)),
            dma((8 * layers, CHUNKS)),
            dma((8 * layers, CHUNKS)),
            dma((pieces, 5)),
            dma((pieces, 5)),
            dma((2, 6)),
            dma((2, 6)),
            dma((1,)),
            dma((1,)),
            dma((3,)),
        ],
        compiler_params=pltpu.CompilerParams(
            collective_id=0, has_side_effects=True, vmem_limit_bytes=67_043_328
        ),
        name="encoder_step",
    )(*operands)


def sibling_groups(extra):
    size = lax.axis_size("fsdp")
    return [list(range(first, first + extra)) for first in range(0, size, extra)]


def widen(shard, extra, axis):
    if extra == 1:
        return shard
    return lax.all_gather(
        shard, "fsdp", axis=axis, axis_index_groups=sibling_groups(extra), tiled=True
    )


def sum_siblings(value, extra):
    if extra == 1:
        return value
    return lax.psum(value, "fsdp", axis_index_groups=sibling_groups(extra))


def finish_kernel(
    place_count,
    all_ref,
    mixed_out,
    tokens_grad_out,
    loss_out,
    attn_in_out,
    attn_out_out,
    ff_in_out,
    ff_out_out,
    biases_out,
    gains_out,
    ff_bias_out,
    query_out,
    sums_ref,
):
    layers, share = attn_out_out.shape[0], attn_out_out.shape[1]
    rows, width = mixed_out.shape
    ups = ff_in_out.shape[2] // PIECE
    per_layer = 4 + 2 * ups
    spots = places(layers * per_layer * share, rows)

    def grad(piece):
        return all_ref[pl.ds(piece * share, share)]

    for column in range(width // PIECE):
        lanes = pl.ds(column * PIECE, PIECE)
        tokens_grad_out[:, lanes] = all_ref[pl.ds(spots[0] + column * rows, rows)]
        mixed_out[:, lanes] = all_ref[pl.ds(spots[1] + column * rows, rows)].astype(mixed_out.dtype)
        sums_ref[:, lanes] = all_ref[pl.ds(spots[2] + column * 32, 32)]
    for layer in range(layers):
        base = layer * per_layer
        for j in range(3):
            attn_in_out[layer, j] = grad(base + j)
        attn_out_out[layer] = grad(base + 3)
        for j in range(ups):
            lanes = pl.ds(j * PIECE, PIECE)
            ff_in_out[layer, :, lanes] = grad(base + 4 + j)
            ff_out_out[layer, :, lanes] = grad(base + 4 + ups + j)
    squares = jnp.sum(sums_ref[pl.ds(24, 1)], axis=1, keepdims=True)
    loss_out[...] = squares / (all_ref[pl.ds(spots[3], 8)][:1, :1] * width)
    place = lax.axis_index("fsdp")
    share = width // place_count
    own = pltpu.roll(sums_ref[:16], (width - place * share) % width, 1)[:, :share]
    up_share = ff_bias_out.shape[1]
    first = place * up_share
    for layer in range(layers):
        for kind in range(biases_out.shape[0]):
            biases_out[kind, pl.ds(layer, 1)] = own[layer * 8 + kind : layer * 8 + kind + 1]
        gains_out[layer] = own[layer * 8 + 5 : layer * 8 + 7]
        query_out[pl.ds(layer, 1)] = own[layer * 8 + 7 : layer * 8 + 8]
        row = jnp.broadcast_to(sums_ref[pl.ds(16 + layer * 4 + first // width, 1)], (8, width))
        ff_bias_out[pl.ds(layer, 1)] = pltpu.roll(row, (width - first % width) % width, 1)[:1, :up_share]


def on_device(
    tokens,
    segments,
    valid,
    teacher,
    attn_in,
    attn_out,
    ff_in,
    ff_out,
    biases,
    gains,
    ff_bias,
    query_bias,
):
    size = lax.axis_size("fsdp")
    extra = size // GROUP
    layers = attn_in.shape[0]
    rows_dev, width = tokens.shape[1], tokens.shape[2]
    length = segments.shape[1]

    matrices = (
        jnp.swapaxes(widen(attn_in, extra, 1), 1, 2),
        widen(attn_out, extra, 1),
        widen(ff_in, extra, 1),
        widen(ff_out, extra, 1),
    )
    vectors = (
        jnp.swapaxes(widen(biases, extra, 2), 0, 1),
        widen(gains, extra, 2),
        widen(ff_bias, extra, 1),
        widen(query_bias, extra, 1),
    )
    counted = None
    if extra > 1:
        own_seg = lax.dynamic_slice_in_dim(segments, lax.axis_index("tp") * rows_dev, rows_dev, 1)
        total = sum_siblings(jnp.sum((valid * (own_seg > 0)).astype(jnp.float32)), extra)
        counted = jnp.broadcast_to(total, (8, LANES))
    results = run_step(
        extra,
        float(length * size),
        matrices,
        vectors,
        tokens[0],
        teacher[0],
        valid,
        segments,
        counted,
    )
    if extra > 1:
        share = width // GROUP
        spots = places(results.shape[0] - places(0, rows_dev)[4], rows_dev)
        grads = lax.psum_scatter(
            results[: spots[0]].reshape(-1, share, PIECE),
            "fsdp",
            scatter_dimension=1,
            axis_index_groups=sibling_groups(extra),
            tiled=True,
        )
        sums = sum_siblings(results[spots[2] : spots[3]], extra)
        results = jnp.concatenate(
            [grads.reshape(-1, PIECE), results[spots[0] : spots[2]], sums, results[spots[3] :]], axis=0
        )
    vmem = pl.BlockSpec(memory_space=pltpu.VMEM)
    full = jnp.float32
    shapes = [
        jax.ShapeDtypeStruct((rows_dev, width), jnp.bfloat16),
        jax.ShapeDtypeStruct((rows_dev, width), full),
        jax.ShapeDtypeStruct((1, 1), full),
    ]
    turned_in = (layers, 3, attn_in.shape[1], PIECE)
    turned_biases = (biases.shape[1], layers, biases.shape[2])
    for shape in (turned_in, attn_out.shape, ff_in.shape, ff_out.shape, turned_biases):
        shapes.append(jax.ShapeDtypeStruct(shape, full))
    for part in (gains, ff_bias, query_bias):
        shapes.append(jax.ShapeDtypeStruct(part.shape, full))
    mixed, tokens_grad, loss, in_grad, out_grad, up_grad, down_grad, bias_grad, *rest = pl.pallas_call(
        functools.partial(finish_kernel, size),
        out_shape=tuple(shapes),
        in_specs=[vmem],
        out_specs=(vmem,) * len(shapes),
        scratch_shapes=[pltpu.VMEM((32, width), full)],
        compiler_params=pltpu.CompilerParams(vmem_limit_bytes=24 * 1024 * 1024),
        name="place_results",
    )(results)
    return (
        mixed[None],
        tokens_grad[None],
        loss[0, 0],
        jnp.swapaxes(in_grad, 1, 2),
        out_grad,
        up_grad,
        down_grad,
        jnp.swapaxes(bias_grad, 0, 1),
        *rest,
    )


def solution(mesh):
    in_specs = (
        P("fsdp", "tp", None),
        P("fsdp", None),
        P("fsdp", "tp"),
        P("fsdp", "tp", None),
        P(None, "fsdp", None, "tp"),
        P(None, "fsdp", "tp"),
        P(None, "fsdp", "tp"),
        P(None, "fsdp", "tp"),
        P(None, None, "fsdp"),
        P(None, None, "fsdp"),
        P(None, "fsdp"),
        P(None, "fsdp"),
    )
    out_specs = (
        P("fsdp", "tp", None),
        P("fsdp", "tp", None),
        P(),
        P(None, "fsdp", None, "tp"),
        P(None, "fsdp", "tp"),
        P(None, "fsdp", "tp"),
        P(None, "fsdp", "tp"),
        P(None, None, "fsdp"),
        P(None, None, "fsdp"),
        P(None, "fsdp"),
        P(None, "fsdp"),
    )
    return jax.shard_map(
        on_device, mesh=mesh, in_specs=in_specs, out_specs=out_specs, check_vma=False
    )
```

```python
import functools

import jax
import jax.numpy as jnp
from jax import lax
from jax.experimental import pallas as pl
from jax.experimental.pallas import tpu as pltpu
from jax.sharding import PartitionSpec as P

HEAD_DIM = 64
MESH = pl.DeviceIdType.MESH
PIECE = 384
CHUNKS = 2
LANES = 128
GROUP = 16
WINDOW = 2
ROW_LEAD = 1
COL_LEAD = 1
PUMPS = (
    {
        "projected": (4,),
        "attend": ((1, 5), (2, 6)),
        "norm": ((0, 7), (1, 8)),
        "feed own": (9,),
        "feed": ((0, 10),),
        "fed": (11, 12),
        "sent": (13,),
        "kept": (14,),
        "end": ((0, 15), (1, 16)),
    },
    {
        "own projected": (17, 18),
        "projected": (19,),
        "attend": ((2, 20),),
        "norm": ((0, 21), (1, 22)),
        "feed": ((0, 23),),
        "fed": (24,),
    },
)
LAG = 2
LATE = 6

epsilon = 1e-05
root_half = 0.7071067811865476
inv_root_tau = 0.3989422804014327
masked = -1e30


def product(left, right):
    return lax.dot_general(left, right, (((1,), (0,)), ((), ())), preferred_element_type=jnp.float32)


def product_nt(left, right):
    return lax.dot_general(left, right, (((1,), (1,)), ((), ())), preferred_element_type=jnp.float32)


def norm_stats(total):
    centred = total - jnp.mean(total, axis=-1, keepdims=True)
    inverse = lax.rsqrt(jnp.mean(centred * centred, axis=-1, keepdims=True) + epsilon)
    return centred * inverse, inverse


def norm_back(grad_out, normed, inverse, gain):
    scaled = grad_out * gain
    return inverse * (
        scaled
        - jnp.mean(scaled, axis=-1, keepdims=True)
        - normed * jnp.mean(scaled * normed, axis=-1, keepdims=True)
    )


def places(grad_rows, rows):
    first = grad_rows
    return first, first + 2 * rows, first + 4 * rows, first + 4 * rows + 64, first + 4 * rows + 72


def step_kernel(
    extra,
    token_total,
    attn_in_ref,
    attn_out_ref,
    ff_in_ref,
    ff_out_ref,
    tokens_ref,
    biases_ref,
    gains_ref,
    ff_bias_ref,
    query_ref,
    teacher_ref,
    valid_ref,
    seg_ref,
    count_in_ref,
    result_ref,
    out_ref,
    mats,
    small_all,
    param,
    ff_shift,
    from_core,
    from_col,
    from_row,
    x_low,
    qkv,
    heads,
    log_sum,
    h_low,
    act,
    slope,
    normed,
    inverse,
    stream,
    out_part,
    in_part,
    own_part,
    d_low,
    d_qkv,
    d_heads,
    mask,
    pair_turn,
    probs_all,
    scores_all,
    pair_sums,
    turned,
    sums_in,
    sums_ref,
    count_mine,
    count_theirs,
    small_ref,
    weight_ref,
    z_send,
    z_recv,
    hop_send,
    hop_recv,
    local_sem,
    s_send,
    s_recv,
    x_send,
    x_recv,
    r_send,
    r_recv,
    a_send,
    a_recv,
    c_send,
    c_recv,
    out_sem,
):
    pieces = mats.shape[0]
    spots = places(pieces * mats.shape[4], teacher_ref.shape[0])
    layers = x_low.shape[0]
    per_layer = pieces // layers
    half_rows = tokens_ref.shape[0]
    width = tokens_ref.shape[1]
    length = 2 * half_rows
    rows = half_rows // CHUNKS
    pairs = PIECE // LANES
    ups = act.shape[3] // PIECE

    spot = lax.axis_index("fsdp") // extra
    rest = lax.axis_index("fsdp") % extra
    t = lax.axis_index("tp")
    z, y, c = spot // 4, (spot // 2) % 2, spot % 2

    def peer(row, col, core):
        return {"fsdp": ((row * 2 + col) * 2 + core) * extra + rest, "tp": t}

    z_peers = [peer((z + step) % 4, y, c) for step in (1, 2, 3)]
    y_peer = peer(z, 1 - y, c)
    c_peer = peer(z, y, 1 - c)
    x_peer = {"fsdp": lax.axis_index("fsdp"), "tp": 1 - t}
    shards = []
    for layer in range(layers):
        shards += [attn_in_ref.at[layer, j] for j in range(3)]
        for source in (attn_out_ref, ff_in_ref, ff_out_ref):
            shards += [
                source.at[layer, :, pl.ds(j * PIECE, PIECE)] for j in range(source.shape[2] // PIECE)
            ]

    def own_copy(piece):
        return pltpu.make_async_copy(shards[piece], mats.at[piece, z, y, c], local_sem.at[piece])

    own_tokens = pltpu.make_async_copy(tokens_ref, x_low.at[0, t], local_sem.at[pieces])
    own_tokens.start()
    for piece in range(pieces):
        own_copy(piece).start()
    everyone = (*z_peers, y_peer, c_peer, x_peer)
    barrier = pltpu.get_barrier_semaphore()
    for other in everyone:
        pl.semaphore_signal(barrier, inc=1, device_id=other, device_id_type=MESH)
    seg_q = seg_ref[...].astype(jnp.float32)
    half_lanes = pl.ds(pl.multiple_of(t * half_rows, LANES), half_rows)
    counted_rows = valid_ref[...] * (seg_ref[:, half_lanes] > 0).astype(jnp.int32)
    weights = jnp.broadcast_to(counted_rows.astype(jnp.float32), (8, half_rows)).T
    weight_ref[...] = weights[:, :1]
    if count_in_ref is None:
        count_local = jnp.sum(weights[:, :1], axis=0, keepdims=True)
    else:
        count_local = count_in_ref[:1, :1]
    small_ref[...] = jnp.zeros_like(small_ref)
    share = biases_ref.shape[2]
    kinds = biases_ref.shape[0]
    for layer in range(layers):
        for kind in range(kinds):
            line = biases_ref[kind].astype(jnp.float32)[layer : layer + 1]
            small_ref[pl.ds(layer * kinds + kind, 1), pl.ds(0, share)] = line
        small_ref[pl.ds(10 + layer * 2, 2), pl.ds(0, share)] = gains_ref[layer].astype(jnp.float32)
    small_ref[pl.ds(14, layers), pl.ds(0, share)] = query_ref[...].astype(jnp.float32)
    small_ref[pl.ds(16, layers), pl.ds(0, ff_bias_ref.shape[1])] = ff_bias_ref[...].astype(jnp.float32)
    small_ref[pl.ds(18, 6)] = jnp.broadcast_to(count_local, (6, small_ref.shape[1]))
    pl.semaphore_wait(barrier, len(everyone))

    def remote(src, dst, send_sem, recv_sem, device):
        return pltpu.make_async_remote_copy(
            src_ref=src,
            dst_ref=dst,
            send_sem=send_sem,
            recv_sem=recv_sem,
            device_id=device,
            device_id_type=MESH,
        )

    def z_copy(piece, step):
        return remote(
            mats.at[piece, z, y, c],
            mats.at[piece, z, y, c],
            z_send.at[piece, step],
            z_recv.at[piece, step],
            z_peers[step],
        )

    relays = (z == 1) | (z == 2)

    def goes(step):
        if step == 1:
            return None
        return (z != 0) if step == 2 else (z != 3)

    def when(condition, action):
        if condition is None:
            action()
        else:
            pl.when(condition)(action)

    def relay(piece):
        source = jnp.where(z == 2, 0, 3)
        block = mats.at[piece, source, y, c]
        return remote(
            block,
            block,
            z_send.at[piece, 3],
            z_recv.at[piece, jnp.where(z == 2, 2, 0)],
            peer(3 - source, y, c),
        )

    def push(piece):
        for step in range(3):
            when(goes(step), lambda step=step: z_copy(piece, step).start())

    def relay_half(piece):
        z_copy(piece, 1).wait_recv()
        pl.when(relays)(lambda: relay(piece).start())
        if isinstance(piece, int):
            if piece + WINDOW < pieces:
                push(piece + WINDOW)
        else:
            pl.when(piece + WINDOW < pieces)(lambda: push(piece + WINDOW))

    def hop_copy(piece, kind):
        column = 1 - y if kind == 2 else y
        block = mats.at[piece, :, column, c]
        return remote(
            block,
            block,
            hop_send.at[piece, kind],
            hop_recv.at[piece, kind],
            y_peer if kind == 0 else c_peer,
        )

    def small_z(step):
        block = small_all.at[z, y, c]
        return remote(small_ref, block, s_send.at[step], s_recv.at[step], z_peers[step])

    def small_hop(kind):
        column = 1 - y if kind == 2 else y
        block = small_all.at[:, column, c]
        return remote(
            block, block, s_send.at[3 + kind], s_recv.at[3 + kind], y_peer if kind == 0 else c_peer
        )

    def first_half(piece):
        z_copy(piece, 0).wait_recv()
        z_copy(piece, 2).wait_recv()
        hop_copy(piece, 0).start()
        hop_copy(piece, 1).start()

    def second_half(piece):
        hop_copy(piece, 0).wait_recv()
        hop_copy(piece, 2).start()

    def advance(step):
        if isinstance(step, int):
            if step == 0:
                for piece in range(ROW_LEAD):
                    relay_half(piece)
                for piece in range(COL_LEAD):
                    first_half(piece)
            if step + ROW_LEAD < pieces:
                relay_half(step + ROW_LEAD)
            if step + COL_LEAD < pieces:
                first_half(step + COL_LEAD)
            if 0 < step <= pieces:
                second_half(step - 1)
        else:
            pl.when(step + ROW_LEAD < pieces)(lambda: relay_half(step + ROW_LEAD))
            pl.when(step + COL_LEAD < pieces)(lambda: first_half(step + COL_LEAD))
            pl.when(step <= pieces)(lambda: second_half(step - 1))

    def need(first, count=1):
        for piece in range(first, first + count):
            hop_copy(piece, 1).wait_recv()
            hop_copy(piece, 2).wait_recv()

    def chunk_rows(chunk):
        if isinstance(chunk, int):
            return pl.ds(chunk * rows, rows)
        return pl.ds(pl.multiple_of(chunk * rows, rows), rows)

    def put_wide(first, chunk, value):
        for column in range(width // PIECE):
            start = first + column * half_rows + chunk * rows
            if not isinstance(start, int):
                start = pl.multiple_of(start, 8)
            out_ref[pl.ds(start, rows)] = value[:, column * PIECE : (column + 1) * PIECE]

    def give_rows(number, chunk, block):
        place = block.at[t, chunk_rows(chunk)]
        return remote(place, place, x_send.at[number, chunk], x_recv.at[number, chunk], x_peer)

    def give_part(number, chunk):
        return remote(
            out_part.at[chunk_rows(chunk)],
            in_part.at[chunk_rows(chunk)],
            x_send.at[number, chunk],
            x_recv.at[number, chunk],
            x_peer,
        )

    def put_part(number, previous, chunk, value):
        if previous is not None:
            give_part(previous, chunk).wait_send()
        out_part[chunk_rows(chunk)] = value.astype(jnp.bfloat16)
        give_part(number, chunk).start()

    def place_part(index, number, previous, value):
        chunk = index % CHUNKS

        @pl.when(index < CHUNKS)
        def _():
            put_part(number, previous, chunk, value)

        @pl.when(index >= CHUNKS)
        def _():
            own_part[chunk_rows(chunk)] = value

    def core_copy(piece):
        return remote(
            mats.at[piece, :, :, 1 - c],
            from_core.at[piece],
            r_send.at[piece, 0],
            r_recv.at[piece, 0],
            c_peer,
        )

    def col_copy(piece):
        return remote(
            from_core.at[piece, :, 1 - y],
            from_col.at[piece],
            r_send.at[piece, 1],
            r_recv.at[piece, 1],
            y_peer,
        )

    def row_copy(piece, step):
        return remote(
            from_core.at[piece, (z + step + 1) % 4, y],
            from_row.at[piece, step],
            r_send.at[piece, 2 + step],
            r_recv.at[piece, 2 + step],
            z_peers[step],
        )

    def reduce_core(piece):
        core_copy(piece).wait_recv()

        def add_row(row, carry):
            from_core[piece, row] = from_core[piece, row] + mats[piece, row, :, c]
            return carry

        lax.fori_loop(0, 4, add_row, 0)
        col_copy(piece).start()

    def reduce_col(piece):
        col_copy(piece).wait_recv()

        def add_row(row, carry):
            from_core[piece, row, y] = from_core[piece, row, y] + from_col[piece, row]
            return carry

        lax.fori_loop(0, 4, add_row, 0)
        for step in range(3):
            row_copy(piece, step).start()

    def reduce_row(piece):
        for step in range(3):
            row_copy(piece, step).wait_recv()
        total = from_core[piece, z, y].astype(jnp.float32)
        for step in range(3):
            total = total + from_row[piece, step].astype(jnp.float32)
        out_ref[pl.ds(piece * total.shape[0], total.shape[0])] = total

    def reduce_step(index):
        if isinstance(index, int):
            if index < pieces:
                reduce_core(pieces - 1 - index)
            if 0 <= index - LAG < pieces:
                reduce_col(pieces - 1 - (index - LAG))
            if 0 <= index - LATE < pieces:
                reduce_row(pieces - 1 - (index - LATE))
        else:
            pl.when(index < pieces)(lambda: reduce_core(pieces - 1 - index))
            pl.when((index >= LAG) & (index < pieces + LAG))(
                lambda: reduce_col(pieces - 1 - (index - LAG))
            )
            pl.when(index >= LATE)(lambda: reduce_row(pieces - 1 - (index - LATE)))

    def put_grad(piece, value):
        mats[piece] = value.astype(jnp.bfloat16).reshape(mats.shape[1:])
        core_copy(piece).start()

    sum_blocks = ((8, 24), (0, 8))

    def sum_copy(phase, step):
        first, count = sum_blocks[phase]
        part = sums_ref.at[pl.ds(first, count)]
        slot = step if step < 3 else 3 + z
        device = (c_peer, y_peer, x_peer)[step] if step < 3 else z_peers[step - 3]
        return remote(
            part,
            sums_in.at[slot, pl.ds(first, count)],
            a_send.at[phase, step],
            a_recv.at[phase, step],
            device,
        )

    def sum_start(phase, step):
        if step < 3:
            sum_copy(phase, step).start()
            return
        first, count = sum_blocks[phase]
        for k in range(3, 6):
            sum_copy(phase, k).start()
        sums_in[3 + z, pl.ds(first, count)] = sums_ref[pl.ds(first, count)]

    def sum_finish(phase, step):
        first, count = sum_blocks[phase]
        block = pl.ds(first, count)
        if step < 3:
            sum_copy(phase, step).wait()
            sums_ref[block] = sums_ref[block] + sums_in[step, block]
            return
        for k in range(3, 6):
            sum_copy(phase, k).wait()
        sums_ref[block] = (sums_in[3, block] + sums_in[4, block]) + (
            sums_in[5, block] + sums_in[6, block]
        )

    def add_sum(row, value, column=None):
        if column is None:
            sums_ref[pl.ds(row, 1)] += value
        else:
            sums_ref[pl.ds(row, 1), column] += value

    def par(row):
        return param[pl.ds(row, 1)]

    def matrix(piece, count=1):
        parts = [mats[piece + j].reshape(width, PIECE) for j in range(count)]
        return parts[0] if count == 1 else jnp.concatenate(parts, axis=1)

    def turn(source):
        def turn_rows(index, carry):
            half, chunk = index // CHUNKS, index % CHUNKS
            columns = pl.ds(pl.multiple_of(index * rows, LANES), rows)
            turned[:, columns] = source[half, chunk_rows(chunk)].T
            return carry

        lax.fori_loop(0, 2 * CHUNKS, turn_rows, 0)

    own_columns = pl.ds(pl.multiple_of(t * PIECE, LANES), PIECE)

    for step in range(3):
        small_z(step).start()
    for piece in range(WINDOW):
        own_copy(piece).wait()
        push(piece)
    for chunk in range(CHUNKS):
        place = x_low.at[0, t, chunk_rows(chunk)]
        remote(
            tokens_ref.at[chunk_rows(chunk)],
            place,
            x_send.at[0, chunk],
            x_recv.at[0, chunk],
            x_peer,
        ).start()
    own_tokens.wait()
    stream[...] = x_low[0, t].astype(jnp.float32)
    small_all[z, y, c] = small_ref[...]
    for piece in range(WINDOW, pieces):
        own_copy(piece).wait()
    seg_k = jnp.broadcast_to(seg_q, (8, length)).T[:, :1]
    allowed = (seg_k > 0) & ((seg_k == seg_q) | (seg_q == 0))
    mask[...] = jnp.where(allowed, 0.0, masked)
    sums_ref[...] = jnp.zeros_like(sums_ref)
    lane = lax.broadcasted_iota(jnp.int32, (1, LANES), 1)
    low_lanes = lane < HEAD_DIM
    low_sub = lax.broadcasted_iota(jnp.int32, (LANES, 1), 0) < HEAD_DIM

    for step in range(3):
        small_z(step).wait_recv()
    small_hop(0).start()
    small_hop(1).start()
    advance(0)
    small_hop(0).wait_recv()
    small_hop(2).start()
    advance(1)
    small_hop(1).wait_recv()
    small_hop(2).wait_recv()
    param[...] = jnp.zeros_like(param)
    ff_shift[...] = jnp.zeros_like(ff_shift)
    counted = jnp.zeros((8, LANES), jnp.float32)
    for place in range(GROUP):
        block = small_all[place // 4, (place // 2) % 2, place % 2]
        offset = place * share
        tile = min(offset // LANES * LANES, width - 2 * LANES)
        shifted = block[:16] if offset == tile else pltpu.roll(block[:16], offset - tile, 1)
        param[pl.ds(0, 16), pl.ds(tile, 2 * LANES)] += shifted
        counted = counted + block[16:24, :LANES]
    hidden_share = ff_shift.shape[1] // (GROUP // 2)
    for place in range(GROUP // 2):
        block = small_all[2 * t + place // 4, (place // 2) % 2, place % 2][16:24]
        offset = place * hidden_share
        tile = offset // LANES * LANES
        if offset != tile:
            block = pltpu.roll(block, offset - tile, 1)
        ff_shift[:, pl.ds(tile, 2 * LANES)] += block
    count_mine[...] = counted
    remote(count_mine, count_theirs, c_send.at[0], c_recv.at[0], x_peer).start()

    def split_heads(pair):
        return jnp.concatenate(
            [jnp.where(low_lanes, pair, 0), jnp.where(low_lanes, 0, pair)], axis=0
        ).astype(pair.dtype)

    def merge_heads(turned_pair):
        size = turned_pair.shape[1] // 2
        return jnp.where(low_sub, turned_pair[:, :size], turned_pair[:, size:]).T

    def pair_lanes(pair):
        return pl.ds(pl.multiple_of(pair * LANES, LANES), LANES)

    def pair_rows(layer, which, pair):
        return qkv[layer, which, :, :, pair_lanes(pair)].reshape(length, LANES)

    def half_of(index):
        return jnp.where(index < CHUNKS, 1 - t, t)

    for layer in range(layers):
        base = layer * per_layer
        ex = 4 * layer
        early = layer == 0

        def project(half, first, count, layer=layer, base=base):
            acc = product(x_low[layer, half], matrix(base + first, count))
            for j in range(first, first + count):
                part = acc[:, (j - first) * PIECE : (j - first + 1) * PIECE]
                if j == 0:
                    part = part + param[pl.ds(14 + layer, 1), own_columns]
                if j == 2:
                    part = part + param[pl.ds(layer * 5, 1), own_columns]
                low = part.astype(jnp.bfloat16)
                if j == 0:
                    low = low * jnp.bfloat16(HEAD_DIM**-0.5)
                qkv[layer, j, half] = low

        def pump(slot, index=None, layer=layer):
            steps = PUMPS[layer].get(slot, ())
            if index is None:
                for step in steps:
                    advance(step)
                return
            for place, step in steps:
                pl.when(index == place)(lambda step=step: advance(step))

        if early:
            for j in range(3):
                if j > 0:
                    advance(j + 1)
                need(base + j)
                project(t, j, 1)
        else:
            need(base, 3)
            project(t, 0, 3)
        pump("own projected")
        for chunk in range(CHUNKS):
            give_rows(ex, chunk, x_low.at[layer]).wait_recv()
        project(1 - t, 0, 3)
        pump("projected")
        for pair in range(pairs):
            pair_turn[pair] = pair_rows(layer, 2, pair).T

        def attend(index, carry, layer=layer, base=base, ex=ex, early=early, pump=pump):
            half, chunk = half_of(index), index % CHUNKS
            where = chunk_rows(chunk)
            columns = pl.ds(pl.multiple_of(half * half_rows + chunk * rows, rows), rows)
            bias = mask[:, columns]
            bias = jnp.concatenate([bias, bias], axis=1)
            pump("attend", index)
            for pair in range(pairs):
                queries = split_heads(qkv[layer, 0, half, where, pair_lanes(pair)])
                scores = product_nt(pair_rows(layer, 1, pair), queries) + bias
                highest = jnp.max(scores, axis=0, keepdims=True)
                exponent = jnp.exp(scores - highest)
                total = jnp.sum(exponent, axis=0, keepdims=True)
                probs = (exponent * (1.0 / total)).astype(jnp.bfloat16)
                log_sum[layer, pair, half, chunk] = highest + jnp.log(total)
                mixed_pair = merge_heads(product(pair_turn[pair], probs))
                heads[layer, half, where, pair_lanes(pair)] = mixed_pair.astype(jnp.bfloat16)
            pl.when(index == 0)(lambda: need(base + 3))
            part = product_nt(heads[layer, half, where], matrix(base + 3))
            place_part(index, ex + 1, None if early else ex - 1, part)
            return carry

        lax.fori_loop(0, 2 * CHUNKS, attend, 0)

        def norm_rows(chunk, carry, layer=layer, ex=ex, pump=pump):
            where = chunk_rows(chunk)
            pump("norm", chunk)
            give_part(ex + 1, chunk).wait_recv()
            total = (
                stream[where] + own_part[where] + in_part[where].astype(jnp.float32) + par(layer * 5 + 1)
            )
            unit, scale = norm_stats(total)
            normed[layer, 0, where] = unit
            inverse[layer, 0, where] = scale
            value = unit * par(10 + layer * 2) + par(layer * 5 + 2)
            stream[where] = value
            h_low[layer, t, where] = value.astype(jnp.bfloat16)
            give_rows(ex + 2, chunk, h_low.at[layer]).start()
            return carry

        lax.fori_loop(0, CHUNKS, norm_rows, 0)

        need(base + 4, 4)

        def feed(half, where, layer=layer, base=base):
            source = h_low[layer, half, where]
            for j in range(0, ups, 2):
                lanes = pl.ds(j * PIECE, 2 * PIECE)
                u = product(source, matrix(base + 4 + j, 2)) + ff_shift[pl.ds(layer, 1), lanes]
                cdf = 0.5 * (1.0 + lax.erf(u * root_half))
                bell = jnp.exp(-0.5 * u * u) * inv_root_tau
                act[layer, half, where, lanes] = (u * cdf).astype(jnp.bfloat16)
                slope[layer, half, where, lanes] = (cdf + u * bell).astype(jnp.bfloat16)

        def down(half, where, layer=layer, base=base):
            return product_nt(act[layer, half, where], matrix(base + 8, ups))

        def feed_peer(chunk, carry, layer=layer, base=base, ex=ex, feed=feed, down=down, pump=pump):
            pump("feed", chunk)
            give_rows(ex + 2, chunk, h_low.at[layer]).wait_recv()
            feed(1 - t, chunk_rows(chunk))
            if layer > 0:

                @pl.when(chunk == 0)
                def _():
                    pump("fed")
                    need(base + 8, 4)

                put_part(ex + 3, ex + 1, chunk, down(1 - t, chunk_rows(chunk)))
            return carry

        def down_peer(chunk, carry, down=down, ex=ex):
            put_part(ex + 3, ex + 1, chunk, down(1 - t, chunk_rows(chunk)))
            return carry

        everything = pl.ds(0, half_rows)
        pump("feed own")
        feed(t, everything)
        lax.fori_loop(0, CHUNKS, feed_peer, 0)
        if layer == 0:
            pump("fed")
            need(base + 8, 4)
            lax.fori_loop(0, CHUNKS, down_peer, 0)
        pump("sent")
        own_part[...] = down(t, everything)
        pump("kept")

        if layer == layers - 1:
            remote(count_mine, count_theirs, c_send.at[0], c_recv.at[0], x_peer).wait()
            count_all = (count_mine[...] + count_theirs[...])[2:3, :1]
            out_ref[pl.ds(spots[3], 8)] = jnp.broadcast_to(count_all, (8, PIECE))
            loss_scale = token_total / count_all
        def end_rows(chunk, carry, layer=layer, ex=ex, pump=pump):
            where = chunk_rows(chunk)
            give_part(ex + 3, chunk).wait_recv()
            total = (
                stream[where] + own_part[where] + in_part[where].astype(jnp.float32) + par(layer * 5 + 3)
            )
            unit, scale = norm_stats(total)
            normed[layer, 1, where] = unit
            inverse[layer, 1, where] = scale
            value = unit * par(11 + layer * 2) + par(layer * 5 + 4)
            if layer < layers - 1:
                stream[where] = value
                x_low[layer + 1, t, where] = value.astype(jnp.bfloat16)
                give_rows(ex + 4, chunk, x_low.at[layer + 1]).start()
            else:
                put_wide(spots[1], chunk, value)
                deviation = value - teacher_ref[where].astype(jnp.float32)
                weighted = weight_ref[where] * deviation
                add_sum(24, jnp.sum(weighted * deviation, axis=0, keepdims=True))
                stream[where] = loss_scale * weighted
            pump("end", chunk)
            return carry

        lax.fori_loop(0, CHUNKS, end_rows, 0)

    def finish_gather(piece, carry):
        for k in range(3):
            when(goes(k), lambda k=k: z_copy(piece, k).wait_send())
            hop_copy(piece, k).wait_send()
        pl.when(relays)(lambda: relay(piece).wait_send())
        return carry

    lax.fori_loop(0, pieces, finish_gather, 0)

    for layer in range(layers - 1, -1, -1):
        base = layer * per_layer
        ex = 4 * layers + 4 * (layers - 1 - layer)
        last = layer == layers - 1
        done = 0 if last else per_layer
        sums_base = layer * 8

        def top_rows(chunk, carry, layer=layer, ex=ex, last=last, sums_base=sums_base):
            where = chunk_rows(chunk)
            if not last:
                give_part(ex - 1, chunk).wait_recv()
                stream[where] += own_part[where] + in_part[where].astype(jnp.float32)
            grad_out, unit = stream[where], normed[layer, 1, where]
            below = norm_back(grad_out, unit, inverse[layer, 1, where], par(11 + layer * 2))
            d_low[layer, 0, t, where] = below.astype(jnp.bfloat16)
            give_rows(ex, chunk, d_low.at[layer, 0]).start()
            stream[where] = below
            add_sum(sums_base + 6, jnp.sum(grad_out * unit, axis=0, keepdims=True))
            add_sum(sums_base + 4, jnp.sum(grad_out, axis=0, keepdims=True))
            add_sum(sums_base + 3, jnp.sum(below, axis=0, keepdims=True))
            return carry

        lax.fori_loop(0, CHUNKS, top_rows, 0)
        if not last:
            reduce_step(9)

        def feed_back(half, where, layer=layer, base=base):
            source = d_low[layer, 0, half, where]
            per_row = width // PIECE
            for j in range(0, ups, 2):
                lanes = pl.ds(j * PIECE, 2 * PIECE)
                du = product(source, matrix(base + 8 + j, 2)) * slope[
                    layer, half, where, lanes
                ].astype(jnp.float32)
                total = jnp.sum(du, axis=0, keepdims=True)
                for k in range(j, j + 2):
                    add_sum(
                        16 + layer * 4 + 2 * t + k // per_row,
                        total[:, (k - j) * PIECE : (k - j + 1) * PIECE],
                        pl.ds(k % per_row * PIECE, PIECE),
                    )
                slope[layer, half, where, lanes] = du.astype(jnp.bfloat16)

        def up_back(half, where, layer=layer, base=base):
            return product_nt(slope[layer, half, where], matrix(base + 4, ups))

        def feed_back_peer(chunk, carry, layer=layer, ex=ex, last=last, feed_back=feed_back, up_back=up_back):
            if not last:
                reduce_step(10 + chunk)
            where = chunk_rows(chunk)
            give_rows(ex, chunk, d_low.at[layer, 0]).wait_recv()
            feed_back(1 - t, where)
            put_part(ex + 1, 4 * layers - 1 if last else ex - 1, chunk, up_back(1 - t, where))
            return carry

        feed_back(t, everything)
        own_part[...] = up_back(t, everything)
        lax.fori_loop(0, CHUNKS, feed_back_peer, 0)

        def mid_rows(chunk, layer=layer, ex=ex, sums_base=sums_base):
            where = chunk_rows(chunk)
            give_part(ex + 1, chunk).wait_recv()
            grad_out = stream[where] + own_part[where] + in_part[where].astype(jnp.float32)
            unit = normed[layer, 0, where]
            below = norm_back(grad_out, unit, inverse[layer, 0, where], par(10 + layer * 2))
            d_low[layer, 1, t, where] = below.astype(jnp.bfloat16)
            give_rows(ex + 2, chunk, d_low.at[layer, 1]).start()
            stream[where] = below
            add_sum(sums_base + 5, jnp.sum(grad_out * unit, axis=0, keepdims=True))
            add_sum(sums_base + 2, jnp.sum(grad_out, axis=0, keepdims=True))
            add_sum(sums_base + 1, jnp.sum(below, axis=0, keepdims=True))

        def pair_grad(piece, left, right, j):
            lanes = pl.ds(j * PIECE, 2 * PIECE)
            if not isinstance(j, int):
                lanes = pl.ds(pl.multiple_of(j * PIECE, LANES), 2 * PIECE)
            both = product(left, right[:, :, lanes].reshape(length, 2 * PIECE))
            put_grad(piece + 1, both[:, PIECE:])
            put_grad(piece, both[:, :PIECE])

        def up_grad(j, layer=layer, base=base, pair_grad=pair_grad):
            pair_grad(base + 4 + j, turned[...], slope.at[layer], j)


        def out_grad(layer=layer, base=base):
            turn(d_low.at[layer, 1])
            put_grad(base + 3, product(turned[...], heads[layer].reshape(length, PIECE)))

        def in_grads(layer=layer, base=base):
            turn(x_low.at[layer])

            def one(index, carry):
                j = 2 - index
                put_grad(base + j, product(turned[...], d_qkv[j].reshape(length, PIECE)))
                return carry

            lax.fori_loop(0, 3, one, 0)

        def sum_move(step, last=last):
            if not last:
                if step > 0:
                    sum_finish(0, step - 1)
                sum_start(0, step)

        def attend_back(turn_number, carry, layer=layer, base=base, ex=ex, done=done):
            half = jnp.where(turn_number == 0, t, 1 - t)

            @pl.when(turn_number == 1)
            def _():
                for chunk in range(CHUNKS):
                    give_rows(ex + 2, chunk, d_low.at[layer, 1]).wait_recv()

            d_heads[half] = product(d_low[layer, 1, half], matrix(base + 3)).astype(jnp.bfloat16)

            def pair_back(pair, carry):
                lanes = pair_lanes(pair)
                keys_in, values_in = pair_rows(layer, 1, pair), pair_rows(layer, 2, pair)

                def chunk_back(chunk, carry):
                    where = chunk_rows(chunk)
                    columns = pl.ds(pl.multiple_of(half * half_rows + chunk * rows, rows), rows)
                    bias = mask[:, columns]
                    bias = jnp.concatenate([bias, bias], axis=1)
                    queries = split_heads(qkv[layer, 0, half, where, lanes])
                    grads = split_heads(d_heads[half, where, lanes])
                    scores = product_nt(keys_in, queries) + bias
                    probs = jnp.exp(scores - log_sum[layer, pair, half, chunk])
                    d_probs = product_nt(values_in, grads)
                    delta = jnp.sum(probs * d_probs, axis=0, keepdims=True)
                    d_scores = (probs * (d_probs - delta)).astype(jnp.bfloat16)
                    double = pl.ds(chunk * 2 * rows, 2 * rows)
                    probs_all[:, double] = probs.astype(jnp.bfloat16)
                    scores_all[:, double] = d_scores
                    d_query = merge_heads(product(pair_turn[pair], d_scores)) * HEAD_DIM**-0.5
                    d_qkv[0, half, where, lanes] = d_query.astype(jnp.bfloat16)
                    return carry

                for chunk in range(CHUNKS):
                    chunk_back(chunk, 0)
                query_list, grad_list = [], []
                for chunk in range(CHUNKS):
                    where = chunk_rows(chunk)
                    query_list.append(split_heads(qkv[layer, 0, half, where, lanes]))
                    grad_list.append(split_heads(d_heads[half, where, lanes]))
                d_keys = product(scores_all[...], jnp.concatenate(query_list, axis=0))
                d_values = product(probs_all[...], jnp.concatenate(grad_list, axis=0))

                @pl.when(turn_number == 0)
                def _():
                    pair_sums[pair, 0] = d_keys
                    pair_sums[pair, 1] = d_values

                @pl.when(turn_number == 1)
                def _():
                    for which, total in ((1, d_keys), (2, d_values)):
                        total = (total + pair_sums[pair, which - 1]).astype(jnp.bfloat16)
                        d_qkv[which, :, :, lanes] = total.reshape(2, half_rows, LANES)

                pl.when(pair != 1)(lambda: reduce_step(done + 3 + 2 * turn_number + pair // 2))
                return carry

            lax.fori_loop(0, pairs, pair_back, 0)
            return carry

        sum_move(0)
        turn(d_low.at[layer, 0])
        pair_grad(base + 8 + ups - 2, turned[...], act.at[layer], ups - 2)
        mid_rows(0)
        sum_move(1)
        for j in range(ups - 4, -1, -2):
            pair_grad(base + 8 + j, turned[...], act.at[layer], j)
        reduce_step(done)
        mid_rows(1)
        sum_move(2)
        reduce_step(done + 1)
        turn(h_low.at[layer])

        def up_grads(index, carry, up_grad=up_grad):
            up_grad(ups - 2 - 2 * index)
            return carry

        lax.fori_loop(0, ups // 2, up_grads, 0)
        reduce_step(done + 2)
        sum_move(3)
        for pair in range(pairs):
            pair_turn[pair] = pair_rows(layer, 1, pair).T
        lax.fori_loop(0, 2, attend_back, 0)
        if not last:
            out_grad()

        def query_rows(half, where, base=base):
            parts = jnp.concatenate([d_qkv[j, half, where] for j in range(3)], axis=1)
            return product_nt(parts, matrix(base, 3))

        def query_peer(chunk, carry, ex=ex, query_rows=query_rows):
            put_part(ex + 3, ex + 1, chunk, query_rows(1 - t, chunk_rows(chunk)))
            return carry

        add_sum(
            sums_base + 7,
            jnp.sum(d_qkv[0].reshape(length, PIECE).astype(jnp.float32), axis=0, keepdims=True),
            own_columns,
        )
        add_sum(
            sums_base,
            jnp.sum(d_qkv[2].reshape(length, PIECE).astype(jnp.float32), axis=0, keepdims=True),
            own_columns,
        )
        if not last:
            sum_start(1, 0)
        lax.fori_loop(0, CHUNKS, query_peer, 0)
        own_part[...] = query_rows(t, everything)
        reduce_step(done + 7)
        if last:
            out_grad()
        in_grads()
        reduce_step(done + 8)
    def store(first, count, number):
        block = pl.ds(first, count)
        return pltpu.make_async_copy(out_ref.at[block], result_ref.at[block], out_sem.at[number])

    later = per_layer * mats.shape[4]
    stores = (
        store(later, spots[0] - later, 0),
        store(spots[0], spots[4] - spots[0], 1),
        store(0, later, 2),
    )
    stores[0].start()
    for step in range(3):
        sum_finish(1, step)
        sum_start(1, step + 1)
        reduce_step(pieces - 3 + step)
    ex = 8 * layers - 1
    for chunk in range(CHUNKS):
        where = chunk_rows(chunk)
        give_part(ex, chunk).wait_recv()
        put_wide(spots[0], chunk, stream[where] + own_part[where] + in_part[where].astype(jnp.float32))
    sum_finish(0, 3)
    sum_finish(1, 3)
    for column in range(width // PIECE):
        out_ref[pl.ds(spots[2] + column * 32, 32)] = sums_ref[:, column * PIECE : (column + 1) * PIECE]
    stores[1].start()

    def drain(step, carry):
        reduce_step(step)
        return carry

    lax.fori_loop(pieces, pieces + LATE, drain, 0)
    stores[2].start()

    for step in range(3):
        small_z(step).wait_send()
        small_hop(step).wait_send()
    for chunk in range(CHUNKS):
        give_part(8 * layers - 1, chunk).wait_send()
        for layer in range(layers):
            give_rows(4 * layer, chunk, x_low.at[layer]).wait_send()
            give_rows(4 * layer + 2, chunk, h_low.at[layer]).wait_send()
            number = 4 * layers + 4 * (layers - 1 - layer)
            give_rows(number, chunk, d_low.at[layer, 0]).wait_send()
            give_rows(number + 2, chunk, d_low.at[layer, 1]).wait_send()

    def finish_grads(piece, carry):
        core_copy(piece).wait_send()
        col_copy(piece).wait_send()
        for step in range(3):
            row_copy(piece, step).wait_send()
        return carry

    lax.fori_loop(0, pieces, finish_grads, 0)
    for copy in stores:
        copy.wait()


def run_step(extra, token_total, matrices, vectors, tokens, teacher, valid, seg_ids, counted):
    attn_in, attn_out, ff_in, ff_out = matrices
    rows, width = tokens.shape
    length = 2 * rows
    layers, share, hidden_width = ff_in.shape
    ups = hidden_width // PIECE
    pieces = layers * (4 + 2 * ups)
    low, full = jnp.bfloat16, jnp.float32
    chunk = rows // CHUNKS
    pairs = PIECE // LANES
    blocks = (4, 2, 2, share, PIECE)
    dma = pltpu.SemaphoreType.DMA
    vmem = pl.BlockSpec(memory_space=pltpu.VMEM)
    operands = [*matrices, tokens, *vectors, teacher, valid, seg_ids]
    kernel = functools.partial(step_kernel, extra, token_total)
    if counted is None:
        inputs = len(operands)

        def body(*refs):
            kernel(*refs[:inputs], None, *refs[inputs:])

    else:
        operands.append(counted)
        body = kernel
    return pl.pallas_call(
        body,
        out_shape=jax.ShapeDtypeStruct((places(pieces * share, rows)[4], PIECE), full),
        in_specs=[pl.BlockSpec(memory_space=pl.ANY)] * 5 + [vmem] * (len(operands) - 5),
        out_specs=pl.BlockSpec(memory_space=pl.ANY),
        scratch_shapes=[
            pltpu.VMEM((places(pieces * share, rows)[4], PIECE), full),
            pltpu.VMEM((pieces, *blocks), low),
            pltpu.VMEM((4, 2, 2, 24, 2 * LANES), full),
            pltpu.VMEM((16, width), full),
            pltpu.VMEM((8, hidden_width), full),
            pltpu.VMEM((pieces, 4, 2, share, PIECE), low),
            pltpu.VMEM((pieces, 4, share, PIECE), low),
            pltpu.VMEM((pieces, 3, share, PIECE), low),
            pltpu.VMEM((layers, 2, rows, width), low),
            pltpu.VMEM((layers, 3, 2, rows, PIECE), low),
            pltpu.VMEM((layers, 2, rows, PIECE), low),
            pltpu.VMEM((layers, pairs, 2, CHUNKS, 1, 2 * chunk), full),
            pltpu.VMEM((layers, 2, rows, width), low),
            pltpu.VMEM((layers, 2, rows, hidden_width), low),
            pltpu.VMEM((layers, 2, rows, hidden_width), low),
            pltpu.VMEM((layers, 2, rows, width), full),
            pltpu.VMEM((layers, 2, rows, 1), full),
            pltpu.VMEM((rows, width), full),
            pltpu.VMEM((rows, width), low),
            pltpu.VMEM((rows, width), low),
            pltpu.VMEM((rows, width), full),
            pltpu.VMEM((layers, 2, 2, rows, width), low),
            pltpu.VMEM((3, 2, rows, PIECE), low),
            pltpu.VMEM((2, rows, PIECE), low),
            pltpu.VMEM((length, length), full),
            pltpu.VMEM((pairs, LANES, length), low),
            pltpu.VMEM((length, length), low),
            pltpu.VMEM((length, length), low),
            pltpu.VMEM((pairs, 2, length, LANES), full),
            pltpu.VMEM((width, length), low),
            pltpu.VMEM((7, 32, width), full),
            pltpu.VMEM((32, width), full),
            pltpu.VMEM((8, LANES), full),
            pltpu.VMEM((8, LANES), full),
            pltpu.VMEM((24, 2 * LANES), full),
            pltpu.VMEM((rows, 1), full),
            dma((pieces, 4)),
            dma((pieces, 3)),
            dma((pieces, 3)),
            dma((pieces, 3)),
            dma((pieces + 1,)),
            dma((6,)),
            dma((6,)),
            dma((8 * layers, CHUNKS)),
            dma((8 * layers, CHUNKS)),
            dma((pieces, 5)),
            dma((pieces, 5)),
            dma((2, 6)),
            dma((2, 6)),
            dma((1,)),
            dma((1,)),
            dma((3,)),
        ],
        compiler_params=pltpu.CompilerParams(
            collective_id=0, has_side_effects=True, vmem_limit_bytes=67_043_328
        ),
        name="encoder_step",
    )(*operands)


def sibling_groups(extra):
    size = lax.axis_size("fsdp")
    return [list(range(first, first + extra)) for first in range(0, size, extra)]


def widen(shard, extra, axis):
    if extra == 1:
        return shard
    return lax.all_gather(
        shard, "fsdp", axis=axis, axis_index_groups=sibling_groups(extra), tiled=True
    )


def sum_siblings(value, extra):
    if extra == 1:
        return value
    return lax.psum(value, "fsdp", axis_index_groups=sibling_groups(extra))


def finish_kernel(
    place_count,
    all_ref,
    mixed_out,
    tokens_grad_out,
    loss_out,
    attn_in_out,
    attn_out_out,
    ff_in_out,
    ff_out_out,
    biases_out,
    gains_out,
    ff_bias_out,
    query_out,
    sums_ref,
):
    layers, share = attn_out_out.shape[0], attn_out_out.shape[1]
    rows, width = mixed_out.shape
    ups = ff_in_out.shape[2] // PIECE
    per_layer = 4 + 2 * ups
    spots = places(layers * per_layer * share, rows)

    def grad(piece):
        return all_ref[pl.ds(piece * share, share)]

    for column in range(width // PIECE):
        lanes = pl.ds(column * PIECE, PIECE)
        tokens_grad_out[:, lanes] = all_ref[pl.ds(spots[0] + column * rows, rows)]
        mixed_out[:, lanes] = all_ref[pl.ds(spots[1] + column * rows, rows)].astype(mixed_out.dtype)
        sums_ref[:, lanes] = all_ref[pl.ds(spots[2] + column * 32, 32)]
    for layer in range(layers):
        base = layer * per_layer
        for j in range(3):
            attn_in_out[layer, j] = grad(base + j)
        attn_out_out[layer] = grad(base + 3)
        for j in range(ups):
            lanes = pl.ds(j * PIECE, PIECE)
            ff_in_out[layer, :, lanes] = grad(base + 4 + j)
            ff_out_out[layer, :, lanes] = grad(base + 4 + ups + j)
    squares = jnp.sum(sums_ref[pl.ds(24, 1)], axis=1, keepdims=True)
    loss_out[...] = squares / (all_ref[pl.ds(spots[3], 8)][:1, :1] * width)
    place = lax.axis_index("fsdp")
    share = width // place_count
    own = pltpu.roll(sums_ref[:16], (width - place * share) % width, 1)[:, :share]
    up_share = ff_bias_out.shape[1]
    first = place * up_share
    for layer in range(layers):
        for kind in range(biases_out.shape[0]):
            biases_out[kind, pl.ds(layer, 1)] = own[layer * 8 + kind : layer * 8 + kind + 1]
        gains_out[layer] = own[layer * 8 + 5 : layer * 8 + 7]
        query_out[pl.ds(layer, 1)] = own[layer * 8 + 7 : layer * 8 + 8]
        row = jnp.broadcast_to(sums_ref[pl.ds(16 + layer * 4 + first // width, 1)], (8, width))
        ff_bias_out[pl.ds(layer, 1)] = pltpu.roll(row, (width - first % width) % width, 1)[:1, :up_share]


def on_device(
    tokens,
    segments,
    valid,
    teacher,
    attn_in,
    attn_out,
    ff_in,
    ff_out,
    biases,
    gains,
    ff_bias,
    query_bias,
):
    size = lax.axis_size("fsdp")
    extra = size // GROUP
    layers = attn_in.shape[0]
    rows_dev, width = tokens.shape[1], tokens.shape[2]
    length = segments.shape[1]

    matrices = (
        jnp.swapaxes(widen(attn_in, extra, 1), 1, 2),
        widen(attn_out, extra, 1),
        widen(ff_in, extra, 1),
        widen(ff_out, extra, 1),
    )
    vectors = (
        jnp.swapaxes(widen(biases, extra, 2), 0, 1),
        widen(gains, extra, 2),
        widen(ff_bias, extra, 1),
        widen(query_bias, extra, 1),
    )
    counted = None
    if extra > 1:
        own_seg = lax.dynamic_slice_in_dim(segments, lax.axis_index("tp") * rows_dev, rows_dev, 1)
        total = sum_siblings(jnp.sum((valid * (own_seg > 0)).astype(jnp.float32)), extra)
        counted = jnp.broadcast_to(total, (8, LANES))
    results = run_step(
        extra,
        float(length * size),
        matrices,
        vectors,
        tokens[0],
        teacher[0],
        valid,
        segments,
        counted,
    )
    if extra > 1:
        share = width // GROUP
        spots = places(results.shape[0] - places(0, rows_dev)[4], rows_dev)
        grads = lax.psum_scatter(
            results[: spots[0]].reshape(-1, share, PIECE),
            "fsdp",
            scatter_dimension=1,
            axis_index_groups=sibling_groups(extra),
            tiled=True,
        )
        sums = sum_siblings(results[spots[2] : spots[3]], extra)
        results = jnp.concatenate(
            [grads.reshape(-1, PIECE), results[spots[0] : spots[2]], sums, results[spots[3] :]], axis=0
        )
    vmem = pl.BlockSpec(memory_space=pltpu.VMEM)
    full = jnp.float32
    shapes = [
        jax.ShapeDtypeStruct((rows_dev, width), jnp.bfloat16),
        jax.ShapeDtypeStruct((rows_dev, width), full),
        jax.ShapeDtypeStruct((1, 1), full),
    ]
    turned_in = (layers, 3, attn_in.shape[1], PIECE)
    turned_biases = (biases.shape[1], layers, biases.shape[2])
    for shape in (turned_in, attn_out.shape, ff_in.shape, ff_out.shape, turned_biases):
        shapes.append(jax.ShapeDtypeStruct(shape, full))
    for part in (gains, ff_bias, query_bias):
        shapes.append(jax.ShapeDtypeStruct(part.shape, full))
    mixed, tokens_grad, loss, in_grad, out_grad, up_grad, down_grad, bias_grad, *rest = pl.pallas_call(
        functools.partial(finish_kernel, size),
        out_shape=tuple(shapes),
        in_specs=[vmem],
        out_specs=(vmem,) * len(shapes),
        scratch_shapes=[pltpu.VMEM((32, width), full)],
        compiler_params=pltpu.CompilerParams(vmem_limit_bytes=24 * 1024 * 1024),
        name="place_results",
    )(results)
    return (
        mixed[None],
        tokens_grad[None],
        loss[0, 0],
        jnp.swapaxes(in_grad, 1, 2),
        out_grad,
        up_grad,
        down_grad,
        jnp.swapaxes(bias_grad, 0, 1),
        *rest,
    )


def solution(mesh):
    in_specs = (
        P("fsdp", "tp", None),
        P("fsdp", None),
        P("fsdp", "tp"),
        P("fsdp", "tp", None),
        P(None, "fsdp", None, "tp"),
        P(None, "fsdp", "tp"),
        P(None, "fsdp", "tp"),
        P(None, "fsdp", "tp"),
        P(None, None, "fsdp"),
        P(None, None, "fsdp"),
        P(None, "fsdp"),
        P(None, "fsdp"),
    )
    out_specs = (
        P("fsdp", "tp", None),
        P("fsdp", "tp", None),
        P(),
        P(None, "fsdp", None, "tp"),
        P(None, "fsdp", "tp"),
        P(None, "fsdp", "tp"),
        P(None, "fsdp", "tp"),
        P(None, None, "fsdp"),
        P(None, None, "fsdp"),
        P(None, "fsdp"),
        P(None, "fsdp"),
    )
    return jax.shard_map(
        on_device, mesh=mesh, in_specs=in_specs, out_specs=out_specs, check_vma=False
    )
```
